32 devices in a mesh: spec: 4 (over z), space: 8 (over y, x, core).
Axes of the slice: x: 2, y: 2, z: 4, core: 2. Of those that a mesh axis runs over, the one named last changes fastest.
Arguments:
- spectrum: bfloat16 [1296, 128, 256], P('spec', 'space'), may hold values from 0.049804688 to 1
- land_sea: int32 [128, 256], P('space'), may hold values from 0 to 1, as said below
- owners: int32 [4], replicated, may hold values from 0 to 3, each once
- proj_weight: bfloat16 [512, 1296], replicated, may hold values from -0.15625 to 0.15625
- back_weight: bfloat16 [1296, 512], replicated, may hold values from -0.25 to 0.25
- ocean_vel: float32 [2, 32, 4, 8, 1024], P(None, None, 'spec', 'space'), may hold values from -4 to 4
- mixing: float32 [32, 4, 8, 1024], P(None, 'spec', 'space'), may hold values from 0.03 to 0.25
- active_layers: int32 [4, 8, 1024], P('spec', 'space'), may hold values from 1 to 32
Outputs:
- new_spectrum: bfloat16 [1296, 128, 256], P('spec', 'space')
- new_ocean: float32 [2, 32, 4, 8, 1024], P(None, None, 'spec', 'space')
The draws below stay inside these ranges and needn't reach their ends.
Inputs may be any that keep to these rules, and one draw needn't show every extreme that they name: `land_sea`: in every aligned block of 4 rows (1024 points) at most 768 points are sea; some block has exactly 768. `owners`: A permutation: the ocean slots of a strip cover its 4 blocks once each.
All inputs are finite; a program needn't handle non-finite values.
Results may differ from the reference program's by a relative error of at most 0.0064.
Values may be sent and summed in bfloat16 or wider, within the bound.
A program may use at most 64 MiB of HBM per device.

```python
import math
import jax
import jax.numpy as jnp
from jax import lax

NDIR = 36
NFREQ = 36
K = 1296
RANK = 512
LAYERS = 32
STEPS = 2
RX = 16
NY = 256
SLOTS = 4
STRIPS = 8
PTS = 1024
CAP = 768
NX = 128
NBLK = 32
PROFILE = 66
N_SPEC = 4
N_SPACE = 8


def draw_land_sea(key, part):
    count_key, full_key, perm_key = jax.random.split(key, 3)
    counts = jax.random.randint(count_key, (NBLK,), PTS // 4, CAP + 1)
    chosen = jax.random.randint(full_key, (), 0, NBLK)
    counts = jnp.where(jnp.arange(NBLK) == chosen, CAP, counts)

    def block_ranks(block_key):
        return jax.random.permutation(block_key, PTS)
    rank_values = jax.vmap(block_ranks)(jax.random.split(perm_key, NBLK))
    sea_points = (rank_values < counts[:, None]).astype(jnp.int32)
    return sea_points.reshape(NX, NY)


def place_ends(result, stream_key, smallest, largest):
    index_at = [jax.random.randint(jax.random.fold_in(stream_key, axis), (), 0, length) for axis, length in enumerate(result.shape)]
    longest = result.shape.index(max(result.shape))
    next_to = index_at[:longest] + [(index_at[longest] + 1) % result.shape[longest]] + index_at[longest + 1:]
    return result.at[tuple(index_at)].set(smallest).at[tuple(next_to)].set(largest)


def steps_of(stream_key, extent, cuts, low, top_value):
    factor_of = 1.0
    for dim, shards_of in cuts:
        steps = jax.random.uniform(jax.random.fold_in(jax.random.fold_in(stream_key, 6), dim), (shards_of,), jnp.float32, low / len(cuts), top_value / len(cuts))
        factor_of = factor_of * jnp.repeat(jnp.exp(steps), extent[dim] // shards_of).reshape((-1,) + (1,) * (len(extent) - 1 - dim))
    return factor_of


def gaussian(own_key, shape, scale, reach, shards=(), held_as=jnp.bfloat16):
    loudness = steps_of(own_key, shape, shards, -0.22, 0.18) if shards else 1.0
    entries = jax.random.normal(own_key, shape, jnp.float32) * scale * loudness
    return jnp.minimum(jnp.maximum(entries, -reach), reach).astype(held_as)


def setup_inputs(seed: int = 0) -> dict:
    seeds = jax.random.split(jax.random.key(seed), 9)
    spectrum = jnp.clip(jnp.exp(math.log(1.0) - 2.9996462 * jax.random.uniform(seeds[0], (K, NX, NY), jnp.float32) ** steps_of(seeds[0], (K, NX, NY), ((0, 4), (1, 8)), -0.2, 0.2)), 0.049804688, 1.0).astype(jnp.bfloat16)
    land_sea = draw_land_sea(jax.random.fold_in(seeds[8], 71), 0)
    owners = jax.random.permutation(seeds[2], SLOTS).astype(jnp.int32)
    proj_weight = gaussian(seeds[3], (RANK, K), K ** -0.5, 0.15625)
    back_weight = gaussian(seeds[4], (K, RANK), RANK ** -0.5, 0.25)
    ocean_vel = gaussian(seeds[5], (2, LAYERS, SLOTS, STRIPS, PTS), 1.0, 4.0, ((2, 4), (3, 8)), jnp.float32)
    mixing = jnp.clip(jnp.exp(math.log(0.25) - 2.1202636 * jax.random.uniform(seeds[6], (LAYERS, SLOTS, STRIPS, PTS), jnp.float32) ** steps_of(seeds[6], (LAYERS, SLOTS, STRIPS, PTS), ((1, 4), (2, 8)), -0.2, 0.2)), 0.03, 0.25)
    active_layers = place_ends(jax.random.randint(seeds[7], (SLOTS, STRIPS, PTS), 1, LAYERS + 1), jax.random.fold_in(seeds[7], 1), 1, LAYERS).astype(jnp.int32)
    return {"spectrum": spectrum, "land_sea": land_sea, "owners": owners, "proj_weight": proj_weight, "back_weight": back_weight, "ocean_vel": ocean_vel, "mixing": mixing, "active_layers": active_layers}


courant_scale = 0.5
current_scale = 0.15
source_step = 0.25
coriolis = 0.3
stress_scale = 0.5
drift_scale = 4.0

def component_tables():
    component = jnp.arange(K, dtype=jnp.int32)
    frequency = component // NDIR
    direction = component % NDIR
    angle = (direction.astype(jnp.float32) + 0.5) * (2.0 * math.pi / NDIR)
    group_speed = courant_scale * jnp.exp(-2.0 * frequency.astype(jnp.float32) / NFREQ)
    eastward = (4 * direction + 2 < NDIR) | (4 * direction + 2 > 3 * NDIR)
    northward = 2 * direction + 1 < NDIR
    return (group_speed * jnp.cos(angle), group_speed * jnp.sin(angle), eastward, northward)

def coupling_tables():
    component = jnp.arange(K, dtype=jnp.int32)
    frequency = (component // NDIR).astype(jnp.float32)
    direction = (component % NDIR).astype(jnp.float32)
    angle = (direction + 0.5) * (2.0 * math.pi / NDIR)
    wavenum = 0.02 * jnp.exp(6.0 * frequency / NFREQ)
    depth = jnp.arange(LAYERS, dtype=jnp.float32)[:, None] + 0.5
    decay_rows = wavenum[None, :] ** 1.5 * jnp.exp(-2.0 * wavenum[None, :] * depth)
    decay_rows = decay_rows / jnp.sqrt(lax.optimization_barrier(jnp.sum(decay_rows * decay_rows, axis=1, keepdims=True)))
    drift_rows = drift_scale * jnp.concatenate([decay_rows * jnp.cos(angle)[None, :], decay_rows * jnp.sin(angle)[None, :]], 0)
    stress = wavenum / jnp.sqrt(jnp.sum(wavenum * wavenum))
    stress_rows = -stress_scale * jnp.stack([stress * jnp.cos(angle), stress * jnp.sin(angle)], 0)
    return (drift_rows, stress_rows)

def face_difference(padded, forward_mask, axis):
    face_count = padded.shape[axis] - 4
    cell_before = lax.slice_in_dim(padded, 0, face_count + 1, axis=axis)
    cell_left = lax.slice_in_dim(padded, 1, face_count + 2, axis=axis)
    cell_right = lax.slice_in_dim(padded, 2, face_count + 3, axis=axis)
    cell_after = lax.slice_in_dim(padded, 3, face_count + 4, axis=axis)
    forward = (5.0 * cell_left + 2.0 * cell_right - cell_before) / 6.0
    backward = (2.0 * cell_left + 5.0 * cell_right - cell_after) / 6.0
    face_flux = jnp.where(forward_mask, forward, backward)
    return lax.slice_in_dim(face_flux, 1, face_count + 1, axis=axis) - lax.slice_in_dim(face_flux, 0, face_count, axis=axis)

def propagate(spectral_state, land_mask, currents, speed_east, speed_north, eastward, northward):
    masked = spectral_state.astype(jnp.float32) * land_mask
    flux_east = (speed_east[:, None, None] + current_scale * currents[0]) * masked
    flux_north = (speed_north[:, None, None] + current_scale * currents[1]) * masked
    padded_east = jnp.pad(flux_east, ((0, 0), (2, 2), (0, 0)))
    padded_north = jnp.pad(flux_north, ((0, 0), (0, 0), (2, 2)))
    advected = masked - face_difference(padded_east, eastward[:, None, None], 1) - face_difference(padded_north, northward[:, None, None], 2)
    return (advected * land_mask).astype(jnp.bfloat16)

def source_block(drift_block, proj_weight, back_weight, drift_rows, stress_rows):
    projected = jnp.dot(proj_weight, drift_block, preferred_element_type=jnp.float32)
    cubed = (projected * projected * projected).astype(jnp.bfloat16)
    transfer = jnp.dot(back_weight, cubed, preferred_element_type=jnp.float32)
    updated = drift_block.astype(jnp.float32) + source_step * transfer
    payload = jnp.concatenate([jnp.dot(drift_rows, updated, precision=lax.Precision.HIGHEST), jnp.dot(stress_rows, transfer, precision=lax.Precision.HIGHEST)], 0)
    return (updated.astype(jnp.bfloat16), payload)

def ocean_step(velocity, payload, mixing, active):
    layer_index = lax.broadcasted_iota(jnp.int32, mixing.shape, 0)
    live_layer = (layer_index < active[None]).astype(jnp.float32)
    bottom = (layer_index == active[None] - 1).astype(jnp.float32)
    surface = (layer_index == 0).astype(jnp.float32)
    upper_mix = mixing[:-1] * live_layer[1:]

    def mixed(field):
        between = upper_mix * (field[:-1] - field[1:])
        inflow = jnp.concatenate([jnp.zeros_like(between[:1]), between], 0)
        outflow = jnp.concatenate([between, jnp.zeros_like(between[:1])], 0)
        return inflow - outflow - mixing * bottom * field
    east_vel = velocity[0]
    north_vel = velocity[1]
    drift_east = payload[:LAYERS]
    drift_north = payload[LAYERS:2 * LAYERS]
    stress_east = payload[2 * LAYERS][None]
    stress_north = payload[2 * LAYERS + 1][None]
    new_east = live_layer * (east_vel + coriolis * (north_vel + drift_north) + mixed(east_vel) + surface * stress_east)
    new_north = live_layer * (north_vel - coriolis * (east_vel + drift_east) + mixed(north_vel) + surface * stress_north)
    return jnp.stack([new_east, new_north], 0)

def reference(spectrum, land_sea, owners, proj_weight, back_weight, ocean_vel, mixing, active_layers):
    speed_east, speed_north, eastward, northward = component_tables()
    drift_rows, stress_rows = coupling_tables()
    land_mask = land_sea.astype(jnp.float32)
    inverse = jnp.argsort(owners).astype(jnp.int32)
    velocity = ocean_vel
    spectral_state = spectrum
    for step_index in range(STEPS):
        surface = jnp.transpose(velocity[:, 0], (0, 2, 1, 3))
        currents = surface[:, :, inverse].reshape(2, NX, NY)
        drifted = propagate(spectral_state, land_mask, currents, speed_east, speed_north, eastward, northward)

        def per_strip(strip_index):
            block = lax.dynamic_slice_in_dim(drifted, strip_index * RX, RX, 1).reshape(K, RX * NY)
            return source_block(block, proj_weight, back_weight, drift_rows, stress_rows)
        new_blocks, payloads = lax.map(per_strip, jnp.arange(N_SPACE, dtype=jnp.int32))
        spectral_state = jnp.transpose(new_blocks, (1, 0, 2)).reshape(K, NX, NY)
        payloads = payloads.reshape(N_SPACE, PROFILE, N_SPEC, PTS)[:, :, owners]
        payloads = jnp.transpose(payloads, (1, 2, 0, 3))
        velocity = ocean_step(velocity, payloads, mixing, active_layers)
    return (spectral_state, velocity)
```

```python
import functools
import math

import jax
import jax.numpy as jnp
import numpy as np
from jax import lax
from jax.experimental import pallas as pl
from jax.experimental.pallas import tpu as pltpu
from jax.sharding import PartitionSpec as P

NDIR = 36
NFREQ = 36
K = NDIR * NFREQ
STEPS = 2

courant_scale = 0.5
current_scale = 0.15
source_step = 0.25
coriolis = 0.3
stress_scale = 0.5
drift_scale = 4.0

MESH = pl.DeviceIdType.MESH
F32 = jnp.float32
BF16 = jnp.bfloat16
VMEM_LIMIT = 60 * 1024 * 1024
ROWS = 16


def tap_table():
    component = np.arange(K)
    frequency = component // NDIR
    direction = component % NDIR
    angle = (direction + 0.5) * (2.0 * math.pi / NDIR)
    speed = courant_scale * np.exp(-2.0 * frequency / NFREQ)
    eastward = (4 * direction + 2 < NDIR) | (4 * direction + 2 > 3 * NDIR)
    northward = 2 * direction + 1 < NDIR
    forward = (1.0 / 6.0, -1.0, 0.5, 2.0 / 6.0, 0.0)
    backward = (0.0, -2.0 / 6.0, -0.5, 1.0, -1.0 / 6.0)
    columns = [speed * np.cos(angle), speed * np.sin(angle)]
    for mask in (eastward, northward):
        for f, b in zip(forward, backward):
            columns.append(np.where(mask, f, b))
    return np.stack(columns, 1).astype(np.float32)


def coupling_tables(layers):
    component = np.arange(K)
    frequency = component // NDIR
    angle = (component % NDIR + 0.5) * (2.0 * math.pi / NDIR)
    wavenum = 0.02 * np.exp(6.0 * frequency / NFREQ)
    depth = np.arange(layers)[:, None] + 0.5
    decay_rows = wavenum[None, :] ** 1.5 * np.exp(-2.0 * wavenum[None, :] * depth)
    decay_rows = decay_rows / np.sqrt(np.sum(decay_rows * decay_rows, axis=1, keepdims=True))
    drift_rows = drift_scale * np.concatenate(
        [decay_rows * np.cos(angle)[None, :], decay_rows * np.sin(angle)[None, :]], 0
    )
    stress = wavenum / np.sqrt(np.sum(wavenum * wavenum))
    stress_rows = -stress_scale * np.stack([stress * np.cos(angle), stress * np.sin(angle)], 0)
    return (drift_rows.astype(np.float32), stress_rows.astype(np.float32))


def two_pieces(rows):
    first = rows.astype(BF16)
    second = (rows - first.astype(np.float32)).astype(BF16)
    return np.concatenate([first, second], 0)


FORWARD = (1, -6, 3, 2, 0)
BACKWARD = (0, -2, -3, 6, -1)


def stencil_tables(seg, rows_in_chunk, edge_rows):
    lanes = rows_in_chunk * seg
    band = np.zeros((128, 256), np.float32)
    for a in range(128):
        for b in range(128):
            if a // seg == b // seg and abs(a - b) <= 2:
                band[a, b] = FORWARD[a - b + 2]
                band[a, 128 + b] = BACKWARD[a - b + 2]
    spread = np.zeros((2 * edge_rows, 2 * lanes), np.float32)
    pick = np.zeros((2 * edge_rows, lanes), np.float32)
    for k in range(rows_in_chunk):
        for i in range(2):
            pick[k * 2 + i, k * seg + i] = 1
            pick[edge_rows + k * 2 + i, k * seg + seg - 2 + i] = 1
            for c in range(seg):
                lane = k * seg + c
                at = lane // 128 * 256 + lane % 128
                for row, offset in ((k * 2 + i, i - 2 - c), (edge_rows + k * 2 + i, seg + i - c)):
                    if abs(offset) <= 2:
                        spread[row, at] = FORWARD[offset + 2]
                        spread[row, at + 128] = BACKWARD[offset + 2]
    return band.astype(BF16), spread.astype(BF16), pick.astype(BF16)


def turn_table(rows):
    table = np.zeros((rows * ROWS, rows * ROWS), np.float32)
    for c in range(ROWS):
        for r in range(rows):
            table[r * ROWS + c, c * rows + r] = 1
    return table.astype(BF16)


def steps_kernel(
    sizes, owners, spectrum, land_sea, velocity, mixing, active, taps, proj, back, outer, inner, turn, unturn,
    band, spread, pick,
    out, new_velocity,
    field, east, north, land_row, surface, surfaces, tile,
    blocks, got, state, fluxx, fluxy, drift, stencil, made, returned,
    pay, pay_out, pay_in, row_out, row_in, col_out, col_in,
    head, tail, before, after, east_head, east_tail, east_before, east_after,
    send_in, recv_in, send_back, recv_back, send_top, recv_top, send_edge, recv_edge,
    send_row, recv_row, send_col, recv_col, send_pay, recv_pay,
):
    comps, rows, width, slots = sizes
    padded = field.shape[0]
    chunks, lanes = got.shape[0], got.shape[3]
    seg = width // slots
    per_tile = 128 // seg
    tiles = lanes // 128
    chunk_rows = lanes // seg
    block = velocity.shape[2]
    block_rows = block // width
    part = block_rows * seg
    points = rows * width
    tile_points = rows * seg
    layers = mixing.shape[0]
    groups = padded // ROWS
    me = lax.axis_index("spec")
    strip = lax.axis_index("space")
    strips = lax.axis_size("space")
    edge = 2 * width
    has_before = strip > 0
    has_after = strip < strips - 1
    has_left = me > 0
    has_right = me < slots - 1
    odd = lax.rem(strip, 2) == 1

    def peer(delta):
        return lax.rem(me + delta, slots)

    def flip(base):
        return jnp.where(odd, chunks - 1 - base, base)

    def first_order(t):
        return flip(jnp.where(t < 2, 1 - t, t) if chunks > 1 else t)

    def copy(source, target, send, receive, device):
        return pltpu.make_async_remote_copy(
            src_ref=source, dst_ref=target, send_sem=send, recv_sem=receive,
            device_id=device, device_id_type=MESH,
        )

    def inward(j, delta):
        return copy(
            blocks.at[peer(delta), j], got.at[j, me],
            send_in.at[j, delta], recv_in.at[j, delta], {"spec": peer(delta)},
        )

    def homeward(j, delta):
        return copy(
            made.at[j, peer(delta)], returned.at[j, me],
            send_back.at[j, delta], recv_back.at[j, delta], {"spec": peer(delta)},
        )

    def upward(delta):
        return copy(
            surface, surfaces.at[me], send_top.at[delta], recv_top.at[delta], {"spec": peer(delta)}
        )

    def pay_over(step, delta):
        return copy(
            pay_out.at[step, peer(delta)], pay_in.at[step, me],
            send_pay.at[step, delta], recv_pay.at[step, delta], {"spec": peer(delta)},
        )

    def to_before(source, target, i):
        return copy(source, target, send_edge.at[i], recv_edge.at[i], {"space": strip - 1})

    def to_after(source, target, i):
        return copy(source, target, send_edge.at[i], recv_edge.at[i], {"space": strip + 1})

    def row_up():
        return copy(row_out.at[0], row_in.at[1], send_row.at[0], recv_row.at[0], {"space": strip - 1})

    def row_down():
        return copy(row_out.at[1], row_in.at[0], send_row.at[1], recv_row.at[1], {"space": strip + 1})

    def col_left(j):
        return copy(col_out.at[j, 0], col_in.at[j, 1], send_col.at[j, 0], recv_col.at[j, 0], {"spec": me - 1})

    def col_right(j):
        return copy(col_out.at[j, 1], col_in.at[j, 0], send_col.at[j, 1], recv_col.at[j, 1], {"spec": me + 1})

    barrier = pltpu.get_barrier_semaphore()
    for delta in range(1, slots):
        pl.semaphore_signal(barrier, inc=1, device_id={"spec": peer(delta)}, device_id_type=MESH)

    @pl.when(has_before)
    def _():
        pl.semaphore_signal(barrier, inc=1, device_id={"space": strip - 1}, device_id_type=MESH)

    @pl.when(has_after)
    def _():
        pl.semaphore_signal(barrier, inc=1, device_id={"space": strip + 1}, device_id_type=MESH)

    surface[0:1, :] = velocity[0, 0:1, :]
    surface[1:2, :] = velocity[1, 0:1, :]
    surface[2:3, :] = velocity[0, 1:2, :]
    surface[3:4, :] = velocity[1, 1:2, :]
    surface[4:5, :] = mixing[0:1, :]
    surface[5:6, :] = active[...].astype(F32)
    surface[6:8, :] = jnp.zeros((2, block), F32)
    expected = slots - 1 + has_before.astype(jnp.int32) + has_after.astype(jnp.int32)
    pl.semaphore_wait(barrier, expected)
    for delta in range(1, slots):
        upward(delta).start()
    surfaces[me] = surface[...]

    land = land_sea[...].astype(F32)
    for r in range(rows):
        land_row[:, r * width : (r + 1) * width] = land[r : r + 1, :]

    def turned(value, count):
        wet = (value.astype(F32) * land[None]).astype(BF16).reshape(count * rows, width)
        return jnp.dot(turn[:, : count * rows], wet, preferred_element_type=F32).astype(BF16)

    def place_turned(value, at):
        for r in range(rows):
            field[at, (r + 2) * width : (r + 3) * width] = value[r * ROWS : (r + 1) * ROWS]

    def turn_group(q, carry):
        at = pl.ds(pl.multiple_of(q * ROWS, ROWS), ROWS)
        place_turned(turned(spectrum[at], ROWS), at)
        return carry

    whole_groups = comps // ROWS
    rest = comps - whole_groups * ROWS
    lax.fori_loop(0, whole_groups, turn_group, 0)
    if rest:
        place_turned(turned(spectrum[whole_groups * ROWS :], rest), slice(whole_groups * ROWS, padded))
    head[...] = field[:, edge : 2 * edge]
    tail[...] = field[:, points : points + edge]

    @pl.when(has_before)
    def _():
        to_before(head, after, 0).start()

    @pl.when(has_after)
    def _():
        to_after(tail, before, 1).start()

    for delta in range(1, slots):
        upward(delta).wait()
    strip_rows = []
    for b in range(slots):
        here = jnp.zeros((8, block), F32)
        for s in range(slots):
            here = here + (owners[s] == b).astype(F32) * surfaces[s]
        strip_rows.append(here)
        east[:, edge + b * block : edge + (b + 1) * block] = current_scale * here[0:1]
        north[:, b * block : (b + 1) * block] = current_scale * here[1:2]
    east_head[...] = east[:, edge : 2 * edge]
    east_tail[...] = east[:, points : points + edge]

    @pl.when(has_before)
    def _():
        to_before(east_head, east_after, 2).start()

    @pl.when(has_after)
    def _():
        to_after(east_tail, east_before, 3).start()

    sub = lax.broadcasted_iota(jnp.int32, (8, width), 0)
    pieces_of = [[] for _ in range(slots)]
    for r in range(rows):
        at = r * width - (r * width // block) * block
        line = strip_rows[r * width // block][:, at : at + width]
        line = jnp.where(sub == 6, jnp.broadcast_to(land[r : r + 1], (8, width)), line)
        for d in range(slots):
            pieces_of[d].append(line[:, d * seg : (d + 1) * seg])
    mine = jnp.zeros((8, tile_points), F32)
    for d in range(slots):
        mine = mine + (me == d).astype(F32) * jnp.concatenate(pieces_of[d], 1)
    tile[...] = mine

    @pl.when(has_after)
    def _():
        to_after(head, after, 0).wait_recv()
        to_after(east_head, east_after, 2).wait_recv()
        field[:, edge + points :] = after[...]
        east[:, edge + points :] = east_after[...]

    @pl.when(jnp.logical_not(has_after))
    def _():
        field[:, edge + points :] = jnp.zeros((padded, edge), BF16)
        east[:, edge + points :] = jnp.zeros((1, edge), F32)

    @pl.when(has_before)
    def _():
        to_before(tail, before, 1).wait_recv()
        to_before(east_tail, east_before, 3).wait_recv()
        field[:, :edge] = before[...]
        east[:, :edge] = east_before[...]

    @pl.when(jnp.logical_not(has_before))
    def _():
        field[:, :edge] = jnp.zeros((padded, edge), BF16)
        east[:, :edge] = jnp.zeros((1, edge), F32)

    column = lax.broadcasted_iota(jnp.int32, (ROWS, width), 1)

    def shifted(value, by):
        rolled = pltpu.roll(value, by % width, 1)
        inside = (column >= by) if by > 0 else (column < width + by)
        return jnp.where(inside, rolled, 0.0)

    def advect_first(t, carry):
        j = first_order(t)
        base = j * lanes * slots

        def one_group(q, carry):
            here = pl.ds(pl.multiple_of(q * ROWS, ROWS), ROWS)
            tap = taps[me, here, :]

            def wide(i):
                return jnp.broadcast_to(tap[:, i : i + 1], (ROWS, width))

            speed_east, speed_north = wide(0), wide(1)
            row_tap = [wide(2 + i) for i in range(5)]
            col_tap = [wide(7 + i) for i in range(5)]
            masked = {}
            flow = {}
            done = []
            for r in range(-2, chunk_rows + 2):
                at = pl.ds(pl.multiple_of(base + (r + 2) * width, 128), width)
                masked[r] = field[here, at].astype(F32)
                flow[r] = (speed_east + east[:, at]) * masked[r]
                c = r - 2
                if c < 0:
                    continue
                at = pl.ds(pl.multiple_of(base + c * width, 128), width)
                m = masked.pop(c)
                along = (speed_north + north[:, at]) * m
                total = m
                for i in range(5):
                    total = total - row_tap[i] * flow[c - 2 + i]
                total = total - col_tap[2] * along
                for i in (0, 1, 3, 4):
                    total = total - col_tap[i] * shifted(along, 2 - i)
                flow.pop(c - 2)
                done.append(total * land_row[:, at])
                if len(done) == per_tile:
                    lane = (c + 1 - per_tile) * seg
                    for d in range(slots):
                        blocks[d, j, here, lane : lane + 128] = jnp.concatenate(
                            [line[:, d * seg : (d + 1) * seg] for line in done], 1
                        ).astype(BF16)
                    done = []
            return carry

        lax.fori_loop(0, groups, one_group, 0)
        for delta in range(1, slots):
            inward(j, delta).start()
        return carry

    lax.fori_loop(0, chunks, advect_first, 0)

    @pl.when(jnp.logical_not(has_left))
    def _():
        col_in[:, 0] = jnp.zeros_like(col_in[:, 0])

    @pl.when(jnp.logical_not(has_right))
    def _():
        col_in[:, 1] = jnp.zeros_like(col_in[:, 1])

    zeros = jnp.zeros((padded, 128), F32)

    def clear(g, carry):
        @pl.when(jnp.logical_not(has_before))
        def _():
            fluxx[g, :, :128] = zeros

        @pl.when(jnp.logical_not(has_after))
        def _():
            fluxx[g, :, 128 + tile_points :] = zeros

        return carry

    lax.fori_loop(0, slots, clear, 0)
    for j in range(chunks):
        got[j, me] = blocks[me, j]

    def project(values, step, j):
        every = values.reshape(slots * padded, lanes)
        projected = jnp.dot(proj[...], every, preferred_element_type=F32)
        cubed = (projected * projected * projected).astype(BF16)
        more = jnp.dot(outer[...], every, preferred_element_type=F32)
        more = more + jnp.dot(inner[...], cubed, preferred_element_type=F32)
        half = more.shape[0] // 2
        payload = more[:half] + more[half:]
        pay[step, j, :half] = payload
        return cubed, payload

    def send_payload(step):
        whole_pay = jnp.concatenate([pay[step, j] for j in range(chunks)], 1)
        for s in range(slots):
            value = jnp.zeros((whole_pay.shape[0], part), F32)
            for b in range(slots):
                value = value + (owners[s] == b).astype(F32) * whole_pay[:, b * part : (b + 1) * part]
            pay_out[step, s] = value.astype(BF16)
        pay_in[step, me] = pay_out[step, me]
        for delta in range(1, slots):
            pay_over(step, delta).start()

    def source_first(t):
        j = first_order(t)
        for delta in range(1, slots):
            inward(j, delta).wait_recv()
        cubed, payload = project(got[j], 0, j)
        own = tile[:, pl.ds(pl.multiple_of(j * lanes, 128), lanes)]
        u0, v0, u1, v1 = own[0:1], own[1:2], own[2:3], own[3:4]
        mix, depth = own[4:5], own[5:6]
        live = (depth > 0.5).astype(F32)
        below = mix * (depth > 1.5).astype(F32)
        floor = mix * ((depth > 0.5) & (depth < 1.5)).astype(F32)
        drift_u, drift_v = payload[0:1], payload[layers : layers + 1]
        stress_u, stress_v = payload[2 * layers : 2 * layers + 1], payload[2 * layers + 1 : 2 * layers + 2]
        new_u = live * (u0 + coriolis * (v0 + drift_v) - below * (u0 - u1) - floor * u0 + stress_u)
        new_v = live * (v0 - coriolis * (u0 + drift_u) - below * (v0 - v1) - floor * v0 + stress_v)
        east_here = current_scale * new_u
        north_here = current_scale * new_v

        def one_source(g, carry):
            transfer = jnp.dot(back[g], cubed, preferred_element_type=F32)
            updated = (got[j, g].astype(F32) + source_step * transfer).astype(BF16)
            state[j, g] = updated
            updated = updated.astype(F32)
            along_x = (taps[g, :, 0:1] + east_here) * updated
            fluxx[g, :, pl.ds(pl.multiple_of(128 + j * lanes, 128), lanes)] = along_x
            along_y = ((taps[g, :, 1:2] + north_here) * updated).astype(BF16)
            fluxy[j, g] = along_y
            ends = lax.dot_general(
                pick[...], along_y, (((1,), (1,)), ((), ())), preferred_element_type=F32
            ).astype(BF16)
            edge_rows = ends.shape[0] // 2
            col_out[j, 0, g] = ends[:edge_rows]
            col_out[j, 1, g] = ends[edge_rows:]

            @pl.when(j == 0)
            def _():
                row_out[0, g] = along_x[:, :128].astype(BF16)

            @pl.when(j == chunks - 1)
            def _():
                row_out[1, g] = along_x[:, lanes - 128 :].astype(BF16)

            return carry

        lax.fori_loop(0, slots, one_source, 0)

        @pl.when(has_left)
        def _():
            col_left(j).start()

        @pl.when(has_right)
        def _():
            col_right(j).start()

        @pl.when((j == 0) & has_before)
        def _():
            row_up().start()

        @pl.when((j == chunks - 1) & has_after)
        def _():
            row_down().start()

    lane_at = lax.broadcasted_iota(jnp.int32, (ROWS, 128), 1)

    def advect_second(j):
        @pl.when((j == 0) & has_before)
        def _():
            row_down().wait_recv()

            def put(g, carry):
                fluxx[g, :, :128] = row_in[0, g].astype(F32)
                return carry

            lax.fori_loop(0, slots, put, 0)

        @pl.when((j == chunks - 1) & has_after)
        def _():
            row_up().wait_recv()

            def put(g, carry):
                fluxx[g, :, 128 + tile_points :] = row_in[1, g].astype(F32)
                return carry

            lax.fori_loop(0, slots, put, 0)

        @pl.when(has_left)
        def _():
            col_right(j).wait_recv()

        @pl.when(has_right)
        def _():
            col_left(j).wait_recv()

        start = j * lanes
        land_here = tile[6:7, pl.ds(pl.multiple_of(start, 128), lanes)]

        def one_advect(g, carry):
            ends = jnp.concatenate([col_in[j, 0, g], col_in[j, 1, g]], 0)
            for v in range(tiles):
                inside = jnp.dot(
                    fluxy[j, g, :, v * 128 : (v + 1) * 128], band[...], preferred_element_type=F32
                )
                border = lax.dot_general(
                    ends, spread[:, v * 256 : (v + 1) * 256], (((0,), (0,)), ((), ())),
                    preferred_element_type=F32,
                )
                stencil[:, v * 256 : (v + 1) * 256] = inside + border

            def one_group(q, carry):
                here = pl.ds(pl.multiple_of(q * ROWS, ROWS), ROWS)
                tap = taps[g, here, :]

                def wide(i):
                    return jnp.broadcast_to(tap[:, i : i + 1], (ROWS, 128))

                row_tap = [wide(2 + i) for i in range(5)]
                northward = wide(7) != 0.0
                flow = {
                    v: fluxx[g, here, pl.ds(pl.multiple_of(128 + start + v * 128, 128), 128)]
                    for v in range(-1, tiles + 1)
                }
                rolled = {}

                def moved(v, by):
                    amount = abs(by)
                    step = 1 if by > 0 else -1
                    if amount == 128:
                        return flow[v + step]
                    shift = (-by) % 128
                    for w in (v, v + step):
                        if (w, shift) not in rolled:
                            rolled[w, shift] = pltpu.roll(flow[w], shift, 1)
                    own = (lane_at < 128 - by) if by > 0 else (lane_at >= amount)
                    return jnp.where(own, rolled[v, shift], rolled[v + step, shift])

                for v in range(tiles):
                    total = state[j, g, here, v * 128 : (v + 1) * 128].astype(F32)
                    for i in range(5):
                        value = flow[v] if i == 2 else moved(v, (i - 2) * seg)
                        total = total - row_tap[i] * value
                    both = stencil[here, v * 256 : (v + 1) * 256]
                    along = jnp.where(northward, both[:, :128], both[:, 128:])
                    total = total - along * (1.0 / 6.0)
                    total = total * land_here[:, v * 128 : (v + 1) * 128]
                    drift[g, here, v * 128 : (v + 1) * 128] = total.astype(BF16)
                return carry

            lax.fori_loop(0, groups, one_group, 0)
            return carry

        lax.fori_loop(0, slots, one_advect, 0)

    def source_second(t):
        j = flip(t)
        advect_second(j)
        cubed, _ = project(drift[...], 1, j)

        @pl.when(t == chunks - 1)
        def _():
            send_payload(1)

        for delta in range(slots):
            g = peer(delta)
            transfer = jnp.dot(back[g], cubed, preferred_element_type=F32)
            updated = (drift[g].astype(F32) + source_step * transfer).astype(BF16)
            if delta:
                made[j, g] = updated
                homeward(j, delta).start()
            else:
                returned[j, g] = updated

    pay[:, :, pay.shape[2] - 8 :] = jnp.zeros_like(pay[:, :, pay.shape[2] - 8 :])

    def middle(u, carry):
        @pl.when(u < chunks)
        def _():
            source_first(u)

        @pl.when(u == chunks - 1)
        def _():
            send_payload(0)

        @pl.when(u > 0)
        def _():
            source_second(u - 1)

        return carry

    lax.fori_loop(0, chunks + 1, middle, 0)

    layer = lax.broadcasted_iota(jnp.int32, (layers, block), 0)
    depth = active[...]
    live = (layer < depth).astype(F32)
    bottom = (layer == depth - 1).astype(F32)
    top = (layer == 0).astype(F32)
    mix = mixing[...]
    upper = mix * ((layer + 1 < depth) & (layer < layers - 1)).astype(F32)

    def mixed(value):
        between = upper * (value - pltpu.roll(value, layers - 1, 0))
        return pltpu.roll(between, 1, 0) - between - mix * bottom * value

    old = (velocity[0], velocity[1])
    for step in range(STEPS):
        for delta in range(1, slots):
            pay_over(step, delta).wait_recv()
        lines = []
        for r in range(block_rows):
            for d in range(slots):
                lines.append(pay_in[step, d].astype(F32)[:, r * seg : (r + 1) * seg])
        payload = jnp.concatenate(lines, 1)
        drift_east = payload[:layers]
        drift_north = payload[layers : 2 * layers]
        stress_east = payload[2 * layers : 2 * layers + 1]
        stress_north = payload[2 * layers + 1 : 2 * layers + 2]
        old_east, old_north = old
        old = (
            live * (old_east + coriolis * (old_north + drift_north) + mixed(old_east) + top * stress_east),
            live * (old_north - coriolis * (old_east + drift_east) + mixed(old_north) + top * stress_north),
        )
    new_velocity[0] = old[0]
    new_velocity[1] = old[1]

    def unpack(t, carry):
        j = flip(t)
        for delta in range(1, slots):
            homeward(j, delta).wait_recv()

        def one_group(q, carry):
            here = pl.ds(pl.multiple_of(q * ROWS, ROWS), ROWS)
            parts = [returned[j, d, here, :].astype(F32) for d in range(slots)]
            for k in range(chunk_rows):
                line = jnp.concatenate([p[:, k * seg : (k + 1) * seg] for p in parts], 1)
                at = pl.ds(pl.multiple_of((j * chunk_rows + k) * width, 128), width)
                field[here, at] = line.astype(BF16)
            return carry

        lax.fori_loop(0, groups, one_group, 0)
        return carry

    lax.fori_loop(0, chunks, unpack, 0)

    def unturned(at, count):
        value = jnp.concatenate([field[at, r * width : (r + 1) * width] for r in range(rows)], 0)
        back_again = jnp.dot(unturn[: count * rows], value, preferred_element_type=F32)
        return back_again.astype(BF16).reshape(count, rows, width)

    def unturn_group(q, carry):
        at = pl.ds(pl.multiple_of(q * ROWS, ROWS), ROWS)
        out[at] = unturned(at, ROWS)
        return carry

    lax.fori_loop(0, whole_groups, unturn_group, 0)
    if rest:
        out[whole_groups * ROWS :] = unturned(slice(whole_groups * ROWS, padded), rest)

    @pl.when(has_before)
    def _():
        to_before(head, after, 0).wait_send()
        to_before(east_head, east_after, 2).wait_send()
        row_up().wait_send()

    @pl.when(has_after)
    def _():
        to_after(tail, before, 1).wait_send()
        to_after(east_tail, east_before, 3).wait_send()
        row_down().wait_send()

    for j in range(chunks):
        for delta in range(1, slots):
            inward(j, delta).wait_send()
            homeward(j, delta).wait_send()

        @pl.when(has_left)
        def _():
            col_left(j).wait_send()

        @pl.when(has_right)
        def _():
            col_right(j).wait_send()

    for step in range(STEPS):
        for delta in range(1, slots):
            pay_over(step, delta).wait_send()


def whole(count, memory=pltpu.VMEM):
    return [pl.BlockSpec(memory_space=memory)] * count


def body(spectrum, land_sea, owners, proj_weight, back_weight, ocean_vel, mixing, active_layers):
    comps, rows, width = spectrum.shape
    slots = lax.axis_size("spec")
    points = rows * width
    block = points // slots
    seg = width // slots
    tile_points = rows * seg
    lanes = 256 if tile_points % 256 == 0 else tile_points
    chunks = tile_points // lanes
    chunk_rows = lanes // seg
    layers = mixing.shape[0]
    rank_rows = proj_weight.shape[0]
    padded = -(-comps // ROWS) * ROWS
    edge = 2 * width
    edge_rows = max(ROWS, 2 * chunk_rows)
    part = block // slots

    def grouped(table):
        result = np.zeros((table.shape[0], slots, padded), table.dtype)
        result[:, :, :comps] = table.reshape(table.shape[0], slots, comps)
        return result.reshape(table.shape[0], slots * padded)

    taps = np.zeros((slots, padded, 12), np.float32)
    taps[:, :comps] = tap_table().reshape(slots, comps, 12)
    drift_rows, stress_rows = coupling_tables(layers)
    zeros = np.zeros((6, K), np.float32)
    outer = grouped(two_pieces(np.concatenate([drift_rows, zeros, zeros[:2]], 0)))
    through = jnp.dot(
        jnp.asarray(np.concatenate([source_step * drift_rows, stress_rows, zeros], 0)),
        back_weight.astype(F32),
        precision=lax.Precision.HIGHEST,
    )
    first = lax.reduce_precision(through, 8, 7)
    inner = jnp.concatenate([first, through - first], 0).astype(BF16)
    pad = ((0, 0), (0, 0), (0, padded - comps))
    proj = jnp.pad(proj_weight.reshape(rank_rows, slots, comps), pad).reshape(rank_rows, slots * padded)
    pad = ((0, 0), (0, padded - comps), (0, 0))
    back = jnp.pad(back_weight.reshape(slots, comps, rank_rows), pad)
    band, spread, pick = stencil_tables(seg, chunk_rows, edge_rows)
    turn = turn_table(rows)

    velocity = ocean_vel.reshape(2, layers, block)
    exchange = pltpu.VMEM((chunks, slots, padded, lanes), BF16)
    pay_rows = -(-(2 * layers + 2) // 16) * 16
    state, velocity = pl.pallas_call(
        functools.partial(steps_kernel, (comps, rows, width, slots)),
        out_shape=(
            jax.ShapeDtypeStruct((comps, rows, width), BF16),
            jax.ShapeDtypeStruct((2, layers, block), F32),
        ),
        in_specs=whole(1, pltpu.SMEM) + whole(15),
        out_specs=tuple(whole(2)),
        scratch_shapes=[
            pltpu.VMEM((padded, points + 2 * edge), BF16),
            pltpu.VMEM((1, points + 2 * edge), F32),
            pltpu.VMEM((1, points), F32),
            pltpu.VMEM((1, points), F32),
            pltpu.VMEM((8, block), F32),
            pltpu.VMEM((slots, 8, block), F32),
            pltpu.VMEM((8, tile_points), F32),
            pltpu.VMEM((slots, chunks, padded, lanes), BF16),
            exchange,
            exchange,
            pltpu.VMEM((slots, padded, tile_points + 256), F32),
            exchange,
            pltpu.VMEM((slots, padded, lanes), BF16),
            pltpu.VMEM((padded, 2 * lanes), F32),
            exchange,
            exchange,
            pltpu.VMEM((STEPS, chunks, pay_rows, lanes), F32),
            pltpu.VMEM((STEPS, slots, pay_rows, part), BF16),
            pltpu.VMEM((STEPS, slots, pay_rows, part), BF16),
            pltpu.VMEM((2, slots, padded, 128), BF16),
            pltpu.VMEM((2, slots, padded, 128), BF16),
            pltpu.VMEM((chunks, 2, slots, edge_rows, padded), BF16),
            pltpu.VMEM((chunks, 2, slots, edge_rows, padded), BF16),
        ]
        + [pltpu.VMEM((padded, edge), BF16)] * 4
        + [pltpu.VMEM((1, edge), F32)] * 4
        + [pltpu.SemaphoreType.DMA((chunks, slots))] * 4
        + [pltpu.SemaphoreType.DMA((slots,))] * 2
        + [pltpu.SemaphoreType.DMA((4,))] * 2
        + [pltpu.SemaphoreType.DMA((2,))] * 2
        + [pltpu.SemaphoreType.DMA((chunks, 2))] * 2
        + [pltpu.SemaphoreType.DMA((STEPS, slots))] * 2,
        compiler_params=pltpu.CompilerParams(
            vmem_limit_bytes=VMEM_LIMIT, collective_id=0, has_side_effects=True
        ),
        name="steps",
    )(owners, spectrum, land_sea, velocity, mixing.reshape(layers, block), active_layers.reshape(1, block),
      jnp.asarray(taps), proj, back, jnp.asarray(outer), inner, jnp.asarray(turn),
      jnp.asarray(np.ascontiguousarray(turn.T)), jnp.asarray(band), jnp.asarray(spread), jnp.asarray(pick))
    return (state, velocity.reshape(ocean_vel.shape))


def solution(mesh):
    placed = (
        P("spec", "space", None),
        P("space", None),
        P(),
        P(),
        P(),
        P(None, None, "spec", "space", None),
        P(None, "spec", "space", None),
        P("spec", "space", None),
    )
    return jax.shard_map(
        body,
        mesh=mesh,
        in_specs=placed,
        out_specs=(P("spec", "space", None), P(None, None, "spec", "space", None)),
        check_vma=False,
    )
```

```python
import functools
import math

import jax
import jax.numpy as jnp
import numpy as np
from jax import lax
from jax.experimental import pallas as pl
from jax.experimental.pallas import tpu as pltpu
from jax.sharding import PartitionSpec as P

NDIR = 36
NFREQ = 36
K = NDIR * NFREQ
STEPS = 2

courant_scale = 0.5
current_scale = 0.15
source_step = 0.25
coriolis = 0.3
stress_scale = 0.5
drift_scale = 4.0

MESH = pl.DeviceIdType.MESH
F32 = jnp.float32
BF16 = jnp.bfloat16
VMEM_LIMIT = 60 * 1024 * 1024
ROWS = 16


def tap_table():
    component = np.arange(K)
    frequency = component // NDIR
    direction = component % NDIR
    angle = (direction + 0.5) * (2.0 * math.pi / NDIR)
    speed = courant_scale * np.exp(-2.0 * frequency / NFREQ)
    eastward = (4 * direction + 2 < NDIR) | (4 * direction + 2 > 3 * NDIR)
    northward = 2 * direction + 1 < NDIR
    forward = (1.0 / 6.0, -1.0, 0.5, 2.0 / 6.0, 0.0)
    backward = (0.0, -2.0 / 6.0, -0.5, 1.0, -1.0 / 6.0)
    columns = [speed * np.cos(angle), speed * np.sin(angle)]
    for mask in (eastward, northward):
        for f, b in zip(forward, backward):
            columns.append(np.where(mask, f, b))
    return np.stack(columns, 1).astype(np.float32)


def coupling_tables(layers):
    component = np.arange(K)
    frequency = component // NDIR
    angle = (component % NDIR + 0.5) * (2.0 * math.pi / NDIR)
    wavenum = 0.02 * np.exp(6.0 * frequency / NFREQ)
    depth = np.arange(layers)[:, None] + 0.5
    decay_rows = wavenum[None, :] ** 1.5 * np.exp(-2.0 * wavenum[None, :] * depth)
    decay_rows = decay_rows / np.sqrt(np.sum(decay_rows * decay_rows, axis=1, keepdims=True))
    drift_rows = drift_scale * np.concatenate(
        [decay_rows * np.cos(angle)[None, :], decay_rows * np.sin(angle)[None, :]], 0
    )
    stress = wavenum / np.sqrt(np.sum(wavenum * wavenum))
    stress_rows = -stress_scale * np.stack([stress * np.cos(angle), stress * np.sin(angle)], 0)
    return (drift_rows.astype(np.float32), stress_rows.astype(np.float32))


def two_pieces(rows):
    first = rows.astype(BF16)
    second = (rows - first.astype(np.float32)).astype(BF16)
    return np.concatenate([first, second], 0)


FORWARD = (1, -6, 3, 2, 0)
BACKWARD = (0, -2, -3, 6, -1)


def stencil_tables(seg, width, rows_in_chunk, edge_rows):
    lanes = rows_in_chunk * seg
    inside = np.zeros((4, lanes + 256, lanes), np.float32)
    across = np.zeros((2, width, width), np.float32)
    spread = np.zeros((2, 2 * edge_rows, lanes), np.float32)
    pick = np.zeros((2 * edge_rows, lanes), np.float32)
    for v, taps in enumerate((FORWARD, BACKWARD)):
        for b in range(lanes):
            for k in range(-2, 3):
                inside[v, 128 + b + k * seg, b] = taps[k + 2]
                if b // seg == (b + k) // seg:
                    inside[2 + v, b + k, b] = taps[k + 2]
        for b in range(width):
            for k in range(-2, 3):
                if 0 <= b + k < width:
                    across[v, b + k, b] = taps[k + 2]
        for k in range(rows_in_chunk):
            for i in range(2):
                for c in range(seg):
                    for row, offset in ((k * 2 + i, i - 2 - c), (edge_rows + k * 2 + i, seg + i - c)):
                        if abs(offset) <= 2:
                            spread[v, row, k * seg + c] = taps[offset + 2]
    for k in range(rows_in_chunk):
        for i in range(2):
            pick[k * 2 + i, k * seg + i] = 1
            pick[edge_rows + k * 2 + i, k * seg + seg - 2 + i] = 1
    inside = np.concatenate([inside[0], inside[1], inside[2, :lanes], inside[3, :lanes]], 0)
    tables = (inside, across.reshape(2 * width, width), spread.reshape(-1, lanes), pick)
    return [table.astype(BF16) for table in tables]


def turn_table(rows):
    table = np.zeros((rows * ROWS, rows * ROWS), np.float32)
    for c in range(ROWS):
        for r in range(rows):
            table[r * ROWS + c, c * rows + r] = 1
    return table.astype(BF16)


def steps_kernel(
    sizes, owners, spectrum, land_sea, velocity, mixing, active, taps, proj, back, outer, inner, turn, unturn,
    inside, across, spread, pick, north_mask,
    out, new_velocity,
    field, east, north, land_row, surface, surfaces, tile,
    flow_rows, flow_cols, blocks, got, state, flux_e, flux_w, flux_n, flux_s, drift, made, returned,
    pay, pay_out, pay_in, row_out, row_in, col_out, col_in,
    head, tail, before, after, east_head, east_tail, east_before, east_after,
    send_in, recv_in, send_back, recv_back, send_top, recv_top, send_edge, recv_edge,
    send_row, recv_row, send_col, recv_col, send_pay, recv_pay,
):
    comps, rows, width, slots = sizes
    padded = field.shape[0]
    chunks, lanes = got.shape[0], got.shape[3]
    seg = width // slots
    per_tile = 128 // seg
    tiles = lanes // 128
    chunk_rows = lanes // seg
    block = velocity.shape[2]
    block_rows = block // width
    part = block_rows * seg
    points = rows * width
    tile_points = rows * seg
    layers = mixing.shape[0]
    groups = padded // ROWS
    me = lax.axis_index("spec")
    strip = lax.axis_index("space")
    strips = lax.axis_size("space")
    edge = 2 * width
    has_before = strip > 0
    has_after = strip < strips - 1
    has_left = me > 0
    has_right = me < slots - 1
    odd = lax.rem(strip, 2) == 1

    def peer(delta):
        return lax.rem(me + delta, slots)

    def flip(base):
        return jnp.where(odd, chunks - 1 - base, base)

    def first_order(t):
        return flip(jnp.where(t < 2, 1 - t, t) if chunks > 1 else t)

    def copy(source, target, send, receive, device):
        return pltpu.make_async_remote_copy(
            src_ref=source, dst_ref=target, send_sem=send, recv_sem=receive,
            device_id=device, device_id_type=MESH,
        )

    def inward(j, delta):
        return copy(
            blocks.at[peer(delta), j], got.at[j, me],
            send_in.at[j, delta], recv_in.at[j, delta], {"spec": peer(delta)},
        )

    def homeward(j, delta):
        return copy(
            made.at[j, peer(delta)], returned.at[j, me],
            send_back.at[j, delta], recv_back.at[j, delta], {"spec": peer(delta)},
        )

    def upward(delta):
        return copy(
            surface, surfaces.at[me], send_top.at[delta], recv_top.at[delta], {"spec": peer(delta)}
        )

    def pay_over(step, delta):
        return copy(
            pay_out.at[step, peer(delta)], pay_in.at[step, me],
            send_pay.at[step, delta], recv_pay.at[step, delta], {"spec": peer(delta)},
        )

    def to_before(source, target, i):
        return copy(source, target, send_edge.at[i], recv_edge.at[i], {"space": strip - 1})

    def to_after(source, target, i):
        return copy(source, target, send_edge.at[i], recv_edge.at[i], {"space": strip + 1})

    def row_up():
        return copy(row_out.at[0], row_in.at[1], send_row.at[0], recv_row.at[0], {"space": strip - 1})

    def row_down():
        return copy(row_out.at[1], row_in.at[0], send_row.at[1], recv_row.at[1], {"space": strip + 1})

    def col_left(j):
        return copy(col_out.at[j, 0], col_in.at[j, 1], send_col.at[j, 0], recv_col.at[j, 0], {"spec": me - 1})

    def col_right(j):
        return copy(col_out.at[j, 1], col_in.at[j, 0], send_col.at[j, 1], recv_col.at[j, 1], {"spec": me + 1})

    barrier = pltpu.get_barrier_semaphore()
    for delta in range(1, slots):
        pl.semaphore_signal(barrier, inc=1, device_id={"spec": peer(delta)}, device_id_type=MESH)

    @pl.when(has_before)
    def _():
        pl.semaphore_signal(barrier, inc=1, device_id={"space": strip - 1}, device_id_type=MESH)

    @pl.when(has_after)
    def _():
        pl.semaphore_signal(barrier, inc=1, device_id={"space": strip + 1}, device_id_type=MESH)

    surface[0:1, :] = velocity[0, 0:1, :]
    surface[1:2, :] = velocity[1, 0:1, :]
    surface[2:3, :] = velocity[0, 1:2, :]
    surface[3:4, :] = velocity[1, 1:2, :]
    surface[4:5, :] = mixing[0:1, :]
    surface[5:6, :] = active[...].astype(F32)
    surface[6:8, :] = jnp.zeros((2, block), F32)
    expected = slots - 1 + has_before.astype(jnp.int32) + has_after.astype(jnp.int32)
    pl.semaphore_wait(barrier, expected)
    for delta in range(1, slots):
        upward(delta).start()
    surfaces[me] = surface[...]

    land = land_sea[...].astype(F32)
    for r in range(rows):
        land_row[:, r * width : (r + 1) * width] = land[r : r + 1, :]

    def turned(value, count):
        wet = (value.astype(F32) * land[None]).astype(BF16).reshape(count * rows, width)
        return jnp.dot(turn[:, : count * rows], wet, preferred_element_type=F32).astype(BF16)

    def place_turned(value, at):
        for r in range(rows):
            field[at, (r + 2) * width : (r + 3) * width] = value[r * ROWS : (r + 1) * ROWS]

    def turn_group(q, carry):
        at = pl.ds(pl.multiple_of(q * ROWS, ROWS), ROWS)
        place_turned(turned(spectrum[at], ROWS), at)
        return carry

    whole_groups = comps // ROWS
    rest = comps - whole_groups * ROWS
    lax.fori_loop(0, whole_groups, turn_group, 0)
    if rest:
        place_turned(turned(spectrum[whole_groups * ROWS :], rest), slice(whole_groups * ROWS, padded))
    head[...] = field[:, edge : 2 * edge]
    tail[...] = field[:, points : points + edge]

    @pl.when(has_before)
    def _():
        to_before(head, after, 0).start()

    @pl.when(has_after)
    def _():
        to_after(tail, before, 1).start()

    for delta in range(1, slots):
        upward(delta).wait()
    strip_rows = []
    for b in range(slots):
        here = jnp.zeros((8, block), F32)
        for s in range(slots):
            here = here + (owners[s] == b).astype(F32) * surfaces[s]
        strip_rows.append(here)
        east[:, edge + b * block : edge + (b + 1) * block] = current_scale * here[0:1]
        north[:, b * block : (b + 1) * block] = current_scale * here[1:2]
    east_head[...] = east[:, edge : 2 * edge]
    east_tail[...] = east[:, points : points + edge]

    @pl.when(has_before)
    def _():
        to_before(east_head, east_after, 2).start()

    @pl.when(has_after)
    def _():
        to_after(east_tail, east_before, 3).start()

    sub = lax.broadcasted_iota(jnp.int32, (8, width), 0)
    pieces_of = [[] for _ in range(slots)]
    for r in range(rows):
        at = r * width - (r * width // block) * block
        line = strip_rows[r * width // block][:, at : at + width]
        line = jnp.where(sub == 6, jnp.broadcast_to(land[r : r + 1], (8, width)), line)
        for d in range(slots):
            pieces_of[d].append(line[:, d * seg : (d + 1) * seg])
    mine = jnp.zeros((8, tile_points), F32)
    for d in range(slots):
        mine = mine + (me == d).astype(F32) * jnp.concatenate(pieces_of[d], 1)
    tile[...] = mine

    def take_halos():
        @pl.when(has_after)
        def _():
            to_after(head, after, 0).wait_recv()
            to_after(east_head, east_after, 2).wait_recv()
            field[:, edge + points :] = after[...]
            east[:, edge + points :] = east_after[...]

        @pl.when(jnp.logical_not(has_after))
        def _():
            field[:, edge + points :] = jnp.zeros((padded, edge), BF16)
            east[:, edge + points :] = jnp.zeros((1, edge), F32)

        @pl.when(has_before)
        def _():
            to_before(tail, before, 1).wait_recv()
            to_before(east_tail, east_before, 3).wait_recv()
            field[:, :edge] = before[...]
            east[:, :edge] = east_before[...]

        @pl.when(jnp.logical_not(has_before))
        def _():
            field[:, :edge] = jnp.zeros((padded, edge), BF16)
            east[:, :edge] = jnp.zeros((1, edge), F32)

    def grouped(body):
        many = 3 if groups % 3 == 0 else 1

        def some(q, carry):
            for i in range(many):
                body(pl.ds(pl.multiple_of((q * many + i) * ROWS, ROWS), ROWS))
            return carry

        lax.fori_loop(0, groups // many, some, 0)

    halves = width // 128

    def wide(tap, i):
        return jnp.broadcast_to(tap[:, i : i + 1], (ROWS, 128))

    def advect_first(t, carry):
        @pl.when(t == min(1, chunks - 1))
        def _():
            take_halos()

        j = first_order(t)
        base = j * lanes * slots

        def lane(row, half):
            return pl.ds(pl.multiple_of(base + row * width + half * 128, 128), 128)

        def along_columns(here):
            tap = taps[me, here, :]
            speed = wide(tap, 1)
            northward = wide(tap, 7) != 0.0
            for c in range(chunk_rows):
                for half in range(halves):
                    along = (speed + north[:, lane(c, half)]) * field[here, lane(c + 2, half)].astype(F32)
                    at = half * 128
                    flow_cols[c, here, at : at + 128] = jnp.where(northward, along, 0.0).astype(BF16)
                    at = width + half * 128
                    flow_cols[c, here, at : at + 128] = jnp.where(northward, 0.0, along).astype(BF16)

        grouped(along_columns)

        def one_row(c, carry):
            flow_rows[c] = jnp.dot(flow_cols[c], across[...], preferred_element_type=F32)
            return carry

        lax.fori_loop(0, chunk_rows, one_row, 0)

        def along_rows(here):
            tap = taps[me, here, :]
            speed = wide(tap, 0)
            row_tap = [wide(tap, 2 + i) for i in range(5)]
            done = {}
            for half in range(halves):
                masked = {}
                flow = {}
                for r in range(-2, chunk_rows + 2):
                    masked[r] = field[here, lane(r + 2, half)].astype(F32)
                    flow[r] = (speed + east[:, lane(r + 2, half)]) * masked[r]
                    c = r - 2
                    if c < 0:
                        continue
                    total = masked.pop(c) - flow_rows[c, here, half * 128 : (half + 1) * 128] * (1.0 / 6.0)
                    for i in range(5):
                        total = total - row_tap[i] * flow[c - 2 + i]
                    flow.pop(c - 2)
                    done[c, half] = total * land_row[:, lane(c, half)]
            for d in range(slots):
                half, at = d * seg // 128, d * seg % 128
                for v in range(tiles):
                    blocks[d, j, here, v * 128 : (v + 1) * 128] = jnp.concatenate(
                        [done[v * per_tile + h, half][:, at : at + seg] for h in range(per_tile)], 1
                    ).astype(BF16)

        grouped(along_rows)
        for delta in range(1, slots):
            inward(j, delta).start()
        return carry

    lax.fori_loop(0, chunks, advect_first, 0)

    @pl.when(jnp.logical_not(has_left))
    def _():
        col_in[:, 0] = jnp.zeros_like(col_in[:, 0])

    @pl.when(jnp.logical_not(has_right))
    def _():
        col_in[:, 1] = jnp.zeros_like(col_in[:, 1])

    zeros = jnp.zeros((padded, 128), BF16)

    def clear(g, carry):
        for flux in (flux_e, flux_w):

            @pl.when(jnp.logical_not(has_before))
            def _():
                flux[g, :, :128] = zeros

            @pl.when(jnp.logical_not(has_after))
            def _():
                flux[g, :, 128 + tile_points :] = zeros

        return carry

    lax.fori_loop(0, slots, clear, 0)
    for j in range(chunks):
        got[j, me] = blocks[me, j]

    def project(values, step, j):
        every = values.reshape(slots * padded, lanes)
        projected = jnp.dot(proj[...], every, preferred_element_type=F32)
        cubed = (projected * projected * projected).astype(BF16)
        more = jnp.dot(outer[...], every, preferred_element_type=F32)
        more = more + jnp.dot(inner[...], cubed, preferred_element_type=F32)
        half = more.shape[0] // 2
        payload = more[:half] + more[half:]
        pay[step, j, :half] = payload
        return cubed, payload

    def send_payload(step):
        whole_pay = jnp.concatenate([pay[step, j] for j in range(chunks)], 1)
        for s in range(slots):
            value = jnp.zeros((whole_pay.shape[0], part), F32)
            for b in range(slots):
                value = value + (owners[s] == b).astype(F32) * whole_pay[:, b * part : (b + 1) * part]
            pay_out[step, s] = value.astype(BF16)
        pay_in[step, me] = pay_out[step, me]
        for delta in range(1, slots):
            pay_over(step, delta).start()

    def source_first(t):
        j = first_order(t)
        for delta in range(1, slots):
            inward(j, delta).wait_recv()
        cubed, payload = project(got[j], 0, j)
        own = tile[:, pl.ds(pl.multiple_of(j * lanes, 128), lanes)]
        u0, v0, u1, v1 = own[0:1], own[1:2], own[2:3], own[3:4]
        mix, depth = own[4:5], own[5:6]
        live = (depth > 0.5).astype(F32)
        below = mix * (depth > 1.5).astype(F32)
        floor = mix * ((depth > 0.5) & (depth < 1.5)).astype(F32)
        drift_u, drift_v = payload[0:1], payload[layers : layers + 1]
        stress_u, stress_v = payload[2 * layers : 2 * layers + 1], payload[2 * layers + 1 : 2 * layers + 2]
        new_u = live * (u0 + coriolis * (v0 + drift_v) - below * (u0 - u1) - floor * u0 + stress_u)
        new_v = live * (v0 - coriolis * (u0 + drift_u) - below * (v0 - v1) - floor * v0 + stress_v)
        east_here = current_scale * new_u
        north_here = current_scale * new_v

        def one_source(g, carry):
            transfer = jnp.dot(back[g], cubed, preferred_element_type=F32)
            updated = (got[j, g].astype(F32) + source_step * transfer).astype(BF16)
            state[j, g] = updated
            updated = updated.astype(F32)
            along_x = (taps[g, :, 0:1] + east_here) * updated
            eastward = taps[g, :, 2:3] != 0.0
            at = pl.ds(pl.multiple_of(128 + j * lanes, 128), lanes)
            flux_e[g, :, at] = jnp.where(eastward, along_x, 0.0).astype(BF16)
            flux_w[g, :, at] = jnp.where(eastward, 0.0, along_x).astype(BF16)
            along_y = (taps[g, :, 1:2] + north_here) * updated
            northward = taps[g, :, 7:8] != 0.0
            flux_n[j, g] = jnp.where(northward, along_y, 0.0).astype(BF16)
            flux_s[j, g] = jnp.where(northward, 0.0, along_y).astype(BF16)
            along_y = along_y.astype(BF16)
            ends = lax.dot_general(
                pick[...], along_y, (((1,), (1,)), ((), ())), preferred_element_type=F32
            ).astype(BF16)
            edge_rows = ends.shape[0] // 2
            col_out[j, 0, g] = ends[:edge_rows]
            col_out[j, 1, g] = ends[edge_rows:]

            @pl.when(j == 0)
            def _():
                row_out[0, g] = along_x[:, :128].astype(BF16)

            @pl.when(j == chunks - 1)
            def _():
                row_out[1, g] = along_x[:, lanes - 128 :].astype(BF16)

            return carry

        lax.fori_loop(0, slots, one_source, 0)

        @pl.when(has_left)
        def _():
            col_left(j).start()

        @pl.when(has_right)
        def _():
            col_right(j).start()

        @pl.when((j == 0) & has_before)
        def _():
            row_up().start()

        @pl.when((j == chunks - 1) & has_after)
        def _():
            row_down().start()

    def advect_second(j):
        def put(place, at):
            def one(g, carry):
                eastward = taps[g, :, 2:3] != 0.0
                value = row_in[place, g].astype(F32)
                flux_e[g, :, at : at + 128] = jnp.where(eastward, value, 0.0).astype(BF16)
                flux_w[g, :, at : at + 128] = jnp.where(eastward, 0.0, value).astype(BF16)
                return carry

            lax.fori_loop(0, slots, one, 0)

        @pl.when((j == 0) & has_before)
        def _():
            row_down().wait_recv()
            put(0, 0)

        @pl.when((j == chunks - 1) & has_after)
        def _():
            row_up().wait_recv()
            put(1, 128 + tile_points)

        @pl.when(has_left)
        def _():
            col_right(j).wait_recv()

        @pl.when(has_right)
        def _():
            col_left(j).wait_recv()

        start = pl.multiple_of(j * lanes, 128)
        land_here = tile[6:7, pl.ds(start, lanes)]

        def one_advect(g, carry):
            rows_at = pl.ds(start, lanes + 256)
            every = jnp.concatenate(
                [flux_e[g, :, rows_at], flux_w[g, :, rows_at], flux_n[j, g], flux_s[j, g]], 1
            )
            ends = jnp.concatenate([col_in[j, 0, g], col_in[j, 1, g]], 0)
            ends_north = ends * north_mask[g]
            ends = jnp.concatenate([ends_north, ends - ends_north], 0)
            change = jnp.dot(every, inside[...], preferred_element_type=F32) + lax.dot_general(
                ends, spread[...], (((0,), (0,)), ((), ())), preferred_element_type=F32
            )
            total = (state[j, g].astype(F32) - change * (1.0 / 6.0)) * land_here
            drift[g] = total.astype(BF16)
            return carry

        lax.fori_loop(0, slots, one_advect, 0)

    def source_second(t):
        j = flip(t)
        advect_second(j)
        cubed, _ = project(drift[...], 1, j)

        @pl.when(t == chunks - 1)
        def _():
            send_payload(1)

        for delta in range(slots):
            g = peer(delta)
            transfer = jnp.dot(back[g], cubed, preferred_element_type=F32)
            updated = (drift[g].astype(F32) + source_step * transfer).astype(BF16)
            if delta:
                made[j, g] = updated
                homeward(j, delta).start()
            else:
                returned[j, g] = updated

    pay[:, :, pay.shape[2] - 8 :] = jnp.zeros_like(pay[:, :, pay.shape[2] - 8 :])

    def middle(u, carry):
        @pl.when(u < chunks)
        def _():
            source_first(u)

        @pl.when(u == chunks - 1)
        def _():
            send_payload(0)

        @pl.when(u > 0)
        def _():
            source_second(u - 1)

        return carry

    lax.fori_loop(0, chunks + 1, middle, 0)

    layer = lax.broadcasted_iota(jnp.int32, (layers, block), 0)
    depth = active[...]
    live = (layer < depth).astype(F32)
    bottom = (layer == depth - 1).astype(F32)
    top = (layer == 0).astype(F32)
    mix = mixing[...]
    upper = mix * ((layer + 1 < depth) & (layer < layers - 1)).astype(F32)

    def mixed(value):
        between = upper * (value - pltpu.roll(value, layers - 1, 0))
        return pltpu.roll(between, 1, 0) - between - mix * bottom * value

    old = (velocity[0], velocity[1])
    for step in range(STEPS):
        for delta in range(1, slots):
            pay_over(step, delta).wait_recv()
        lines = []
        for r in range(block_rows):
            for d in range(slots):
                lines.append(pay_in[step, d].astype(F32)[:, r * seg : (r + 1) * seg])
        payload = jnp.concatenate(lines, 1)
        drift_east = payload[:layers]
        drift_north = payload[layers : 2 * layers]
        stress_east = payload[2 * layers : 2 * layers + 1]
        stress_north = payload[2 * layers + 1 : 2 * layers + 2]
        old_east, old_north = old
        old = (
            live * (old_east + coriolis * (old_north + drift_north) + mixed(old_east) + top * stress_east),
            live * (old_north - coriolis * (old_east + drift_east) + mixed(old_north) + top * stress_north),
        )
    new_velocity[0] = old[0]
    new_velocity[1] = old[1]

    def unpack(t, carry):
        j = flip(t)
        for delta in range(1, slots):
            homeward(j, delta).wait_recv()

        def one_group(here):
            parts = [returned[j, d, here, :].astype(F32) for d in range(slots)]
            for k in range(chunk_rows):
                line = jnp.concatenate([p[:, k * seg : (k + 1) * seg] for p in parts], 1)
                at = pl.ds(pl.multiple_of((j * chunk_rows + k) * width, 128), width)
                field[here, at] = line.astype(BF16)

        grouped(one_group)
        return carry

    lax.fori_loop(0, chunks, unpack, 0)

    def unturned(at, count):
        value = jnp.concatenate([field[at, r * width : (r + 1) * width] for r in range(rows)], 0)
        back_again = jnp.dot(unturn[: count * rows], value, preferred_element_type=F32)
        return back_again.astype(BF16).reshape(count, rows, width)

    def unturn_group(q, carry):
        at = pl.ds(pl.multiple_of(q * ROWS, ROWS), ROWS)
        out[at] = unturned(at, ROWS)
        return carry

    lax.fori_loop(0, whole_groups, unturn_group, 0)
    if rest:
        out[whole_groups * ROWS :] = unturned(slice(whole_groups * ROWS, padded), rest)

    @pl.when(has_before)
    def _():
        to_before(head, after, 0).wait_send()
        to_before(east_head, east_after, 2).wait_send()
        row_up().wait_send()

    @pl.when(has_after)
    def _():
        to_after(tail, before, 1).wait_send()
        to_after(east_tail, east_before, 3).wait_send()
        row_down().wait_send()

    for j in range(chunks):
        for delta in range(1, slots):
            inward(j, delta).wait_send()
            homeward(j, delta).wait_send()

        @pl.when(has_left)
        def _():
            col_left(j).wait_send()

        @pl.when(has_right)
        def _():
            col_right(j).wait_send()

    for step in range(STEPS):
        for delta in range(1, slots):
            pay_over(step, delta).wait_send()


def whole(count, memory=pltpu.VMEM):
    return [pl.BlockSpec(memory_space=memory)] * count


def body(spectrum, land_sea, owners, proj_weight, back_weight, ocean_vel, mixing, active_layers):
    comps, rows, width = spectrum.shape
    slots = lax.axis_size("spec")
    points = rows * width
    block = points // slots
    seg = width // slots
    tile_points = rows * seg
    lanes = 256 if tile_points % 256 == 0 else tile_points
    chunks = tile_points // lanes
    chunk_rows = lanes // seg
    layers = mixing.shape[0]
    rank_rows = proj_weight.shape[0]
    padded = -(-comps // ROWS) * ROWS
    edge = 2 * width
    edge_rows = max(ROWS, 2 * chunk_rows)
    part = block // slots

    def by_slot(table):
        result = np.zeros((table.shape[0], slots, padded), table.dtype)
        result[:, :, :comps] = table.reshape(table.shape[0], slots, comps)
        return result.reshape(table.shape[0], slots * padded)

    taps = np.zeros((slots, padded, 12), np.float32)
    taps[:, :comps] = tap_table().reshape(slots, comps, 12)
    drift_rows, stress_rows = coupling_tables(layers)
    zeros = np.zeros((6, K), np.float32)
    outer = by_slot(two_pieces(np.concatenate([drift_rows, zeros, zeros[:2]], 0)))
    through = jnp.dot(
        jnp.asarray(np.concatenate([source_step * drift_rows, stress_rows, zeros], 0)),
        back_weight.astype(F32),
        precision=lax.Precision.HIGHEST,
    )
    first = lax.reduce_precision(through, 8, 7)
    inner = jnp.concatenate([first, through - first], 0).astype(BF16)
    pad = ((0, 0), (0, 0), (0, padded - comps))
    proj = jnp.pad(proj_weight.reshape(rank_rows, slots, comps), pad).reshape(rank_rows, slots * padded)
    pad = ((0, 0), (0, padded - comps), (0, 0))
    back = jnp.pad(back_weight.reshape(slots, comps, rank_rows), pad)
    tables = stencil_tables(seg, width, chunk_rows, edge_rows)
    north_mask = (taps[:, :, 7] != 0).astype(BF16).reshape(slots, 1, padded)
    turn = turn_table(rows)

    velocity = ocean_vel.reshape(2, layers, block)
    exchange = pltpu.VMEM((chunks, slots, padded, lanes), BF16)
    pay_rows = -(-(2 * layers + 2) // 16) * 16
    state, velocity = pl.pallas_call(
        functools.partial(steps_kernel, (comps, rows, width, slots)),
        out_shape=(
            jax.ShapeDtypeStruct((comps, rows, width), BF16),
            jax.ShapeDtypeStruct((2, layers, block), F32),
        ),
        in_specs=whole(1, pltpu.SMEM) + whole(17),
        out_specs=tuple(whole(2)),
        scratch_shapes=[
            pltpu.VMEM((padded, points + 2 * edge), BF16),
            pltpu.VMEM((1, points + 2 * edge), F32),
            pltpu.VMEM((1, points), F32),
            pltpu.VMEM((1, points), F32),
            pltpu.VMEM((8, block), F32),
            pltpu.VMEM((slots, 8, block), F32),
            pltpu.VMEM((8, tile_points), F32),
            pltpu.VMEM((chunk_rows, padded, width), F32),
            pltpu.VMEM((chunk_rows, padded, 2 * width), BF16),
            pltpu.VMEM((slots, chunks, padded, lanes), BF16),
            exchange,
            exchange,
            pltpu.VMEM((slots, padded, tile_points + 256), BF16),
            pltpu.VMEM((slots, padded, tile_points + 256), BF16),
            exchange,
            exchange,
            pltpu.VMEM((slots, padded, lanes), BF16),
            exchange,
            exchange,
            pltpu.VMEM((STEPS, chunks, pay_rows, lanes), F32),
            pltpu.VMEM((STEPS, slots, pay_rows, part), BF16),
            pltpu.VMEM((STEPS, slots, pay_rows, part), BF16),
            pltpu.VMEM((2, slots, padded, 128), BF16),
            pltpu.VMEM((2, slots, padded, 128), BF16),
            pltpu.VMEM((chunks, 2, slots, edge_rows, padded), BF16),
            pltpu.VMEM((chunks, 2, slots, edge_rows, padded), BF16),
        ]
        + [pltpu.VMEM((padded, edge), BF16)] * 4
        + [pltpu.VMEM((1, edge), F32)] * 4
        + [pltpu.SemaphoreType.DMA((chunks, slots))] * 4
        + [pltpu.SemaphoreType.DMA((slots,))] * 2
        + [pltpu.SemaphoreType.DMA((4,))] * 2
        + [pltpu.SemaphoreType.DMA((2,))] * 2
        + [pltpu.SemaphoreType.DMA((chunks, 2))] * 2
        + [pltpu.SemaphoreType.DMA((STEPS, slots))] * 2,
        compiler_params=pltpu.CompilerParams(
            vmem_limit_bytes=VMEM_LIMIT, collective_id=0, has_side_effects=True
        ),
        name="steps",
    )(owners, spectrum, land_sea, velocity, mixing.reshape(layers, block), active_layers.reshape(1, block),
      jnp.asarray(taps), proj, back, jnp.asarray(outer), inner, jnp.asarray(turn),
      jnp.asarray(np.ascontiguousarray(turn.T)), *[jnp.asarray(table) for table in tables],
      jnp.asarray(north_mask))
    return (state, velocity.reshape(ocean_vel.shape))


def solution(mesh):
    placed = (
        P("spec", "space", None),
        P("space", None),
        P(),
        P(),
        P(),
        P(None, None, "spec", "space", None),
        P(None, "spec", "space", None),
        P("spec", "space", None),
    )
    return jax.shard_map(
        body,
        mesh=mesh,
        in_specs=placed,
        out_specs=(P("spec", "space", None), P(None, None, "spec", "space", None)),
        check_vma=False,
    )
```

```python
import functools
import math

import jax
import jax.numpy as jnp
import numpy as np
from jax import lax
from jax.experimental import pallas as pl
from jax.experimental.pallas import tpu as pltpu
from jax.sharding import PartitionSpec as P

NDIR = 36
NFREQ = 36
K = NDIR * NFREQ
STEPS = 2

courant_scale = 0.5
current_scale = 0.15
source_step = 0.25
coriolis = 0.3
stress_scale = 0.5
drift_scale = 4.0

MESH = pl.DeviceIdType.MESH
F32 = jnp.float32
BF16 = jnp.bfloat16
VMEM_LIMIT = 60 * 1024 * 1024
ROWS = 16


def tap_table():
    component = np.arange(K)
    frequency = component // NDIR
    direction = component % NDIR
    angle = (direction + 0.5) * (2.0 * math.pi / NDIR)
    speed = courant_scale * np.exp(-2.0 * frequency / NFREQ)
    eastward = (4 * direction + 2 < NDIR) | (4 * direction + 2 > 3 * NDIR)
    northward = 2 * direction + 1 < NDIR
    forward = (1.0 / 6.0, -1.0, 0.5, 2.0 / 6.0, 0.0)
    backward = (0.0, -2.0 / 6.0, -0.5, 1.0, -1.0 / 6.0)
    columns = [speed * np.cos(angle), speed * np.sin(angle)]
    for mask in (eastward, northward):
        for f, b in zip(forward, backward):
            columns.append(np.where(mask, f, b))
    return np.stack(columns, 1).astype(np.float32)


def coupling_tables(layers):
    component = np.arange(K)
    frequency = component // NDIR
    angle = (component % NDIR + 0.5) * (2.0 * math.pi / NDIR)
    wavenum = 0.02 * np.exp(6.0 * frequency / NFREQ)
    depth = np.arange(layers)[:, None] + 0.5
    decay_rows = wavenum[None, :] ** 1.5 * np.exp(-2.0 * wavenum[None, :] * depth)
    decay_rows = decay_rows / np.sqrt(np.sum(decay_rows * decay_rows, axis=1, keepdims=True))
    drift_rows = drift_scale * np.concatenate(
        [decay_rows * np.cos(angle)[None, :], decay_rows * np.sin(angle)[None, :]], 0
    )
    stress = wavenum / np.sqrt(np.sum(wavenum * wavenum))
    stress_rows = -stress_scale * np.stack([stress * np.cos(angle), stress * np.sin(angle)], 0)
    return (drift_rows.astype(np.float32), stress_rows.astype(np.float32))


def two_pieces(rows):
    first = rows.astype(BF16)
    second = (rows - first.astype(np.float32)).astype(BF16)
    return np.concatenate([first, second], 0)


FORWARD = (1, -6, 3, 2, 0)
BACKWARD = (0, -2, -3, 6, -1)


def stencil_tables(seg, width, rows_in_chunk, edge_rows, pack):
    lanes = rows_in_chunk * seg
    inside = np.zeros((4, lanes + 256, lanes), np.float32)
    across = np.zeros((2, width, width), np.float32)
    spread = np.zeros((2, 2 * edge_rows, lanes), np.float32)
    pick = np.zeros((2 * edge_rows, lanes), np.float32)
    for v, taps in enumerate((FORWARD, BACKWARD)):
        for b in range(lanes):
            for k in range(-2, 3):
                inside[v, 128 + b + k * seg, b] = taps[k + 2]
                if b // seg == (b + k) // seg:
                    inside[2 + v, b + k, b] = taps[k + 2]
        for b in range(width):
            for k in range(-2, 3):
                if 0 <= b + k < width:
                    across[v, b + k, b] = taps[k + 2]
        for k in range(rows_in_chunk):
            for i in range(2):
                for c in range(seg):
                    for row, offset in ((k * 2 + i, i - 2 - c), (edge_rows + k * 2 + i, seg + i - c)):
                        if abs(offset) <= 2:
                            spread[v, row, k * seg + c] = taps[offset + 2]
    for k in range(rows_in_chunk):
        for i in range(2):
            pick[k * 2 + i, k * seg + i] = 1
            pick[edge_rows + k * 2 + i, k * seg + seg - 2 + i] = 1
    inside = np.concatenate([inside[0], inside[1], inside[2, :lanes], inside[3, :lanes]], 0)
    held = np.zeros((pack, 2, 2, pack, edge_rows, lanes), np.float32)
    for i in range(pack):
        held[i, :, :, i] = spread.reshape(2, 2, edge_rows, lanes)
    held = held.reshape(pack, 4 * pack * edge_rows, lanes)
    tables = (inside, across.reshape(2 * width, width), held, pick)
    return [table.astype(BF16) for table in tables]


def turn_table(first, second):
    table = np.zeros((first * second, first * second), np.float32)
    for c in range(first):
        for r in range(second):
            table[r * first + c, c * second + r] = 1
    return table.astype(BF16)


def steps_kernel(
    sizes, owners, spectrum, land_sea, velocity, mixing, active, taps, turn, unturn, pay_turn,
    across, spread, pick, north_mask, proj_raw, back_raw, outer_raw, through_raw, inside_raw,
    out, new_velocity,
    field, east, north, land_row, surface, surfaces, deeper, deepers, strip_rows, tile,
    proj_held, back_held, outer, through, inside, proj, back, inner,
    flow_rows, flow_cols, blocks, got, state, flux_e, flux_w, flux_n, flux_s, drift, made, returned,
    pay, pay_out, pay_in, row_out, row_in, col_out, col_in,
    head, tail, before, after, east_head, east_tail, east_before, east_after,
    send_in, recv_in, send_back, recv_back, send_top, recv_top, send_deep, recv_deep, send_edge, recv_edge,
    send_row, recv_row, send_col, recv_col, send_pay, recv_pay, held_sem,
):
    comps, rows, width, slots = sizes
    padded = field.shape[0]
    chunks, lanes = got.shape[0], got.shape[3]
    seg = width // slots
    per_tile = 128 // seg
    tiles = lanes // 128
    chunk_rows = lanes // seg
    high = velocity.shape[2]
    block = high * 128
    block_rows = block // width
    part = block_rows * seg
    points = rows * width
    tile_points = rows * seg
    layers = mixing.shape[0]
    groups = padded // ROWS
    pack = slots // col_out.shape[2]
    me = lax.axis_index("spec")
    strip = lax.axis_index("space")
    strips = lax.axis_size("space")
    edge = 2 * width
    has_before = strip > 0
    has_after = strip < strips - 1
    has_left = me > 0
    has_right = me < slots - 1
    odd = lax.rem(strip, 2) == 1

    def peer(delta):
        return lax.rem(me + delta, slots)

    def flip(base):
        return jnp.where(odd, chunks - 1 - base, base)

    def first_order(t):
        return flip(jnp.where(t < 2, 1 - t, t) if chunks > 1 else t)

    def copy(source, target, send, receive, device):
        return pltpu.make_async_remote_copy(
            src_ref=source, dst_ref=target, send_sem=send, recv_sem=receive,
            device_id=device, device_id_type=MESH,
        )

    def inward(j, delta):
        return copy(
            blocks.at[peer(delta), j], got.at[j, me],
            send_in.at[j, delta], recv_in.at[j, delta], {"spec": peer(delta)},
        )

    def homeward(j, delta):
        return copy(
            made.at[j, peer(delta)], returned.at[j, me],
            send_back.at[j, delta], recv_back.at[j, delta], {"spec": peer(delta)},
        )

    def upward(delta):
        return copy(
            surface, surfaces.at[me], send_top.at[delta], recv_top.at[delta], {"spec": peer(delta)}
        )

    def downward(delta):
        return copy(
            deeper, deepers.at[me], send_deep.at[delta], recv_deep.at[delta], {"spec": peer(delta)}
        )

    held = [
        pltpu.make_async_copy(source, target, held_sem.at[i])
        for i, (source, target) in enumerate((
            (proj_raw, proj_held), (back_raw, back_held), (outer_raw, outer), (through_raw, through),
            (inside_raw, inside),
        ))
    ]
    for each in held:
        each.start()

    def pay_over(step, delta):
        return copy(
            pay_out.at[step, peer(delta)], pay_in.at[step, me],
            send_pay.at[step, delta], recv_pay.at[step, delta], {"spec": peer(delta)},
        )

    def to_before(source, target, i):
        return copy(source, target, send_edge.at[i], recv_edge.at[i], {"space": strip - 1})

    def to_after(source, target, i):
        return copy(source, target, send_edge.at[i], recv_edge.at[i], {"space": strip + 1})

    def row_up():
        return copy(row_out.at[0], row_in.at[1], send_row.at[0], recv_row.at[0], {"space": strip - 1})

    def row_down():
        return copy(row_out.at[1], row_in.at[0], send_row.at[1], recv_row.at[1], {"space": strip + 1})

    def col_left(j):
        return copy(col_out.at[j, 0], col_in.at[j, 1], send_col.at[j, 0], recv_col.at[j, 0], {"spec": me - 1})

    def col_right(j):
        return copy(col_out.at[j, 1], col_in.at[j, 0], send_col.at[j, 1], recv_col.at[j, 1], {"spec": me + 1})

    barrier = pltpu.get_barrier_semaphore()
    for delta in range(1, slots):
        pl.semaphore_signal(barrier, inc=1, device_id={"spec": peer(delta)}, device_id_type=MESH)

    @pl.when(has_before)
    def _():
        pl.semaphore_signal(barrier, inc=1, device_id={"space": strip - 1}, device_id_type=MESH)

    @pl.when(has_after)
    def _():
        pl.semaphore_signal(barrier, inc=1, device_id={"space": strip + 1}, device_id_type=MESH)

    for i in range(2):
        surface[i] = velocity[i, 0]
        deeper[i] = velocity[i, 1]
    deeper[2] = mixing[0]
    deeper[3] = active[...].astype(F32)
    expected = slots - 1 + has_before.astype(jnp.int32) + has_after.astype(jnp.int32)
    pl.semaphore_wait(barrier, expected)
    for delta in range(1, slots):
        upward(delta).start()
    for delta in range(1, slots):
        downward(delta).start()
    surfaces[me] = surface[...]
    deepers[me] = deeper[...]

    land = land_sea[...].astype(F32)
    for r in range(rows):
        land_row[:, r * width : (r + 1) * width] = land[r : r + 1, :]

    def turned(value, count):
        wet = (value.astype(F32) * land[None]).astype(BF16).reshape(count * rows, width)
        return jnp.dot(turn[:, : count * rows], wet, preferred_element_type=F32).astype(BF16)

    def place_turned(value, at):
        for r in range(rows):
            field[at, (r + 2) * width : (r + 3) * width] = value[r * ROWS : (r + 1) * ROWS]

    def by_groups(count, body):
        many = next(n for n in (4, 5, 3, 2, 1) if count % n == 0)

        def some(q, carry):
            for i in range(many):
                body(pl.ds(pl.multiple_of((q * many + i) * ROWS, ROWS), ROWS))
            return carry

        lax.fori_loop(0, count // many, some, 0)

    def turn_group(at):
        place_turned(turned(spectrum[at], ROWS), at)

    whole_groups = comps // ROWS
    rest = comps - whole_groups * ROWS
    by_groups(whole_groups, turn_group)
    if rest:
        place_turned(turned(spectrum[whole_groups * ROWS :], rest), slice(whole_groups * ROWS, padded))
    head[...] = field[:, edge : 2 * edge]
    tail[...] = field[:, points : points + edge]

    @pl.when(has_before)
    def _():
        to_before(head, after, 0).start()

    @pl.when(has_after)
    def _():
        to_after(tail, before, 1).start()

    for delta in range(1, slots):
        upward(delta).wait()
    for b in range(slots):
        here = jnp.zeros((2, high, 128), F32)
        for s in range(slots):
            here = here + (owners[s] == b).astype(F32) * surfaces[s]
        for i in range(high):
            at = b * block + i * 128
            strip_rows[0:1, at : at + 128] = here[0, i : i + 1]
            strip_rows[1:2, at : at + 128] = here[1, i : i + 1]
    east[:, edge : edge + points] = current_scale * strip_rows[0:1, :]
    north[...] = current_scale * strip_rows[1:2, :]
    east_head[...] = east[:, edge : 2 * edge]
    east_tail[...] = east[:, points : points + edge]

    @pl.when(has_before)
    def _():
        to_before(east_head, east_after, 2).start()

    @pl.when(has_after)
    def _():
        to_after(east_tail, east_before, 3).start()

    def take_halos():
        @pl.when(has_after)
        def _():
            to_after(head, after, 0).wait_recv()
            to_after(east_head, east_after, 2).wait_recv()
            field[:, edge + points :] = after[...]
            east[:, edge + points :] = east_after[...]

        @pl.when(jnp.logical_not(has_after))
        def _():
            field[:, edge + points :] = jnp.zeros((padded, edge), BF16)
            east[:, edge + points :] = jnp.zeros((1, edge), F32)

        @pl.when(has_before)
        def _():
            to_before(tail, before, 1).wait_recv()
            to_before(east_tail, east_before, 3).wait_recv()
            field[:, :edge] = before[...]
            east[:, :edge] = east_before[...]

        @pl.when(jnp.logical_not(has_before))
        def _():
            field[:, :edge] = jnp.zeros((padded, edge), BF16)
            east[:, :edge] = jnp.zeros((1, edge), F32)

    def grouped(body):
        many = 3 if groups % 3 == 0 else 1

        def some(q, carry):
            for i in range(many):
                body(pl.ds(pl.multiple_of((q * many + i) * ROWS, ROWS), ROWS))
            return carry

        lax.fori_loop(0, groups // many, some, 0)

    halves = width // 128

    def wide(tap, i):
        return jnp.broadcast_to(tap[:, i : i + 1], (ROWS, 128))

    def advect_first(t, carry):
        @pl.when(t == min(1, chunks - 1))
        def _():
            take_halos()

        j = first_order(t)
        base = j * lanes * slots

        def lane(row, half):
            return pl.ds(pl.multiple_of(base + row * width + half * 128, 128), 128)

        def along_columns(here):
            tap = taps[me, here, :]
            speed = wide(tap, 1)
            northward = wide(tap, 7) != 0.0
            for c in range(chunk_rows):
                for half in range(halves):
                    along = (speed + north[:, lane(c, half)]) * field[here, lane(c + 2, half)].astype(F32)
                    at = half * 128
                    flow_cols[c, here, at : at + 128] = jnp.where(northward, along, 0.0).astype(BF16)
                    at = width + half * 128
                    flow_cols[c, here, at : at + 128] = jnp.where(northward, 0.0, along).astype(BF16)

        grouped(along_columns)

        def one_row(c, carry):
            flow_rows[c] = jnp.dot(flow_cols[c], across[...], preferred_element_type=F32)
            return carry

        lax.fori_loop(0, chunk_rows, one_row, 0)

        def along_rows(here):
            tap = taps[me, here, :]
            speed = wide(tap, 0)
            row_tap = [wide(tap, 2 + i) for i in range(5)]
            done = {}
            for half in range(halves):
                masked = {}
                flow = {}
                for r in range(-2, chunk_rows + 2):
                    masked[r] = field[here, lane(r + 2, half)].astype(F32)
                    flow[r] = (speed + east[:, lane(r + 2, half)]) * masked[r]
                    c = r - 2
                    if c < 0:
                        continue
                    total = masked.pop(c) - flow_rows[c, here, half * 128 : (half + 1) * 128] * (1.0 / 6.0)
                    for i in range(5):
                        total = total - row_tap[i] * flow[c - 2 + i]
                    flow.pop(c - 2)
                    done[c, half] = total * land_row[:, lane(c, half)]
            for d in range(slots):
                half, at = d * seg // 128, d * seg % 128
                for v in range(tiles):
                    blocks[d, j, here, v * 128 : (v + 1) * 128] = jnp.concatenate(
                        [done[v * per_tile + h, half][:, at : at + seg] for h in range(per_tile)], 1
                    ).astype(BF16)

        grouped(along_rows)
        for delta in range(1, slots):
            inward(j, delta).start()
        return carry

    lax.fori_loop(0, chunks, advect_first, 0)

    @pl.when(jnp.logical_not(has_left))
    def _():
        col_in[:, 0] = jnp.zeros_like(col_in[:, 0])

    @pl.when(jnp.logical_not(has_right))
    def _():
        col_in[:, 1] = jnp.zeros_like(col_in[:, 1])

    zeros = jnp.zeros((padded, 128), BF16)

    def clear(g, carry):
        for flux in (flux_e, flux_w):

            @pl.when(jnp.logical_not(has_before))
            def _():
                flux[g, :, :128] = zeros

            @pl.when(jnp.logical_not(has_after))
            def _():
                flux[g, :, 128 + tile_points :] = zeros

        return carry

    lax.fori_loop(0, slots, clear, 0)
    for j in range(chunks):
        got[j, me] = blocks[me, j]

    for delta in range(1, slots):
        downward(delta).wait()
    for b in range(slots):
        here = jnp.zeros((4, high, 128), F32)
        for s in range(slots):
            here = here + (owners[s] == b).astype(F32) * deepers[s]
        for f in range(4):
            for i in range(high):
                at = b * block + i * 128
                strip_rows[2 + f : 3 + f, at : at + 128] = here[f, i : i + 1]
    strip_rows[6:7, :] = land_row[...]
    strip_rows[7:8, :] = land_row[...]
    pieces_of = [[] for _ in range(slots)]
    for r in range(rows):
        line = strip_rows[:, r * width : (r + 1) * width]
        for d in range(slots):
            pieces_of[d].append(line[:, d * seg : (d + 1) * seg])
    mine = jnp.zeros((8, tile_points), F32)
    for d in range(slots):
        mine = mine + (me == d).astype(F32) * jnp.concatenate(pieces_of[d], 1)
    tile[...] = mine
    for each in held:
        each.wait()
    eye = lax.broadcasted_iota(jnp.int32, (proj.shape[1], proj.shape[1]), 0)
    eye = (eye == lax.broadcasted_iota(jnp.int32, eye.shape, 1)).astype(F32).astype(BF16)
    mixed_rows = jnp.zeros((through.shape[1], proj.shape[1]), F32)
    for g in range(slots):
        low = g * comps // ROWS * ROWS
        window = min(padded + ROWS, slots * comps - low)
        row = lax.broadcasted_iota(jnp.int32, (padded, window), 0)
        shift = lax.broadcasted_iota(jnp.int32, (padded, window), 1) - row
        shift = ((shift == g * comps - low) & (row < comps)).astype(F32).astype(BF16)
        back[g] = jnp.dot(shift, back_held[low : low + window], preferred_element_type=F32).astype(BF16)
        aligned = jnp.dot(shift, proj_held[low : low + window], preferred_element_type=F32).astype(BF16)
        proj[g] = lax.dot_general(
            eye, aligned, (((1,), (1,)), ((), ())), preferred_element_type=F32
        ).astype(BF16)
        mixed_rows = mixed_rows + jnp.dot(through[g], back[g], preferred_element_type=F32)
    half = mixed_rows.shape[0] // 2
    mixed_rows = mixed_rows[:half] + mixed_rows[half:]
    first = mixed_rows.astype(BF16)
    inner[:half] = first
    inner[half:] = (mixed_rows - first.astype(F32)).astype(BF16)

    def project(values, step, j):
        projected = jnp.dot(proj[0], values[0], preferred_element_type=F32)
        more = jnp.dot(outer[0], values[0], preferred_element_type=F32)
        for g in range(1, slots):
            projected = projected + jnp.dot(proj[g], values[g], preferred_element_type=F32)
            more = more + jnp.dot(outer[g], values[g], preferred_element_type=F32)
        cubed = (projected * projected * projected).astype(BF16)
        more = more + jnp.dot(inner[...], cubed, preferred_element_type=F32)
        half = more.shape[0] // 2
        payload = more[:half] + more[half:]
        pay[step, j] = payload
        return cubed, payload

    def send_payload(step):
        whole_pay = jnp.concatenate([pay[step, j] for j in range(chunks)], 1)
        for s in range(slots):
            value = jnp.zeros((whole_pay.shape[0], part), F32)
            for b in range(slots):
                value = value + (owners[s] == b).astype(F32) * whole_pay[:, b * part : (b + 1) * part]
            pay_out[step, s] = value.astype(BF16)
        pay_in[step, me] = pay_out[step, me]
        for delta in range(1, slots):
            pay_over(step, delta).start()

    def source_first(t):
        j = first_order(t)
        for delta in range(1, slots):
            inward(j, delta).wait_recv()
        cubed, payload = project(got.at[j], 0, j)
        own = tile[:, pl.ds(pl.multiple_of(j * lanes, 128), lanes)]
        u0, v0, u1, v1 = own[0:1], own[1:2], own[2:3], own[3:4]
        mix, depth = own[4:5], own[5:6]
        live = (depth > 0.5).astype(F32)
        below = mix * (depth > 1.5).astype(F32)
        floor = mix * ((depth > 0.5) & (depth < 1.5)).astype(F32)
        push_u, push_v = payload[0:1], payload[layers : layers + 1]
        new_u = live * (u0 + coriolis * v0 - below * (u0 - u1) - floor * u0 + push_u)
        new_v = live * (v0 - coriolis * u0 - below * (v0 - v1) - floor * v0 + push_v)
        east_here = current_scale * new_u
        north_here = current_scale * new_v

        def one_group(g):
            transfer = jnp.dot(back[g], cubed, preferred_element_type=F32)
            updated = (got[j, g].astype(F32) + source_step * transfer).astype(BF16)
            state[j, g] = updated
            updated = updated.astype(F32)
            along_x = (taps[g, :, 0:1] + east_here) * updated
            eastward = taps[g, :, 2:3] != 0.0
            at = pl.ds(pl.multiple_of(128 + j * lanes, 128), lanes)
            flux_e[g, :, at] = jnp.where(eastward, along_x, 0.0).astype(BF16)
            flux_w[g, :, at] = jnp.where(eastward, 0.0, along_x).astype(BF16)
            along_y = (taps[g, :, 1:2] + north_here) * updated
            northward = taps[g, :, 7:8] != 0.0
            flux_n[j, g] = jnp.where(northward, along_y, 0.0).astype(BF16)
            flux_s[j, g] = jnp.where(northward, 0.0, along_y).astype(BF16)
            along_y = along_y.astype(BF16)
            ends = lax.dot_general(
                pick[...], along_y, (((1,), (1,)), ((), ())), preferred_element_type=F32
            )

            @pl.when(j == 0)
            def _():
                row_out[0, g] = along_x[:, :128].astype(BF16)

            @pl.when(j == chunks - 1)
            def _():
                row_out[1, g] = along_x[:, lanes - 128 :].astype(BF16)

            half = ends.shape[0] // 2
            return ends[:half], ends[half:]

        def one_source(p, carry):
            ends = [one_group(p * pack + i) for i in range(pack)]
            for side in range(2):
                col_out[j, side, p] = jnp.concatenate([both[side] for both in ends], 0).astype(BF16)
            return carry

        lax.fori_loop(0, slots // pack, one_source, 0)

        @pl.when(has_left)
        def _():
            col_left(j).start()

        @pl.when(has_right)
        def _():
            col_right(j).start()

        @pl.when((j == 0) & has_before)
        def _():
            row_up().start()

        @pl.when((j == chunks - 1) & has_after)
        def _():
            row_down().start()

    def advect_second(j):
        def put(place, at):
            def one(g, carry):
                eastward = taps[g, :, 2:3] != 0.0
                value = row_in[place, g].astype(F32)
                flux_e[g, :, at : at + 128] = jnp.where(eastward, value, 0.0).astype(BF16)
                flux_w[g, :, at : at + 128] = jnp.where(eastward, 0.0, value).astype(BF16)
                return carry

            lax.fori_loop(0, slots, one, 0)

        @pl.when((j == 0) & has_before)
        def _():
            row_down().wait_recv()
            put(0, 0)

        @pl.when((j == chunks - 1) & has_after)
        def _():
            row_up().wait_recv()
            put(1, 128 + tile_points)

        @pl.when(has_left)
        def _():
            col_right(j).wait_recv()

        @pl.when(has_right)
        def _():
            col_left(j).wait_recv()

        start = pl.multiple_of(j * lanes, 128)
        land_here = tile[6:7, pl.ds(start, lanes)]

        def one_advect(g, carry):
            rows_at = pl.ds(start, lanes + 256)
            every = jnp.concatenate(
                [flux_e[g, :, rows_at], flux_w[g, :, rows_at], flux_n[j, g], flux_s[j, g]], 1
            )
            ends = jnp.concatenate([col_in[j, 0, g // pack], col_in[j, 1, g // pack]], 0)
            ends_north = ends * north_mask[g]
            ends = jnp.concatenate([ends_north, ends - ends_north], 0)
            change = jnp.dot(every, inside[...], preferred_element_type=F32) + lax.dot_general(
                ends, spread[lax.rem(g, pack)], (((0,), (0,)), ((), ())), preferred_element_type=F32
            )
            total = (state[j, g].astype(F32) - change * (1.0 / 6.0)) * land_here
            drift[g] = total.astype(BF16)
            return carry

        lax.fori_loop(0, slots, one_advect, 0)

    def source_second(t):
        j = flip(t)
        advect_second(j)
        cubed, _ = project(drift, 1, j)

        @pl.when(t == chunks - 1)
        def _():
            send_payload(1)

        for delta in range(slots):
            g = peer(delta)
            transfer = jnp.dot(back[g], cubed, preferred_element_type=F32)
            updated = (drift[g].astype(F32) + source_step * transfer).astype(BF16)
            if delta:
                made[j, g] = updated
                homeward(j, delta).start()
            else:
                returned[j, g] = updated

    def middle(u, carry):
        @pl.when(u < chunks)
        def _():
            source_first(u)

        @pl.when(u == chunks - 1)
        def _():
            send_payload(0)

        @pl.when(u > 0)
        def _():
            source_second(u - 1)

        return carry

    lax.fori_loop(0, chunks + 1, middle, 0)

    layer = lax.broadcasted_iota(jnp.int32, (layers, high, 128), 0)
    depth = active[...][None]
    live = (layer < depth).astype(F32)
    bottom = mixing[...] * (layer == depth - 1).astype(F32)
    upper = mixing[...] * ((layer + 1 < depth) & (layer < layers - 1)).astype(F32)
    nothing = jnp.zeros((1, high, 128), F32)

    def mixed(value):
        between = upper * (value - jnp.concatenate([value[1:], nothing], 0))
        return jnp.concatenate([nothing, between[:-1]], 0) - between - bottom * value

    old = (velocity[0], velocity[1])
    for step in range(STEPS):
        for delta in range(1, slots):
            pay_over(step, delta).wait_recv()
        lines = []
        for i in range(high):
            pieces = []
            for h in range(per_tile):
                r, d = divmod(i * per_tile + h, slots)
                pieces.append(pay_in[step, d].astype(F32)[:, r * seg : (r + 1) * seg])
            lines.append(jnp.concatenate(pieces, 1))
        lines = jnp.concatenate(lines, 0).astype(BF16)
        push = jnp.dot(pay_turn[...], lines, preferred_element_type=F32).reshape(2, layers, high, 128)
        east_old, north_old = old
        old = (
            live * (east_old + coriolis * north_old + mixed(east_old) + push[0]),
            live * (north_old - coriolis * east_old + mixed(north_old) + push[1]),
        )
    new_velocity[0] = old[0]
    new_velocity[1] = old[1]

    def unpack(t, carry):
        j = flip(t)
        for delta in range(1, slots):
            homeward(j, delta).wait_recv()

        def one_group(here):
            parts = [returned[j, d, here, :].astype(F32) for d in range(slots)]
            for k in range(chunk_rows):
                line = jnp.concatenate([p[:, k * seg : (k + 1) * seg] for p in parts], 1)
                at = pl.ds(pl.multiple_of((j * chunk_rows + k) * width, 128), width)
                field[here, at] = line.astype(BF16)

        grouped(one_group)
        return carry

    lax.fori_loop(0, chunks, unpack, 0)

    def unturned(at, count):
        value = jnp.concatenate([field[at, r * width : (r + 1) * width] for r in range(rows)], 0)
        back_again = jnp.dot(unturn[: count * rows], value, preferred_element_type=F32)
        return back_again.astype(BF16).reshape(count, rows, width)

    def unturn_group(at):
        out[at] = unturned(at, ROWS)

    by_groups(whole_groups, unturn_group)
    if rest:
        out[whole_groups * ROWS :] = unturned(slice(whole_groups * ROWS, padded), rest)

    @pl.when(has_before)
    def _():
        to_before(head, after, 0).wait_send()
        to_before(east_head, east_after, 2).wait_send()
        row_up().wait_send()

    @pl.when(has_after)
    def _():
        to_after(tail, before, 1).wait_send()
        to_after(east_tail, east_before, 3).wait_send()
        row_down().wait_send()

    for j in range(chunks):
        for delta in range(1, slots):
            inward(j, delta).wait_send()
            homeward(j, delta).wait_send()

        @pl.when(has_left)
        def _():
            col_left(j).wait_send()

        @pl.when(has_right)
        def _():
            col_right(j).wait_send()

    for step in range(STEPS):
        for delta in range(1, slots):
            pay_over(step, delta).wait_send()


def whole(count, memory=pltpu.VMEM):
    return [pl.BlockSpec(memory_space=memory)] * count


def body(spectrum, land_sea, owners, proj_weight, back_weight, ocean_vel, mixing, active_layers):
    comps, rows, width = spectrum.shape
    slots = lax.axis_size("spec")
    points = rows * width
    block = points // slots
    seg = width // slots
    tile_points = rows * seg
    lanes = 256 if tile_points % 256 == 0 else tile_points
    chunks = tile_points // lanes
    chunk_rows = lanes // seg
    layers = mixing.shape[0]
    rank_rows = proj_weight.shape[0]
    padded = -(-comps // ROWS) * ROWS
    edge = 2 * width
    edge_rows = 2 * chunk_rows
    pack = max(1, ROWS // edge_rows)
    high = block // 128
    part = block // slots

    def by_slot(table):
        result = np.zeros((slots, table.shape[0], padded), table.dtype)
        result[:, :, :comps] = table.reshape(table.shape[0], slots, comps).transpose(1, 0, 2)
        return result

    taps = np.zeros((slots, padded, 12), np.float32)
    taps[:, :comps] = tap_table().reshape(slots, comps, 12)
    drift_rows, stress_rows = coupling_tables(layers)
    push = coriolis * np.concatenate([drift_rows[layers:], -drift_rows[:layers]], 0)
    outer = by_slot(two_pieces(push))
    push = source_step * push
    push[0] += stress_rows[0]
    push[layers] += stress_rows[1]
    through = by_slot(two_pieces(push))
    tables = stencil_tables(seg, width, chunk_rows, edge_rows, pack)
    north_mask = (taps[:, :, 7] != 0).astype(BF16).reshape(slots, 1, padded)
    turn = turn_table(ROWS, rows)
    pay_turn = np.zeros((high * 2 * layers,) * 2, np.float32)
    for l in range(2 * layers):
        for i in range(high):
            pay_turn[l * high + i, i * 2 * layers + l] = 1
    pay_turn = pay_turn.astype(BF16)
    velocity = ocean_vel.reshape(2, layers, high, 128)
    exchange = pltpu.VMEM((chunks, slots, padded, lanes), BF16)
    pay_rows = 2 * layers
    state, velocity = pl.pallas_call(
        functools.partial(steps_kernel, (comps, rows, width, slots)),
        out_shape=(
            jax.ShapeDtypeStruct((comps, rows, width), BF16),
            jax.ShapeDtypeStruct((2, layers, high, 128), F32),
        ),
        in_specs=whole(1, pltpu.SMEM) + whole(13) + whole(5, pl.ANY),
        out_specs=tuple(whole(2)),
        scratch_shapes=[
            pltpu.VMEM((padded, points + 2 * edge), BF16),
            pltpu.VMEM((1, points + 2 * edge), F32),
            pltpu.VMEM((1, points), F32),
            pltpu.VMEM((1, points), F32),
            pltpu.VMEM((2, high, 128), F32),
            pltpu.VMEM((slots, 2, high, 128), F32),
            pltpu.VMEM((4, high, 128), F32),
            pltpu.VMEM((slots, 4, high, 128), F32),
            pltpu.VMEM((8, points), F32),
            pltpu.VMEM((8, tile_points), F32),
            pltpu.VMEM((slots * comps, rank_rows), BF16),
            pltpu.VMEM((slots * comps, rank_rows), BF16),
            pltpu.VMEM(outer.shape, BF16),
            pltpu.VMEM(through.shape, BF16),
            pltpu.VMEM(tables[0].shape, BF16),
            pltpu.VMEM((slots, rank_rows, padded), BF16),
            pltpu.VMEM((slots, padded, rank_rows), BF16),
            pltpu.VMEM((outer.shape[1], rank_rows), BF16),
            pltpu.VMEM((chunk_rows, padded, width), F32),
            pltpu.VMEM((chunk_rows, padded, 2 * width), BF16),
            pltpu.VMEM((slots, chunks, padded, lanes), BF16),
            exchange,
            exchange,
            pltpu.VMEM((slots, padded, tile_points + 256), BF16),
            pltpu.VMEM((slots, padded, tile_points + 256), BF16),
            exchange,
            exchange,
            pltpu.VMEM((slots, padded, lanes), BF16),
            exchange,
            exchange,
            pltpu.VMEM((STEPS, chunks, pay_rows, lanes), F32),
            pltpu.VMEM((STEPS, slots, pay_rows, part), BF16),
            pltpu.VMEM((STEPS, slots, pay_rows, part), BF16),
            pltpu.VMEM((2, slots, padded, 128), BF16),
            pltpu.VMEM((2, slots, padded, 128), BF16),
            pltpu.VMEM((chunks, 2, slots // pack, pack * edge_rows, padded), BF16),
            pltpu.VMEM((chunks, 2, slots // pack, pack * edge_rows, padded), BF16),
        ]
        + [pltpu.VMEM((padded, edge), BF16)] * 4
        + [pltpu.VMEM((1, edge), F32)] * 4
        + [pltpu.SemaphoreType.DMA((chunks, slots))] * 4
        + [pltpu.SemaphoreType.DMA((slots,))] * 4
        + [pltpu.SemaphoreType.DMA((4,))] * 2
        + [pltpu.SemaphoreType.DMA((2,))] * 2
        + [pltpu.SemaphoreType.DMA((chunks, 2))] * 2
        + [pltpu.SemaphoreType.DMA((STEPS, slots))] * 2
        + [pltpu.SemaphoreType.DMA((5,))],
        compiler_params=pltpu.CompilerParams(
            vmem_limit_bytes=VMEM_LIMIT, collective_id=0, has_side_effects=True
        ),
        name="steps",
    )(owners, spectrum, land_sea, velocity, mixing.reshape(layers, high, 128), active_layers.reshape(high, 128),
      *[jnp.asarray(np.ascontiguousarray(table)) for table in (taps, turn, turn.T, pay_turn, *tables[1:], north_mask)],
      proj_weight.T, back_weight, jnp.asarray(outer), jnp.asarray(through), jnp.asarray(tables[0]))
    return (state, velocity.reshape(ocean_vel.shape))


def solution(mesh):
    placed = (
        P("spec", "space", None),
        P("space", None),
        P(),
        P(),
        P(),
        P(None, None, "spec", "space", None),
        P(None, "spec", "space", None),
        P("spec", "space", None),
    )
    return jax.shard_map(
        body,
        mesh=mesh,
        in_specs=placed,
        out_specs=(P("spec", "space", None), P(None, None, "spec", "space", None)),
        check_vma=False,
    )
```

```python
import functools
import math

import jax
import jax.numpy as jnp
import numpy as np
from jax import lax
from jax.experimental import pallas as pl
from jax.experimental.pallas import tpu as pltpu
from jax.sharding import PartitionSpec as P

NDIR = 36
NFREQ = 36
K = NDIR * NFREQ
STEPS = 2

courant_scale = 0.5
current_scale = 0.15
source_step = 0.25
coriolis = 0.3
stress_scale = 0.5
drift_scale = 4.0

MESH = pl.DeviceIdType.MESH
F32 = jnp.float32
BF16 = jnp.bfloat16
VMEM_LIMIT = 60 * 1024 * 1024
ROWS = 16


def tap_table():
    component = np.arange(K)
    frequency = component // NDIR
    direction = component % NDIR
    angle = (direction + 0.5) * (2.0 * math.pi / NDIR)
    speed = courant_scale * np.exp(-2.0 * frequency / NFREQ)
    eastward = (4 * direction + 2 < NDIR) | (4 * direction + 2 > 3 * NDIR)
    northward = 2 * direction + 1 < NDIR
    forward = (1.0 / 6.0, -1.0, 0.5, 2.0 / 6.0, 0.0)
    backward = (0.0, -2.0 / 6.0, -0.5, 1.0, -1.0 / 6.0)
    columns = [speed * np.cos(angle), speed * np.sin(angle)]
    for mask in (eastward, northward):
        for f, b in zip(forward, backward):
            columns.append(np.where(mask, f, b))
    return np.stack(columns, 1).astype(np.float32)


def coupling_tables(layers):
    component = np.arange(K)
    frequency = component // NDIR
    angle = (component % NDIR + 0.5) * (2.0 * math.pi / NDIR)
    wavenum = 0.02 * np.exp(6.0 * frequency / NFREQ)
    depth = np.arange(layers)[:, None] + 0.5
    decay_rows = wavenum[None, :] ** 1.5 * np.exp(-2.0 * wavenum[None, :] * depth)
    decay_rows = decay_rows / np.sqrt(np.sum(decay_rows * decay_rows, axis=1, keepdims=True))
    drift_rows = drift_scale * np.concatenate(
        [decay_rows * np.cos(angle)[None, :], decay_rows * np.sin(angle)[None, :]], 0
    )
    stress = wavenum / np.sqrt(np.sum(wavenum * wavenum))
    stress_rows = -stress_scale * np.stack([stress * np.cos(angle), stress * np.sin(angle)], 0)
    return (drift_rows.astype(np.float32), stress_rows.astype(np.float32))


def two_pieces(rows):
    first = rows.astype(BF16)
    second = (rows - first.astype(np.float32)).astype(BF16)
    return np.concatenate([first, second], 0)


FORWARD = (1, -6, 3, 2, 0)
BACKWARD = (0, -2, -3, 6, -1)


def stencil_tables(seg, width, rows_in_chunk, edge_rows, pack):
    lanes = rows_in_chunk * seg
    inside = np.zeros((4, lanes + 256, lanes), np.float32)
    across = np.zeros((2, width, width), np.float32)
    spread = np.zeros((2, 2 * edge_rows, lanes), np.float32)
    pick = np.zeros((2 * edge_rows, lanes), np.float32)
    for v, taps in enumerate((FORWARD, BACKWARD)):
        for b in range(lanes):
            for k in range(-2, 3):
                inside[v, 128 + b + k * seg, b] = taps[k + 2]
                if b // seg == (b + k) // seg:
                    inside[2 + v, b + k, b] = taps[k + 2]
        for b in range(width):
            for k in range(-2, 3):
                if 0 <= b + k < width:
                    across[v, b + k, b] = taps[k + 2]
        for k in range(rows_in_chunk):
            for i in range(2):
                for c in range(seg):
                    for row, offset in ((k * 2 + i, i - 2 - c), (edge_rows + k * 2 + i, seg + i - c)):
                        if abs(offset) <= 2:
                            spread[v, row, k * seg + c] = taps[offset + 2]
    for k in range(rows_in_chunk):
        for i in range(2):
            pick[k * 2 + i, k * seg + i] = 1
            pick[edge_rows + k * 2 + i, k * seg + seg - 2 + i] = 1
    inside = np.concatenate([inside[0], inside[1], inside[2, :lanes], inside[3, :lanes]], 0)
    held = np.zeros((pack, 2, 2, pack, edge_rows, lanes), np.float32)
    for i in range(pack):
        held[i, :, :, i] = spread.reshape(2, 2, edge_rows, lanes)
    held = held.reshape(pack, 4 * pack * edge_rows, lanes)
    tables = (inside, across.reshape(2 * width, width), held, pick)
    return [table.astype(BF16) for table in tables]


def turn_table(first, second):
    table = np.zeros((first * second, first * second), np.float32)
    for c in range(first):
        for r in range(second):
            table[r * first + c, c * second + r] = 1
    return table.astype(BF16)


def steps_kernel(
    sizes, owners, land_sea, velocity, mixing, active, north_mask,
    spectrum_raw, turn_raw, taps_raw, across_raw,
    proj_raw, back_raw, outer_raw, through_raw, inside_raw, spread_raw, pick_raw, pay_turn_raw, unturn_raw,
    out, new_velocity,
    field, east, north, land_row, surface, surfaces, deeper, deepers, strip_rows, tile,
    spectrum, turn, taps, across, proj_held, back_held, outer, through, inside, spread, pick, pay_turn, unturn,
    proj, back, inner, rest_out, rest_in, rest_made, rest_back,
    flow_rows, flow_cols, blocks, got, state, flux_e, flux_w, flux_n, flux_s, drift, made, returned,
    pay, pay_out, pay_in, row_out, row_in, col_out, col_in,
    head, tail, before, after, east_head, east_tail, east_before, east_after,
    send_in, recv_in, send_back, recv_back, send_top, recv_top, send_deep, recv_deep, send_edge, recv_edge,
    send_row, recv_row, send_col, recv_col, send_pay, recv_pay, held_sem,
):
    comps, rows, width, slots = sizes
    padded = field.shape[0]
    chunks, lanes = got.shape[0], got.shape[3]
    seg = width // slots
    per_tile = 128 // seg
    tiles = lanes // 128
    chunk_rows = lanes // seg
    high = velocity.shape[2]
    block = high * 128
    block_rows = block // width
    part = block_rows * seg
    points = rows * width
    tile_points = rows * seg
    layers = mixing.shape[0]
    groups = padded // ROWS
    pack = slots // col_out.shape[2]
    me = lax.axis_index("spec")
    strip = lax.axis_index("space")
    strips = lax.axis_size("space")
    edge = 2 * width
    has_before = strip > 0
    has_after = strip < strips - 1
    has_left = me > 0
    has_right = me < slots - 1
    odd = lax.rem(strip, 2) == 1

    def peer(delta):
        return lax.rem(me + delta, slots)

    def flip(base):
        return jnp.where(odd, chunks - 1 - base, base)

    def first_order(t):
        return flip(jnp.where(t < 2, 1 - t, t) if chunks > 1 else t)

    def copy(source, target, send, receive, device):
        return pltpu.make_async_remote_copy(
            src_ref=source, dst_ref=target, send_sem=send, recv_sem=receive,
            device_id=device, device_id_type=MESH,
        )

    body_rows = comps // ROWS * ROWS
    main = pl.ds(0, body_rows)

    def inward(j, delta):
        return copy(
            blocks.at[peer(delta), j, main], got.at[j, me, main],
            send_in.at[j, delta], recv_in.at[j, delta], {"spec": peer(delta)},
        )

    def homeward(j, delta):
        return copy(
            made.at[j, peer(delta), main], returned.at[j, me, main],
            send_back.at[j, delta], recv_back.at[j, delta], {"spec": peer(delta)},
        )

    def inward_rest(j, delta):
        return copy(
            rest_out.at[peer(delta), j], rest_in.at[j, me],
            send_in.at[j, slots + delta], recv_in.at[j, slots + delta], {"spec": peer(delta)},
        )

    def homeward_rest(j, delta):
        return copy(
            rest_made.at[j, peer(delta)], rest_back.at[j, me],
            send_back.at[j, slots + delta], recv_back.at[j, slots + delta], {"spec": peer(delta)},
        )

    rest = comps - body_rows
    tile_row = lax.broadcasted_iota(jnp.int32, (ROWS, 128), 0)

    def fold(value):
        value = jnp.where(jnp.concatenate([tile_row] * tiles, 1) < rest, value.astype(F32), 0.0)
        folded = value[:, :128]
        for v in range(1, tiles):
            folded = folded + pltpu.roll(value[:, v * 128 : (v + 1) * 128], v * rest, 0)
        return folded.astype(BF16)

    def unfold(value):
        value = value.astype(F32)
        parts = []
        for v in range(tiles):
            moved = pltpu.roll(value, ROWS - v * rest, 0) if v else value
            parts.append(jnp.where(tile_row < rest, moved, 0.0))
        return jnp.concatenate(parts, 1).astype(BF16)

    def upward(delta):
        return copy(
            surface, surfaces.at[me], send_top.at[delta], recv_top.at[delta], {"spec": peer(delta)}
        )

    def downward(delta):
        return copy(
            deeper, deepers.at[me], send_deep.at[delta], recv_deep.at[delta], {"spec": peer(delta)}
        )

    def pay_over(step, delta):
        return copy(
            pay_out.at[step, peer(delta)], pay_in.at[step, me],
            send_pay.at[step, delta], recv_pay.at[step, delta], {"spec": peer(delta)},
        )

    def to_before(source, target, i):
        return copy(source, target, send_edge.at[i], recv_edge.at[i], {"space": strip - 1})

    def to_after(source, target, i):
        return copy(source, target, send_edge.at[i], recv_edge.at[i], {"space": strip + 1})

    def row_up():
        return copy(row_out.at[0], row_in.at[1], send_row.at[0], recv_row.at[0], {"space": strip - 1})

    def row_down():
        return copy(row_out.at[1], row_in.at[0], send_row.at[1], recv_row.at[1], {"space": strip + 1})

    def col_left(j):
        return copy(col_out.at[j, 0], col_in.at[j, 1], send_col.at[j, 0], recv_col.at[j, 0], {"spec": me - 1})

    def col_right(j):
        return copy(col_out.at[j, 1], col_in.at[j, 0], send_col.at[j, 1], recv_col.at[j, 1], {"spec": me + 1})

    barrier = pltpu.get_barrier_semaphore()
    for delta in range(1, slots):
        pl.semaphore_signal(barrier, inc=1, device_id={"spec": peer(delta)}, device_id_type=MESH)

    @pl.when(has_before)
    def _():
        pl.semaphore_signal(barrier, inc=1, device_id={"space": strip - 1}, device_id_type=MESH)

    @pl.when(has_after)
    def _():
        pl.semaphore_signal(barrier, inc=1, device_id={"space": strip + 1}, device_id_type=MESH)

    held = [
        pltpu.make_async_copy(source, target, held_sem.at[i])
        for i, (source, target) in enumerate((
            (spectrum_raw, spectrum), (turn_raw, turn), (taps_raw, taps), (across_raw, across),
            (proj_raw, proj_held), (back_raw, back_held), (outer_raw, outer), (through_raw, through),
            (inside_raw, inside), (spread_raw, spread), (pick_raw, pick), (pay_turn_raw, pay_turn),
            (unturn_raw, unturn),
        ))
    ]
    for each in held:
        each.start()
    for i in range(2):
        surface[i] = velocity[i, 0]
        deeper[i] = velocity[i, 1]
    deeper[2] = mixing[0]
    deeper[3] = active[...].astype(F32)
    expected = slots - 1 + has_before.astype(jnp.int32) + has_after.astype(jnp.int32)
    pl.semaphore_wait(barrier, expected)
    for delta in range(1, slots):
        upward(delta).start()
    for delta in range(1, slots):
        downward(delta).start()
    surfaces[me] = surface[...]
    deepers[me] = deeper[...]

    land = land_sea[...].astype(F32)
    for r in range(rows):
        land_row[:, r * width : (r + 1) * width] = land[r : r + 1, :]

    def turned(value, count):
        wet = (value.astype(F32) * land[None]).astype(BF16).reshape(count * rows, width)
        return jnp.dot(turn[:, : count * rows], wet, preferred_element_type=F32).astype(BF16)

    def place_turned(value, at):
        for r in range(rows):
            field[at, (r + 2) * width : (r + 3) * width] = value[r * ROWS : (r + 1) * ROWS]

    def by_groups(count, body):
        many = next(n for n in (4, 5, 3, 2, 1) if count % n == 0)

        def some(q, carry):
            for i in range(many):
                body(pl.ds(pl.multiple_of((q * many + i) * ROWS, ROWS), ROWS))
            return carry

        lax.fori_loop(0, count // many, some, 0)

    def turn_group(at):
        place_turned(turned(spectrum[at], ROWS), at)

    whole_groups = comps // ROWS
    for each in held[:4]:
        each.wait()
    by_groups(whole_groups, turn_group)
    if rest:
        place_turned(turned(spectrum[whole_groups * ROWS :], rest), slice(whole_groups * ROWS, padded))
    head[...] = field[:, edge : 2 * edge]
    tail[...] = field[:, points : points + edge]

    @pl.when(has_before)
    def _():
        to_before(head, after, 0).start()

    @pl.when(has_after)
    def _():
        to_after(tail, before, 1).start()

    for delta in range(1, slots):
        upward(delta).wait()
    for b in range(slots):
        here = jnp.zeros((2, high, 128), F32)
        for s in range(slots):
            here = here + (owners[s] == b).astype(F32) * surfaces[s]
        for i in range(high):
            at = b * block + i * 128
            strip_rows[0:1, at : at + 128] = here[0, i : i + 1]
            strip_rows[1:2, at : at + 128] = here[1, i : i + 1]
    east[:, edge : edge + points] = current_scale * strip_rows[0:1, :]
    north[...] = current_scale * strip_rows[1:2, :]
    east_head[...] = east[:, edge : 2 * edge]
    east_tail[...] = east[:, points : points + edge]

    @pl.when(has_before)
    def _():
        to_before(east_head, east_after, 2).start()

    @pl.when(has_after)
    def _():
        to_after(east_tail, east_before, 3).start()

    def take_halos():
        @pl.when(has_after)
        def _():
            to_after(head, after, 0).wait_recv()
            to_after(east_head, east_after, 2).wait_recv()
            field[:, edge + points :] = after[...]
            east[:, edge + points :] = east_after[...]

        @pl.when(jnp.logical_not(has_after))
        def _():
            field[:, edge + points :] = jnp.zeros((padded, edge), BF16)
            east[:, edge + points :] = jnp.zeros((1, edge), F32)

        @pl.when(has_before)
        def _():
            to_before(tail, before, 1).wait_recv()
            to_before(east_tail, east_before, 3).wait_recv()
            field[:, :edge] = before[...]
            east[:, :edge] = east_before[...]

        @pl.when(jnp.logical_not(has_before))
        def _():
            field[:, :edge] = jnp.zeros((padded, edge), BF16)
            east[:, :edge] = jnp.zeros((1, edge), F32)

    def grouped(body):
        many = 3 if groups % 3 == 0 else 1

        def some(q, carry):
            for i in range(many):
                body(pl.ds(pl.multiple_of((q * many + i) * ROWS, ROWS), ROWS))
            return carry

        lax.fori_loop(0, groups // many, some, 0)

    halves = width // 128

    def wide(tap, i):
        return jnp.broadcast_to(tap[:, i : i + 1], (ROWS, 128))

    def advect_first(t, carry):
        @pl.when(t == min(1, chunks - 1))
        def _():
            take_halos()

        j = first_order(t)
        base = j * lanes * slots

        def lane(row, half):
            return pl.ds(pl.multiple_of(base + row * width + half * 128, 128), 128)

        def along_columns(here):
            tap = taps[me, here, :]
            speed = wide(tap, 1)
            northward = wide(tap, 7) != 0.0
            for c in range(chunk_rows):
                for half in range(halves):
                    along = (speed + north[:, lane(c, half)]) * field[here, lane(c + 2, half)].astype(F32)
                    at = half * 128
                    flow_cols[c, here, at : at + 128] = jnp.where(northward, along, 0.0).astype(BF16)
                    at = width + half * 128
                    flow_cols[c, here, at : at + 128] = jnp.where(northward, 0.0, along).astype(BF16)

        grouped(along_columns)

        def one_row(c, carry):
            flow_rows[c] = jnp.dot(flow_cols[c], across[...], preferred_element_type=F32)
            return carry

        lax.fori_loop(0, chunk_rows, one_row, 0)

        def along_rows(here):
            tap = taps[me, here, :]
            speed = wide(tap, 0)
            row_tap = [wide(tap, 2 + i) for i in range(5)]
            done = {}
            for half in range(halves):
                masked = {}
                flow = {}
                for r in range(-2, chunk_rows + 2):
                    masked[r] = field[here, lane(r + 2, half)].astype(F32)
                    flow[r] = (speed + east[:, lane(r + 2, half)]) * masked[r]
                    c = r - 2
                    if c < 0:
                        continue
                    total = masked.pop(c) - flow_rows[c, here, half * 128 : (half + 1) * 128] * (1.0 / 6.0)
                    for i in range(5):
                        total = total - row_tap[i] * flow[c - 2 + i]
                    flow.pop(c - 2)
                    done[c, half] = total * land_row[:, lane(c, half)]
            for d in range(slots):
                half, at = d * seg // 128, d * seg % 128
                for v in range(tiles):
                    blocks[d, j, here, v * 128 : (v + 1) * 128] = jnp.concatenate(
                        [done[v * per_tile + h, half][:, at : at + seg] for h in range(per_tile)], 1
                    ).astype(BF16)

        grouped(along_rows)
        if rest:
            for delta in range(1, slots):
                rest_out[peer(delta), j] = fold(blocks[peer(delta), j, body_rows:])
        for delta in range(1, slots):
            inward(j, delta).start()
            if rest:
                inward_rest(j, delta).start()
        return carry

    lax.fori_loop(0, chunks, advect_first, 0)

    @pl.when(jnp.logical_not(has_left))
    def _():
        col_in[:, 0] = jnp.zeros_like(col_in[:, 0])

    @pl.when(jnp.logical_not(has_right))
    def _():
        col_in[:, 1] = jnp.zeros_like(col_in[:, 1])

    zeros = jnp.zeros((padded, 128), BF16)

    def clear(g, carry):
        for flux in (flux_e, flux_w):

            @pl.when(jnp.logical_not(has_before))
            def _():
                flux[g, :, :128] = zeros

            @pl.when(jnp.logical_not(has_after))
            def _():
                flux[g, :, 128 + tile_points :] = zeros

        return carry

    lax.fori_loop(0, slots, clear, 0)
    for j in range(chunks):
        got[j, me] = blocks[me, j]

    for delta in range(1, slots):
        downward(delta).wait()
    for b in range(slots):
        here = jnp.zeros((4, high, 128), F32)
        for s in range(slots):
            here = here + (owners[s] == b).astype(F32) * deepers[s]
        for f in range(4):
            for i in range(high):
                at = b * block + i * 128
                strip_rows[2 + f : 3 + f, at : at + 128] = here[f, i : i + 1]
    strip_rows[6:7, :] = land_row[...]
    strip_rows[7:8, :] = land_row[...]
    pieces_of = [[] for _ in range(slots)]
    for r in range(rows):
        line = strip_rows[:, r * width : (r + 1) * width]
        for d in range(slots):
            pieces_of[d].append(line[:, d * seg : (d + 1) * seg])
    mine = jnp.zeros((8, tile_points), F32)
    for d in range(slots):
        mine = mine + (me == d).astype(F32) * jnp.concatenate(pieces_of[d], 1)
    tile[...] = mine
    for each in held[4:]:
        each.wait()
    eye = lax.broadcasted_iota(jnp.int32, (proj.shape[1], proj.shape[1]), 0)
    eye = (eye == lax.broadcasted_iota(jnp.int32, eye.shape, 1)).astype(F32).astype(BF16)
    mixed_rows = jnp.zeros((through.shape[1], proj.shape[1]), F32)
    for g in range(slots):
        low = g * comps // ROWS * ROWS
        window = min(padded + ROWS, slots * comps - low)
        row = lax.broadcasted_iota(jnp.int32, (padded, window), 0)
        shift = lax.broadcasted_iota(jnp.int32, (padded, window), 1) - row
        shift = ((shift == g * comps - low) & (row < comps)).astype(F32).astype(BF16)
        back[g] = jnp.dot(shift, back_held[low : low + window], preferred_element_type=F32).astype(BF16)
        aligned = jnp.dot(shift, proj_held[low : low + window], preferred_element_type=F32).astype(BF16)
        proj[g] = lax.dot_general(
            eye, aligned, (((1,), (1,)), ((), ())), preferred_element_type=F32
        ).astype(BF16)
        mixed_rows = mixed_rows + jnp.dot(through[g], back[g], preferred_element_type=F32)
    half = mixed_rows.shape[0] // 2
    mixed_rows = mixed_rows[:half] + mixed_rows[half:]
    first = mixed_rows.astype(BF16)
    inner[:half] = first
    inner[half:] = (mixed_rows - first.astype(F32)).astype(BF16)

    def project(values, step, j):
        projected = jnp.dot(proj[0], values[0], preferred_element_type=F32)
        more = jnp.dot(outer[0], values[0], preferred_element_type=F32)
        for g in range(1, slots):
            projected = projected + jnp.dot(proj[g], values[g], preferred_element_type=F32)
            more = more + jnp.dot(outer[g], values[g], preferred_element_type=F32)
        cubed = (projected * projected * projected).astype(BF16)
        more = more + jnp.dot(inner[...], cubed, preferred_element_type=F32)
        half = more.shape[0] // 2
        payload = more[:half] + more[half:]
        pay[step, j] = payload
        return cubed, payload

    def send_payload(step):
        whole_pay = jnp.concatenate([pay[step, j] for j in range(chunks)], 1)
        for s in range(slots):
            value = jnp.zeros((whole_pay.shape[0], part), F32)
            for b in range(slots):
                value = value + (owners[s] == b).astype(F32) * whole_pay[:, b * part : (b + 1) * part]
            pay_out[step, s] = value.astype(BF16)
        pay_in[step, me] = pay_out[step, me]
        for delta in range(1, slots):
            pay_over(step, delta).start()

    def source_first(t):
        j = first_order(t)
        for delta in range(1, slots):
            inward(j, delta).wait_recv()
            if rest:
                inward_rest(j, delta).wait_recv()
                sender = lax.rem(me + slots - delta, slots)
                got[j, sender, body_rows:] = unfold(rest_in[j, sender])
        cubed, payload = project(got.at[j], 0, j)
        own = tile[:, pl.ds(pl.multiple_of(j * lanes, 128), lanes)]
        u0, v0, u1, v1 = own[0:1], own[1:2], own[2:3], own[3:4]
        mix, depth = own[4:5], own[5:6]
        live = (depth > 0.5).astype(F32)
        below = mix * (depth > 1.5).astype(F32)
        floor = mix * ((depth > 0.5) & (depth < 1.5)).astype(F32)
        push_u, push_v = payload[0:1], payload[layers : layers + 1]
        new_u = live * (u0 + coriolis * v0 - below * (u0 - u1) - floor * u0 + push_u)
        new_v = live * (v0 - coriolis * u0 - below * (v0 - v1) - floor * v0 + push_v)
        east_here = current_scale * new_u
        north_here = current_scale * new_v

        def one_group(g):
            transfer = jnp.dot(back[g], cubed, preferred_element_type=F32)
            updated = (got[j, g].astype(F32) + source_step * transfer).astype(BF16)
            state[j, g] = updated
            updated = updated.astype(F32)
            along_x = (taps[g, :, 0:1] + east_here) * updated
            eastward = taps[g, :, 2:3] != 0.0
            at = pl.ds(pl.multiple_of(128 + j * lanes, 128), lanes)
            flux_e[g, :, at] = jnp.where(eastward, along_x, 0.0).astype(BF16)
            flux_w[g, :, at] = jnp.where(eastward, 0.0, along_x).astype(BF16)
            along_y = (taps[g, :, 1:2] + north_here) * updated
            northward = taps[g, :, 7:8] != 0.0
            flux_n[j, g] = jnp.where(northward, along_y, 0.0).astype(BF16)
            flux_s[j, g] = jnp.where(northward, 0.0, along_y).astype(BF16)
            along_y = along_y.astype(BF16)
            ends = lax.dot_general(
                pick[...], along_y, (((1,), (1,)), ((), ())), preferred_element_type=F32
            )

            @pl.when(j == 0)
            def _():
                row_out[0, g] = along_x[:, :128].astype(BF16)

            @pl.when(j == chunks - 1)
            def _():
                row_out[1, g] = along_x[:, lanes - 128 :].astype(BF16)

            half = ends.shape[0] // 2
            return ends[:half], ends[half:]

        def one_source(p, carry):
            ends = [one_group(p * pack + i) for i in range(pack)]
            for side in range(2):
                col_out[j, side, p] = jnp.concatenate([both[side] for both in ends], 0).astype(BF16)
            return carry

        lax.fori_loop(0, slots // pack, one_source, 0)

        @pl.when(has_left)
        def _():
            col_left(j).start()

        @pl.when(has_right)
        def _():
            col_right(j).start()

        @pl.when((j == 0) & has_before)
        def _():
            row_up().start()

        @pl.when((j == chunks - 1) & has_after)
        def _():
            row_down().start()

    def advect_second(j):
        def put(place, at):
            def one(g, carry):
                eastward = taps[g, :, 2:3] != 0.0
                value = row_in[place, g].astype(F32)
                flux_e[g, :, at : at + 128] = jnp.where(eastward, value, 0.0).astype(BF16)
                flux_w[g, :, at : at + 128] = jnp.where(eastward, 0.0, value).astype(BF16)
                return carry

            lax.fori_loop(0, slots, one, 0)

        @pl.when((j == 0) & has_before)
        def _():
            row_down().wait_recv()
            put(0, 0)

        @pl.when((j == chunks - 1) & has_after)
        def _():
            row_up().wait_recv()
            put(1, 128 + tile_points)

        @pl.when(has_left)
        def _():
            col_right(j).wait_recv()

        @pl.when(has_right)
        def _():
            col_left(j).wait_recv()

        start = pl.multiple_of(j * lanes, 128)
        land_here = tile[6:7, pl.ds(start, lanes)]

        def one_advect(g, carry):
            rows_at = pl.ds(start, lanes + 256)
            every = jnp.concatenate(
                [flux_e[g, :, rows_at], flux_w[g, :, rows_at], flux_n[j, g], flux_s[j, g]], 1
            )
            ends = jnp.concatenate([col_in[j, 0, g // pack], col_in[j, 1, g // pack]], 0)
            ends_north = ends * north_mask[g]
            ends = jnp.concatenate([ends_north, ends - ends_north], 0)
            change = jnp.dot(every, inside[...], preferred_element_type=F32) + lax.dot_general(
                ends, spread[lax.rem(g, pack)], (((0,), (0,)), ((), ())), preferred_element_type=F32
            )
            total = (state[j, g].astype(F32) - change * (1.0 / 6.0)) * land_here
            drift[g] = total.astype(BF16)
            return carry

        lax.fori_loop(0, slots, one_advect, 0)

    def source_second(t):
        j = flip(t)
        advect_second(j)
        cubed, _ = project(drift, 1, j)

        for delta in range(slots):
            g = peer(delta)
            transfer = jnp.dot(back[g], cubed, preferred_element_type=F32)
            updated = (drift[g].astype(F32) + source_step * transfer).astype(BF16)
            if delta:
                made[j, g] = updated
                homeward(j, delta).start()
                if rest:
                    rest_made[j, g] = fold(updated[body_rows:])
                    homeward_rest(j, delta).start()
            else:
                returned[j, g] = updated

        @pl.when(t == chunks - 1)
        def _():
            send_payload(1)

    def middle(u, carry):
        @pl.when(u < chunks)
        def _():
            source_first(u)

        @pl.when(u == chunks - 1)
        def _():
            send_payload(0)

        @pl.when(u > 0)
        def _():
            source_second(u - 1)

        return carry

    lax.fori_loop(0, chunks + 1, middle, 0)

    layer = lax.broadcasted_iota(jnp.int32, (layers, high, 128), 0)
    depth = active[...][None]
    live = (layer < depth).astype(F32)
    bottom = mixing[...] * (layer == depth - 1).astype(F32)
    upper = mixing[...] * ((layer + 1 < depth) & (layer < layers - 1)).astype(F32)
    nothing = jnp.zeros((1, high, 128), F32)

    def mixed(value):
        between = upper * (value - jnp.concatenate([value[1:], nothing], 0))
        return jnp.concatenate([nothing, between[:-1]], 0) - between - bottom * value

    def ocean_step(step, east_old, north_old):
        for delta in range(1, slots):
            pay_over(step, delta).wait_recv()
        lines = []
        for i in range(high):
            pieces = []
            for h in range(per_tile):
                r, d = divmod(i * per_tile + h, slots)
                pieces.append(pay_in[step, d].astype(F32)[:, r * seg : (r + 1) * seg])
            lines.append(jnp.concatenate(pieces, 1))
        lines = jnp.concatenate(lines, 0).astype(BF16)
        push = jnp.dot(pay_turn[...], lines, preferred_element_type=F32).reshape(2, layers, high, 128)
        new_velocity[0] = live * (east_old + coriolis * north_old + mixed(east_old) + push[0])
        new_velocity[1] = live * (north_old - coriolis * east_old + mixed(north_old) + push[1])

    ocean_step(0, velocity[0], velocity[1])

    def unpack(t, carry):
        j = flip(t)
        for delta in range(1, slots):
            homeward(j, delta).wait_recv()
            if rest:
                homeward_rest(j, delta).wait_recv()
                sender = lax.rem(me + slots - delta, slots)
                returned[j, sender, body_rows:] = unfold(rest_back[j, sender])

        def one_group(here):
            parts = [returned[j, d, here, :].astype(F32) for d in range(slots)]
            for k in range(chunk_rows):
                line = jnp.concatenate([p[:, k * seg : (k + 1) * seg] for p in parts], 1)
                at = pl.ds(pl.multiple_of((j * chunk_rows + k) * width, 128), width)
                field[here, at] = line.astype(BF16)

        grouped(one_group)
        return carry

    lax.fori_loop(0, chunks, unpack, 0)

    def unturned(at, count):
        value = jnp.concatenate([field[at, r * width : (r + 1) * width] for r in range(rows)], 0)
        back_again = jnp.dot(unturn[: count * rows], value, preferred_element_type=F32)
        return back_again.astype(BF16).reshape(count, rows, width)

    def unturn_group(at):
        out[at] = unturned(at, ROWS)

    by_groups(whole_groups, unturn_group)
    if rest:
        out[whole_groups * ROWS :] = unturned(slice(whole_groups * ROWS, padded), rest)
    for step in range(1, STEPS):
        ocean_step(step, new_velocity[0], new_velocity[1])

    @pl.when(has_before)
    def _():
        to_before(head, after, 0).wait_send()
        to_before(east_head, east_after, 2).wait_send()
        row_up().wait_send()

    @pl.when(has_after)
    def _():
        to_after(tail, before, 1).wait_send()
        to_after(east_tail, east_before, 3).wait_send()
        row_down().wait_send()

    for j in range(chunks):
        for delta in range(1, slots):
            inward(j, delta).wait_send()
            homeward(j, delta).wait_send()
            if rest:
                inward_rest(j, delta).wait_send()
                homeward_rest(j, delta).wait_send()

        @pl.when(has_left)
        def _():
            col_left(j).wait_send()

        @pl.when(has_right)
        def _():
            col_right(j).wait_send()

    for step in range(STEPS):
        for delta in range(1, slots):
            pay_over(step, delta).wait_send()


def whole(count, memory=pltpu.VMEM):
    return [pl.BlockSpec(memory_space=memory)] * count


def body(spectrum, land_sea, owners, proj_weight, back_weight, ocean_vel, mixing, active_layers):
    comps, rows, width = spectrum.shape
    slots = lax.axis_size("spec")
    points = rows * width
    block = points // slots
    seg = width // slots
    tile_points = rows * seg
    lanes = 256 if tile_points % 256 == 0 else tile_points
    chunks = tile_points // lanes
    chunk_rows = lanes // seg
    layers = mixing.shape[0]
    rank_rows = proj_weight.shape[0]
    padded = -(-comps // ROWS) * ROWS
    edge = 2 * width
    edge_rows = 2 * chunk_rows
    pack = max(1, ROWS // edge_rows)
    high = block // 128
    part = block // slots

    def by_slot(table):
        result = np.zeros((slots, table.shape[0], padded), table.dtype)
        result[:, :, :comps] = table.reshape(table.shape[0], slots, comps).transpose(1, 0, 2)
        return result

    taps = np.zeros((slots, padded, 12), np.float32)
    taps[:, :comps] = tap_table().reshape(slots, comps, 12)
    drift_rows, stress_rows = coupling_tables(layers)
    push = coriolis * np.concatenate([drift_rows[layers:], -drift_rows[:layers]], 0)
    outer = by_slot(two_pieces(push))
    push = source_step * push
    push[0] += stress_rows[0]
    push[layers] += stress_rows[1]
    through = by_slot(two_pieces(push))
    tables = stencil_tables(seg, width, chunk_rows, edge_rows, pack)
    north_mask = (taps[:, :, 7] != 0).astype(BF16).reshape(slots, 1, padded)
    turn = turn_table(ROWS, rows)
    pay_turn = np.zeros((high * 2 * layers,) * 2, np.float32)
    for l in range(2 * layers):
        for i in range(high):
            pay_turn[l * high + i, i * 2 * layers + l] = 1
    pay_turn = pay_turn.astype(BF16)
    velocity = ocean_vel.reshape(2, layers, high, 128)
    inside, across, spread, pick = tables
    raw = (spectrum, turn, taps, across, proj_weight.T, back_weight, outer, through, inside, spread, pick, pay_turn,
           np.ascontiguousarray(turn.T))
    raw = [jnp.asarray(each) for each in raw]
    exchange = pltpu.VMEM((chunks, slots, padded, lanes), BF16)
    pay_rows = 2 * layers
    state, velocity = pl.pallas_call(
        functools.partial(steps_kernel, (comps, rows, width, slots)),
        out_shape=(
            jax.ShapeDtypeStruct((comps, rows, width), BF16),
            jax.ShapeDtypeStruct((2, layers, high, 128), F32),
        ),
        in_specs=whole(1, pltpu.SMEM) + whole(5) + whole(13, pl.ANY),
        out_specs=tuple(whole(2)),
        scratch_shapes=[
            pltpu.VMEM((padded, points + 2 * edge), BF16),
            pltpu.VMEM((1, points + 2 * edge), F32),
            pltpu.VMEM((1, points), F32),
            pltpu.VMEM((1, points), F32),
            pltpu.VMEM((2, high, 128), F32),
            pltpu.VMEM((slots, 2, high, 128), F32),
            pltpu.VMEM((4, high, 128), F32),
            pltpu.VMEM((slots, 4, high, 128), F32),
            pltpu.VMEM((8, points), F32),
            pltpu.VMEM((8, tile_points), F32),
            *[pltpu.VMEM(each.shape, each.dtype) for each in raw],
            pltpu.VMEM((slots, rank_rows, padded), BF16),
            pltpu.VMEM((slots, padded, rank_rows), BF16),
            pltpu.VMEM((outer.shape[1], rank_rows), BF16),
            pltpu.VMEM((slots, chunks, ROWS, 128), BF16),
            *[pltpu.VMEM((chunks, slots, ROWS, 128), BF16)] * 3,
            pltpu.VMEM((chunk_rows, padded, width), F32),
            pltpu.VMEM((chunk_rows, padded, 2 * width), BF16),
            pltpu.VMEM((slots, chunks, padded, lanes), BF16),
            exchange,
            exchange,
            pltpu.VMEM((slots, padded, tile_points + 256), BF16),
            pltpu.VMEM((slots, padded, tile_points + 256), BF16),
            exchange,
            exchange,
            pltpu.VMEM((slots, padded, lanes), BF16),
            exchange,
            exchange,
            pltpu.VMEM((STEPS, chunks, pay_rows, lanes), F32),
            pltpu.VMEM((STEPS, slots, pay_rows, part), BF16),
            pltpu.VMEM((STEPS, slots, pay_rows, part), BF16),
            pltpu.VMEM((2, slots, padded, 128), BF16),
            pltpu.VMEM((2, slots, padded, 128), BF16),
            pltpu.VMEM((chunks, 2, slots // pack, pack * edge_rows, padded), BF16),
            pltpu.VMEM((chunks, 2, slots // pack, pack * edge_rows, padded), BF16),
        ]
        + [pltpu.VMEM((padded, edge), BF16)] * 4
        + [pltpu.VMEM((1, edge), F32)] * 4
        + [pltpu.SemaphoreType.DMA((chunks, 2 * slots))] * 4
        + [pltpu.SemaphoreType.DMA((slots,))] * 4
        + [pltpu.SemaphoreType.DMA((4,))] * 2
        + [pltpu.SemaphoreType.DMA((2,))] * 2
        + [pltpu.SemaphoreType.DMA((chunks, 2))] * 2
        + [pltpu.SemaphoreType.DMA((STEPS, slots))] * 2
        + [pltpu.SemaphoreType.DMA((len(raw),))],
        compiler_params=pltpu.CompilerParams(
            vmem_limit_bytes=VMEM_LIMIT, collective_id=0, has_side_effects=True
        ),
        name="steps",
    )(owners, land_sea, velocity, mixing.reshape(layers, high, 128), active_layers.reshape(high, 128),
      jnp.asarray(north_mask), *raw)
    return (state, velocity.reshape(ocean_vel.shape))


def solution(mesh):
    placed = (
        P("spec", "space", None),
        P("space", None),
        P(),
        P(),
        P(),
        P(None, None, "spec", "space", None),
        P(None, "spec", "space", None),
        P("spec", "space", None),
    )
    return jax.shard_map(
        body,
        mesh=mesh,
        in_specs=placed,
        out_specs=(P("spec", "space", None), P(None, None, "spec", "space", None)),
        check_vma=False,
    )
```

```python
import functools
import math

import jax
import jax.numpy as jnp
import numpy as np
from jax import lax
from jax.experimental import pallas as pl
from jax.experimental.pallas import tpu as pltpu
from jax.sharding import PartitionSpec as P

NDIR = 36
NFREQ = 36
K = NDIR * NFREQ
STEPS = 2

courant_scale = 0.5
current_scale = 0.15
source_step = 0.25
coriolis = 0.3
stress_scale = 0.5
drift_scale = 4.0

MESH = pl.DeviceIdType.MESH
F32 = jnp.float32
BF16 = jnp.bfloat16
VMEM_LIMIT = 60 * 1024 * 1024
ROWS = 16


def tap_table():
    component = np.arange(K)
    frequency = component // NDIR
    direction = component % NDIR
    angle = (direction + 0.5) * (2.0 * math.pi / NDIR)
    speed = courant_scale * np.exp(-2.0 * frequency / NFREQ)
    eastward = (4 * direction + 2 < NDIR) | (4 * direction + 2 > 3 * NDIR)
    northward = 2 * direction + 1 < NDIR
    forward = (1.0 / 6.0, -1.0, 0.5, 2.0 / 6.0, 0.0)
    backward = (0.0, -2.0 / 6.0, -0.5, 1.0, -1.0 / 6.0)
    columns = [speed * np.cos(angle), speed * np.sin(angle)]
    for mask in (eastward, northward):
        for f, b in zip(forward, backward):
            columns.append(np.where(mask, f, b))
    return np.stack(columns, 1).astype(np.float32)


def coupling_tables(layers):
    component = np.arange(K)
    frequency = component // NDIR
    angle = (component % NDIR + 0.5) * (2.0 * math.pi / NDIR)
    wavenum = 0.02 * np.exp(6.0 * frequency / NFREQ)
    depth = np.arange(layers)[:, None] + 0.5
    decay_rows = wavenum[None, :] ** 1.5 * np.exp(-2.0 * wavenum[None, :] * depth)
    decay_rows = decay_rows / np.sqrt(np.sum(decay_rows * decay_rows, axis=1, keepdims=True))
    drift_rows = drift_scale * np.concatenate(
        [decay_rows * np.cos(angle)[None, :], decay_rows * np.sin(angle)[None, :]], 0
    )
    stress = wavenum / np.sqrt(np.sum(wavenum * wavenum))
    stress_rows = -stress_scale * np.stack([stress * np.cos(angle), stress * np.sin(angle)], 0)
    return (drift_rows.astype(np.float32), stress_rows.astype(np.float32))


def two_pieces(rows):
    first = rows.astype(BF16)
    second = (rows - first.astype(np.float32)).astype(BF16)
    return np.concatenate([first, second], 0)


FORWARD = (1, -6, 3, 2, 0)
BACKWARD = (0, -2, -3, 6, -1)


def stencil_tables(seg, width, rows_in_chunk, edge_rows, pack):
    lanes = rows_in_chunk * seg
    inside = np.zeros((4, lanes + 256, lanes), np.float32)
    across = np.zeros((2, width, width), np.float32)
    spread = np.zeros((2, 2 * edge_rows, lanes), np.float32)
    pick = np.zeros((2 * edge_rows, lanes), np.float32)
    for v, taps in enumerate((FORWARD, BACKWARD)):
        for b in range(lanes):
            for k in range(-2, 3):
                inside[v, 128 + b + k * seg, b] = taps[k + 2]
                if b // seg == (b + k) // seg:
                    inside[2 + v, b + k, b] = taps[k + 2]
        for b in range(width):
            for k in range(-2, 3):
                if 0 <= b + k < width:
                    across[v, b + k, b] = taps[k + 2]
        for k in range(rows_in_chunk):
            for i in range(2):
                for c in range(seg):
                    for row, offset in ((k * 2 + i, i - 2 - c), (edge_rows + k * 2 + i, seg + i - c)):
                        if abs(offset) <= 2:
                            spread[v, row, k * seg + c] = taps[offset + 2]
    for k in range(rows_in_chunk):
        for i in range(2):
            pick[k * 2 + i, k * seg + i] = 1
            pick[edge_rows + k * 2 + i, k * seg + seg - 2 + i] = 1
    inside = np.concatenate([inside[0], inside[1], inside[2, :lanes], inside[3, :lanes]], 0)
    held = np.zeros((pack, 2, 2, pack, edge_rows, lanes), np.float32)
    for i in range(pack):
        held[i, :, :, i] = spread.reshape(2, 2, edge_rows, lanes)
    held = held.reshape(pack, 4 * pack * edge_rows, lanes)
    tables = (inside, across.reshape(2 * width, width), held, pick)
    return [table.astype(BF16) for table in tables]


def turn_table(first, second):
    table = np.zeros((first * second, first * second), np.float32)
    for c in range(first):
        for r in range(second):
            table[r * first + c, c * second + r] = 1
    return table.astype(BF16)


def steps_kernel(
    sizes, owners, land_sea, velocity, mixing, active, north_mask,
    spectrum_raw, turn_raw, taps_raw, across_raw,
    proj_raw, back_raw, outer_raw, through_raw, inside_raw, spread_raw, pick_raw, pay_turn_raw, unturn_raw,
    out, new_velocity,
    field, east, north, land_row, surface, surfaces, deeper, deepers, strip_rows, tile,
    spectrum, turn, taps, across, proj_held, back_held, outer, through, inside, spread, pick, pay_turn, unturn,
    proj, back, inner, rest_out, rest_in, rest_made, rest_back,
    flow_rows, flow_cols, blocks, got, state, flux_e, flux_w, flux_n, flux_s, drift, made, returned,
    pay, pay_out, pay_in, row_out, row_in, col_out, col_in,
    head, tail, before, after, east_head, east_tail, east_before, east_after,
    send_in, recv_in, send_back, recv_back, send_top, recv_top, send_deep, recv_deep, send_edge, recv_edge,
    send_row, recv_row, send_col, recv_col, send_pay, recv_pay, held_sem,
):
    comps, rows, width, slots = sizes
    padded = field.shape[0]
    chunks, lanes = got.shape[0], got.shape[3]
    seg = width // slots
    per_tile = 128 // seg
    tiles = lanes // 128
    chunk_rows = lanes // seg
    high = velocity.shape[2]
    block = high * 128
    block_rows = block // width
    part = block_rows * seg
    points = rows * width
    tile_points = rows * seg
    layers = mixing.shape[0]
    groups = padded // ROWS
    pack = slots // col_out.shape[2]
    me = lax.axis_index("spec")
    strip = lax.axis_index("space")
    strips = lax.axis_size("space")
    edge = 2 * width
    has_before = strip > 0
    has_after = strip < strips - 1
    has_left = me > 0
    has_right = me < slots - 1
    odd = lax.rem(strip, 2) == 1

    def peer(delta):
        return lax.rem(me + delta, slots)

    def flip(base):
        return jnp.where(odd, chunks - 1 - base, base)

    def first_order(t):
        return flip(jnp.where(t < 2, 1 - t, t) if chunks > 1 else t)

    def copy(source, target, send, receive, device):
        return pltpu.make_async_remote_copy(
            src_ref=source, dst_ref=target, send_sem=send, recv_sem=receive,
            device_id=device, device_id_type=MESH,
        )

    body_rows = comps // ROWS * ROWS
    main = pl.ds(0, body_rows)

    parts = 3 if groups % 3 == 0 else 1
    part_rows = padded // parts
    last_part = pl.ds((parts - 1) * part_rows, body_rows - (parts - 1) * part_rows)
    many = next(n for n in (4, 7, 3, 2, 1) if part_rows // ROWS % n == 0)

    def inward(j, delta, at, p):
        return copy(
            blocks.at[peer(delta), j, at], got.at[j, me, at],
            send_in.at[j, p * slots + delta], recv_in.at[j, p * slots + delta], {"spec": peer(delta)},
        )

    def inward_parts(j, delta):
        early = [inward(j, delta, pl.ds(p * part_rows, part_rows), p) for p in range(parts - 1)]
        return early + [inward(j, delta, last_part, parts - 1)]

    def homeward(j, delta):
        return copy(
            made.at[j, peer(delta), main], returned.at[j, me, main],
            send_back.at[j, delta], recv_back.at[j, delta], {"spec": peer(delta)},
        )

    def inward_rest(j, delta):
        return copy(
            rest_out.at[peer(delta), j], rest_in.at[j, me],
            send_in.at[j, parts * slots + delta], recv_in.at[j, parts * slots + delta], {"spec": peer(delta)},
        )

    def homeward_rest(j, delta):
        return copy(
            rest_made.at[j, peer(delta)], rest_back.at[j, me],
            send_back.at[j, slots + delta], recv_back.at[j, slots + delta], {"spec": peer(delta)},
        )

    rest = comps - body_rows
    tile_row = lax.broadcasted_iota(jnp.int32, (ROWS, 128), 0)

    def fold(value):
        value = jnp.where(jnp.concatenate([tile_row] * tiles, 1) < rest, value.astype(F32), 0.0)
        folded = value[:, :128]
        for v in range(1, tiles):
            folded = folded + pltpu.roll(value[:, v * 128 : (v + 1) * 128], v * rest, 0)
        return folded.astype(BF16)

    def unfold(value):
        value = value.astype(F32)
        parts = []
        for v in range(tiles):
            moved = pltpu.roll(value, ROWS - v * rest, 0) if v else value
            parts.append(jnp.where(tile_row < rest, moved, 0.0))
        return jnp.concatenate(parts, 1).astype(BF16)

    def upward(delta):
        return copy(
            surface, surfaces.at[me], send_top.at[delta], recv_top.at[delta], {"spec": peer(delta)}
        )

    def downward(delta):
        return copy(
            deeper, deepers.at[me], send_deep.at[delta], recv_deep.at[delta], {"spec": peer(delta)}
        )

    def pay_over(step, delta):
        return copy(
            pay_out.at[step, peer(delta)], pay_in.at[step, me],
            send_pay.at[step, delta], recv_pay.at[step, delta], {"spec": peer(delta)},
        )

    def to_before(source, target, i):
        return copy(source, target, send_edge.at[i], recv_edge.at[i], {"space": strip - 1})

    def to_after(source, target, i):
        return copy(source, target, send_edge.at[i], recv_edge.at[i], {"space": strip + 1})

    def row_up():
        return copy(row_out.at[0], row_in.at[1], send_row.at[0], recv_row.at[0], {"space": strip - 1})

    def row_down():
        return copy(row_out.at[1], row_in.at[0], send_row.at[1], recv_row.at[1], {"space": strip + 1})

    def col_left(j):
        return copy(col_out.at[j, 0], col_in.at[j, 1], send_col.at[j, 0], recv_col.at[j, 0], {"spec": me - 1})

    def col_right(j):
        return copy(col_out.at[j, 1], col_in.at[j, 0], send_col.at[j, 1], recv_col.at[j, 1], {"spec": me + 1})

    barrier = pltpu.get_barrier_semaphore()
    for delta in range(1, slots):
        pl.semaphore_signal(barrier, inc=1, device_id={"spec": peer(delta)}, device_id_type=MESH)

    @pl.when(has_before)
    def _():
        pl.semaphore_signal(barrier, inc=1, device_id={"space": strip - 1}, device_id_type=MESH)

    @pl.when(has_after)
    def _():
        pl.semaphore_signal(barrier, inc=1, device_id={"space": strip + 1}, device_id_type=MESH)

    held = [
        pltpu.make_async_copy(source, target, held_sem.at[i])
        for i, (source, target) in enumerate((
            (spectrum_raw, spectrum), (turn_raw, turn), (taps_raw, taps), (across_raw, across),
            (proj_raw, proj_held), (back_raw, back_held), (outer_raw, outer), (through_raw, through),
            (inside_raw, inside), (spread_raw, spread), (pick_raw, pick), (pay_turn_raw, pay_turn),
            (unturn_raw, unturn),
        ))
    ]
    for each in held:
        each.start()
    for i in range(2):
        surface[i] = velocity[i, 0]
        deeper[i] = velocity[i, 1]
    deeper[2] = mixing[0]
    deeper[3] = active[...].astype(F32)
    expected = slots - 1 + has_before.astype(jnp.int32) + has_after.astype(jnp.int32)
    pl.semaphore_wait(barrier, expected)
    for delta in range(1, slots):
        upward(delta).start()
    for delta in range(1, slots):
        downward(delta).start()
    surfaces[me] = surface[...]
    deepers[me] = deeper[...]

    land = land_sea[...].astype(F32)
    for r in range(rows):
        land_row[:, r * width : (r + 1) * width] = land[r : r + 1, :]

    def turned(value, count):
        wet = (value.astype(F32) * land[None]).astype(BF16).reshape(count * rows, width)
        return jnp.dot(turn[:, : count * rows], wet, preferred_element_type=F32).astype(BF16)

    def place_turned(value, at):
        for r in range(rows):
            field[at, (r + 2) * width : (r + 3) * width] = value[r * ROWS : (r + 1) * ROWS]

    def by_groups(count, body):
        many = next(n for n in (4, 5, 3, 2, 1) if count % n == 0)

        def some(q, carry):
            for i in range(many):
                body(pl.ds(pl.multiple_of((q * many + i) * ROWS, ROWS), ROWS))
            return carry

        lax.fori_loop(0, count // many, some, 0)

    def turn_group(at):
        place_turned(turned(spectrum[at], ROWS), at)

    whole_groups = comps // ROWS
    for each in held[:4]:
        each.wait()
    by_groups(whole_groups, turn_group)
    if rest:
        place_turned(turned(spectrum[whole_groups * ROWS :], rest), slice(whole_groups * ROWS, padded))
    head[...] = field[:, edge : 2 * edge]
    tail[...] = field[:, points : points + edge]

    @pl.when(has_before)
    def _():
        to_before(head, after, 0).start()

    @pl.when(has_after)
    def _():
        to_after(tail, before, 1).start()

    for delta in range(1, slots):
        upward(delta).wait()
    for b in range(slots):
        here = jnp.zeros((2, high, 128), F32)
        for s in range(slots):
            here = here + (owners[s] == b).astype(F32) * surfaces[s]
        for i in range(high):
            at = b * block + i * 128
            strip_rows[0:1, at : at + 128] = here[0, i : i + 1]
            strip_rows[1:2, at : at + 128] = here[1, i : i + 1]
    east[:, edge : edge + points] = current_scale * strip_rows[0:1, :]
    north[...] = current_scale * strip_rows[1:2, :]
    east_head[...] = east[:, edge : 2 * edge]
    east_tail[...] = east[:, points : points + edge]

    @pl.when(has_before)
    def _():
        to_before(east_head, east_after, 2).start()

    @pl.when(has_after)
    def _():
        to_after(east_tail, east_before, 3).start()

    def take_halos():
        @pl.when(has_after)
        def _():
            to_after(head, after, 0).wait_recv()
            to_after(east_head, east_after, 2).wait_recv()
            field[:, edge + points :] = after[...]
            east[:, edge + points :] = east_after[...]

        @pl.when(jnp.logical_not(has_after))
        def _():
            field[:, edge + points :] = jnp.zeros((padded, edge), BF16)
            east[:, edge + points :] = jnp.zeros((1, edge), F32)

        @pl.when(has_before)
        def _():
            to_before(tail, before, 1).wait_recv()
            to_before(east_tail, east_before, 3).wait_recv()
            field[:, :edge] = before[...]
            east[:, :edge] = east_before[...]

        @pl.when(jnp.logical_not(has_before))
        def _():
            field[:, :edge] = jnp.zeros((padded, edge), BF16)
            east[:, :edge] = jnp.zeros((1, edge), F32)

    def grouped(body):
        many = 3 if groups % 3 == 0 else 1

        def some(q, carry):
            for i in range(many):
                body(pl.ds(pl.multiple_of((q * many + i) * ROWS, ROWS), ROWS))
            return carry

        lax.fori_loop(0, groups // many, some, 0)

    halves = width // 128

    def wide(tap, i):
        return jnp.broadcast_to(tap[:, i : i + 1], (ROWS, 128))

    def advect_first(t, carry):
        @pl.when(t == min(1, chunks - 1))
        def _():
            take_halos()

        j = first_order(t)
        base = j * lanes * slots

        def lane(row, half):
            return pl.ds(pl.multiple_of(base + row * width + half * 128, 128), 128)

        def along_columns(here):
            tap = taps[me, here, :]
            speed = wide(tap, 1)
            northward = wide(tap, 7) != 0.0
            for c in range(chunk_rows):
                for half in range(halves):
                    along = (speed + north[:, lane(c, half)]) * field[here, lane(c + 2, half)].astype(F32)
                    at = half * 128
                    flow_cols[c, here, at : at + 128] = jnp.where(northward, along, 0.0).astype(BF16)
                    at = width + half * 128
                    flow_cols[c, here, at : at + 128] = jnp.where(northward, 0.0, along).astype(BF16)


        def along_rows(here):
            tap = taps[me, here, :]
            speed = wide(tap, 0)
            row_tap = [wide(tap, 2 + i) for i in range(5)]
            done = {}
            for half in range(halves):
                masked = {}
                flow = {}
                for r in range(-2, chunk_rows + 2):
                    masked[r] = field[here, lane(r + 2, half)].astype(F32)
                    flow[r] = (speed + east[:, lane(r + 2, half)]) * masked[r]
                    c = r - 2
                    if c < 0:
                        continue
                    total = masked.pop(c) - flow_rows[c, here, half * 128 : (half + 1) * 128] * (1.0 / 6.0)
                    for i in range(5):
                        total = total - row_tap[i] * flow[c - 2 + i]
                    flow.pop(c - 2)
                    done[c, half] = total * land_row[:, lane(c, half)]
            for d in range(slots):
                half, at = d * seg // 128, d * seg % 128
                for v in range(tiles):
                    blocks[d, j, here, v * 128 : (v + 1) * 128] = jnp.concatenate(
                        [done[v * per_tile + h, half][:, at : at + seg] for h in range(per_tile)], 1
                    ).astype(BF16)

        def one_part(p, carry):
            low = p * part_rows
            here = pl.ds(pl.multiple_of(low, ROWS), part_rows)

            def over(body):
                def some(q, carry):
                    for i in range(many):
                        body(pl.ds(pl.multiple_of(low + (q * many + i) * ROWS, ROWS), ROWS))
                    return carry

                lax.fori_loop(0, part_rows // ROWS // many, some, 0)

            over(along_columns)

            def one_row(c, carry):
                flow_rows[c, here] = jnp.dot(flow_cols[c, here], across[...], preferred_element_type=F32)
                return carry

            lax.fori_loop(0, chunk_rows, one_row, 0)
            over(along_rows)
            if parts > 1:

                @pl.when(p < parts - 1)
                def _():
                    for delta in range(1, slots):
                        inward(j, delta, here, p).start()

            return carry

        lax.fori_loop(0, parts, one_part, 0)
        if rest:
            for delta in range(1, slots):
                rest_out[peer(delta), j] = fold(blocks[peer(delta), j, body_rows:])
        for delta in range(1, slots):
            inward(j, delta, last_part, parts - 1).start()
            if rest:
                inward_rest(j, delta).start()
        return carry

    lax.fori_loop(0, chunks, advect_first, 0)

    @pl.when(jnp.logical_not(has_left))
    def _():
        col_in[:, 0] = jnp.zeros_like(col_in[:, 0])

    @pl.when(jnp.logical_not(has_right))
    def _():
        col_in[:, 1] = jnp.zeros_like(col_in[:, 1])

    zeros = jnp.zeros((padded, 128), BF16)

    def clear(g, carry):
        for flux in (flux_e, flux_w):

            @pl.when(jnp.logical_not(has_before))
            def _():
                flux[g, :, :128] = zeros

            @pl.when(jnp.logical_not(has_after))
            def _():
                flux[g, :, 128 + tile_points :] = zeros

        return carry

    lax.fori_loop(0, slots, clear, 0)
    for j in range(chunks):
        got[j, me] = blocks[me, j]

    for delta in range(1, slots):
        downward(delta).wait()
    for b in range(slots):
        here = jnp.zeros((4, high, 128), F32)
        for s in range(slots):
            here = here + (owners[s] == b).astype(F32) * deepers[s]
        for f in range(4):
            for i in range(high):
                at = b * block + i * 128
                strip_rows[2 + f : 3 + f, at : at + 128] = here[f, i : i + 1]
    strip_rows[6:7, :] = land_row[...]
    strip_rows[7:8, :] = land_row[...]
    pieces_of = [[] for _ in range(slots)]
    for r in range(rows):
        line = strip_rows[:, r * width : (r + 1) * width]
        for d in range(slots):
            pieces_of[d].append(line[:, d * seg : (d + 1) * seg])
    mine = jnp.zeros((8, tile_points), F32)
    for d in range(slots):
        mine = mine + (me == d).astype(F32) * jnp.concatenate(pieces_of[d], 1)
    tile[...] = mine
    for each in held[4:]:
        each.wait()
    eye = lax.broadcasted_iota(jnp.int32, (proj.shape[1], proj.shape[1]), 0)
    eye = (eye == lax.broadcasted_iota(jnp.int32, eye.shape, 1)).astype(F32).astype(BF16)
    mixed_rows = jnp.zeros((through.shape[1], proj.shape[1]), F32)
    for g in range(slots):
        low = g * comps // ROWS * ROWS
        window = min(padded + ROWS, slots * comps - low)
        row = lax.broadcasted_iota(jnp.int32, (padded, window), 0)
        shift = lax.broadcasted_iota(jnp.int32, (padded, window), 1) - row
        shift = ((shift == g * comps - low) & (row < comps)).astype(F32).astype(BF16)
        back[g] = jnp.dot(shift, back_held[low : low + window], preferred_element_type=F32).astype(BF16)
        aligned = jnp.dot(shift, proj_held[low : low + window], preferred_element_type=F32).astype(BF16)
        proj[g] = lax.dot_general(
            eye, aligned, (((1,), (1,)), ((), ())), preferred_element_type=F32
        ).astype(BF16)
        mixed_rows = mixed_rows + jnp.dot(through[g], back[g], preferred_element_type=F32)
    half = mixed_rows.shape[0] // 2
    mixed_rows = mixed_rows[:half] + mixed_rows[half:]
    first = mixed_rows.astype(BF16)
    inner[:half] = first
    inner[half:] = (mixed_rows - first.astype(F32)).astype(BF16)

    def project(values, step, j):
        projected = jnp.dot(proj[0], values[0], preferred_element_type=F32)
        more = jnp.dot(outer[0], values[0], preferred_element_type=F32)
        for g in range(1, slots):
            projected = projected + jnp.dot(proj[g], values[g], preferred_element_type=F32)
            more = more + jnp.dot(outer[g], values[g], preferred_element_type=F32)
        cubed = (projected * projected * projected).astype(BF16)
        more = more + jnp.dot(inner[...], cubed, preferred_element_type=F32)
        half = more.shape[0] // 2
        payload = more[:half] + more[half:]
        pay[step, j] = payload
        return cubed, payload

    def send_payload(step):
        whole_pay = jnp.concatenate([pay[step, j] for j in range(chunks)], 1)
        for s in range(slots):
            value = jnp.zeros((whole_pay.shape[0], part), F32)
            for b in range(slots):
                value = value + (owners[s] == b).astype(F32) * whole_pay[:, b * part : (b + 1) * part]
            pay_out[step, s] = value.astype(BF16)
        pay_in[step, me] = pay_out[step, me]
        for delta in range(1, slots):
            pay_over(step, delta).start()

    def source_first(t):
        j = first_order(t)
        for delta in range(1, slots):
            for each in inward_parts(j, delta):
                each.wait_recv()
            if rest:
                inward_rest(j, delta).wait_recv()
                sender = lax.rem(me + slots - delta, slots)
                got[j, sender, body_rows:] = unfold(rest_in[j, sender])
        cubed, payload = project(got.at[j], 0, j)
        own = tile[:, pl.ds(pl.multiple_of(j * lanes, 128), lanes)]
        u0, v0, u1, v1 = own[0:1], own[1:2], own[2:3], own[3:4]
        mix, depth = own[4:5], own[5:6]
        live = (depth > 0.5).astype(F32)
        below = mix * (depth > 1.5).astype(F32)
        floor = mix * ((depth > 0.5) & (depth < 1.5)).astype(F32)
        push_u, push_v = payload[0:1], payload[layers : layers + 1]
        new_u = live * (u0 + coriolis * v0 - below * (u0 - u1) - floor * u0 + push_u)
        new_v = live * (v0 - coriolis * u0 - below * (v0 - v1) - floor * v0 + push_v)
        east_here = current_scale * new_u
        north_here = current_scale * new_v

        def one_group(g):
            transfer = jnp.dot(back[g], cubed, preferred_element_type=F32)
            updated = (got[j, g].astype(F32) + source_step * transfer).astype(BF16)
            state[j, g] = updated
            updated = updated.astype(F32)
            along_x = (taps[g, :, 0:1] + east_here) * updated
            eastward = taps[g, :, 2:3] != 0.0
            at = pl.ds(pl.multiple_of(128 + j * lanes, 128), lanes)
            flux_e[g, :, at] = jnp.where(eastward, along_x, 0.0).astype(BF16)
            flux_w[g, :, at] = jnp.where(eastward, 0.0, along_x).astype(BF16)
            along_y = (taps[g, :, 1:2] + north_here) * updated
            northward = taps[g, :, 7:8] != 0.0
            flux_n[j, g] = jnp.where(northward, along_y, 0.0).astype(BF16)
            flux_s[j, g] = jnp.where(northward, 0.0, along_y).astype(BF16)
            along_y = along_y.astype(BF16)
            ends = lax.dot_general(
                pick[...], along_y, (((1,), (1,)), ((), ())), preferred_element_type=F32
            )

            @pl.when(j == 0)
            def _():
                row_out[0, g] = along_x[:, :128].astype(BF16)

            @pl.when(j == chunks - 1)
            def _():
                row_out[1, g] = along_x[:, lanes - 128 :].astype(BF16)

            half = ends.shape[0] // 2
            return ends[:half], ends[half:]

        def one_source(p, carry):
            ends = [one_group(p * pack + i) for i in range(pack)]
            for side in range(2):
                col_out[j, side, p] = jnp.concatenate([both[side] for both in ends], 0).astype(BF16)
            return carry

        lax.fori_loop(0, slots // pack, one_source, 0)

        @pl.when(has_left)
        def _():
            col_left(j).start()

        @pl.when(has_right)
        def _():
            col_right(j).start()

        @pl.when((j == 0) & has_before)
        def _():
            row_up().start()

        @pl.when((j == chunks - 1) & has_after)
        def _():
            row_down().start()

    def advect_second(j):
        def put(place, at):
            def one(g, carry):
                eastward = taps[g, :, 2:3] != 0.0
                value = row_in[place, g].astype(F32)
                flux_e[g, :, at : at + 128] = jnp.where(eastward, value, 0.0).astype(BF16)
                flux_w[g, :, at : at + 128] = jnp.where(eastward, 0.0, value).astype(BF16)
                return carry

            lax.fori_loop(0, slots, one, 0)

        @pl.when((j == 0) & has_before)
        def _():
            row_down().wait_recv()
            put(0, 0)

        @pl.when((j == chunks - 1) & has_after)
        def _():
            row_up().wait_recv()
            put(1, 128 + tile_points)

        @pl.when(has_left)
        def _():
            col_right(j).wait_recv()

        @pl.when(has_right)
        def _():
            col_left(j).wait_recv()

        start = pl.multiple_of(j * lanes, 128)
        land_here = tile[6:7, pl.ds(start, lanes)]

        def one_advect(g, carry):
            rows_at = pl.ds(start, lanes + 256)
            every = jnp.concatenate(
                [flux_e[g, :, rows_at], flux_w[g, :, rows_at], flux_n[j, g], flux_s[j, g]], 1
            )
            ends = jnp.concatenate([col_in[j, 0, g // pack], col_in[j, 1, g // pack]], 0)
            ends_north = ends * north_mask[g]
            ends = jnp.concatenate([ends_north, ends - ends_north], 0)
            change = jnp.dot(every, inside[...], preferred_element_type=F32) + lax.dot_general(
                ends, spread[lax.rem(g, pack)], (((0,), (0,)), ((), ())), preferred_element_type=F32
            )
            total = (state[j, g].astype(F32) - change * (1.0 / 6.0)) * land_here
            drift[g] = total.astype(BF16)
            return carry

        lax.fori_loop(0, slots, one_advect, 0)

    def source_second(t):
        j = flip(t)
        advect_second(j)
        cubed, _ = project(drift, 1, j)

        for delta in range(slots):
            g = peer(delta)
            transfer = jnp.dot(back[g], cubed, preferred_element_type=F32)
            updated = (drift[g].astype(F32) + source_step * transfer).astype(BF16)
            if delta:
                made[j, g] = updated
                homeward(j, delta).start()
                if rest:
                    rest_made[j, g] = fold(updated[body_rows:])
                    homeward_rest(j, delta).start()
            else:
                returned[j, g] = updated

        @pl.when(t == chunks - 1)
        def _():
            send_payload(1)

    def middle(u, carry):
        @pl.when(u < chunks)
        def _():
            source_first(u)

        @pl.when(u == chunks - 1)
        def _():
            send_payload(0)

        @pl.when(u > 0)
        def _():
            source_second(u - 1)

        return carry

    lax.fori_loop(0, chunks + 1, middle, 0)

    layer = lax.broadcasted_iota(jnp.int32, (layers, high, 128), 0)
    depth = active[...][None]
    live = (layer < depth).astype(F32)
    bottom = mixing[...] * (layer == depth - 1).astype(F32)
    upper = mixing[...] * ((layer + 1 < depth) & (layer < layers - 1)).astype(F32)
    nothing = jnp.zeros((1, high, 128), F32)

    def mixed(value):
        between = upper * (value - jnp.concatenate([value[1:], nothing], 0))
        return jnp.concatenate([nothing, between[:-1]], 0) - between - bottom * value

    def ocean_step(step, east_old, north_old):
        for delta in range(1, slots):
            pay_over(step, delta).wait_recv()
        lines = []
        for i in range(high):
            pieces = []
            for h in range(per_tile):
                r, d = divmod(i * per_tile + h, slots)
                pieces.append(pay_in[step, d].astype(F32)[:, r * seg : (r + 1) * seg])
            lines.append(jnp.concatenate(pieces, 1))
        lines = jnp.concatenate(lines, 0).astype(BF16)
        push = jnp.dot(pay_turn[...], lines, preferred_element_type=F32).reshape(2, layers, high, 128)
        new_velocity[0] = live * (east_old + coriolis * north_old + mixed(east_old) + push[0])
        new_velocity[1] = live * (north_old - coriolis * east_old + mixed(north_old) + push[1])

    ocean_step(0, velocity[0], velocity[1])

    def unpack(t, carry):
        j = flip(t)
        for delta in range(1, slots):
            homeward(j, delta).wait_recv()
            if rest:
                homeward_rest(j, delta).wait_recv()
                sender = lax.rem(me + slots - delta, slots)
                returned[j, sender, body_rows:] = unfold(rest_back[j, sender])

        def one_group(here):
            parts = [returned[j, d, here, :].astype(F32) for d in range(slots)]
            for k in range(chunk_rows):
                line = jnp.concatenate([p[:, k * seg : (k + 1) * seg] for p in parts], 1)
                at = pl.ds(pl.multiple_of((j * chunk_rows + k) * width, 128), width)
                field[here, at] = line.astype(BF16)

        grouped(one_group)
        return carry

    lax.fori_loop(0, chunks, unpack, 0)

    def unturned(at, count):
        value = jnp.concatenate([field[at, r * width : (r + 1) * width] for r in range(rows)], 0)
        back_again = jnp.dot(unturn[: count * rows], value, preferred_element_type=F32)
        return back_again.astype(BF16).reshape(count, rows, width)

    def unturn_group(at):
        out[at] = unturned(at, ROWS)

    by_groups(whole_groups, unturn_group)
    if rest:
        out[whole_groups * ROWS :] = unturned(slice(whole_groups * ROWS, padded), rest)
    for step in range(1, STEPS):
        ocean_step(step, new_velocity[0], new_velocity[1])

    @pl.when(has_before)
    def _():
        to_before(head, after, 0).wait_send()
        to_before(east_head, east_after, 2).wait_send()
        row_up().wait_send()

    @pl.when(has_after)
    def _():
        to_after(tail, before, 1).wait_send()
        to_after(east_tail, east_before, 3).wait_send()
        row_down().wait_send()

    for j in range(chunks):
        for delta in range(1, slots):
            for each in inward_parts(j, delta):
                each.wait_send()
            homeward(j, delta).wait_send()
            if rest:
                inward_rest(j, delta).wait_send()
                homeward_rest(j, delta).wait_send()

        @pl.when(has_left)
        def _():
            col_left(j).wait_send()

        @pl.when(has_right)
        def _():
            col_right(j).wait_send()

    for step in range(STEPS):
        for delta in range(1, slots):
            pay_over(step, delta).wait_send()


def handing_kernel(spectrum, velocity, new_spectrum, new_velocity, waves, ocean, sems):
    count = spectrum.shape[0]
    parts = 6
    pieces = [(velocity, ocean, new_velocity)]
    for i in range(parts):
        low, high = i * count // parts, (i + 1) * count // parts
        at = pl.ds(low, high - low)
        pieces.append((spectrum.at[at], waves.at[at], new_spectrum.at[at]))
    loads = [pltpu.make_async_copy(a, b, sems.at[0, i]) for i, (a, b, _) in enumerate(pieces)]
    stores = [pltpu.make_async_copy(b, c, sems.at[1, i]) for i, (_, b, c) in enumerate(pieces)]
    for each in loads:
        each.start()
    for load, store in zip(loads, stores):
        load.wait()
        store.start()
    for each in stores:
        each.wait()


def whole(count, memory=pltpu.VMEM):
    return [pl.BlockSpec(memory_space=memory)] * count


def body(spectrum, land_sea, owners, proj_weight, back_weight, ocean_vel, mixing, active_layers):
    comps, rows, width = spectrum.shape
    slots = lax.axis_size("spec")
    points = rows * width
    block = points // slots
    seg = width // slots
    tile_points = rows * seg
    lanes = 256 if tile_points % 256 == 0 else tile_points
    chunks = tile_points // lanes
    chunk_rows = lanes // seg
    layers = mixing.shape[0]
    rank_rows = proj_weight.shape[0]
    padded = -(-comps // ROWS) * ROWS
    edge = 2 * width
    edge_rows = 2 * chunk_rows
    pack = max(1, ROWS // edge_rows)
    high = block // 128
    part = block // slots

    def by_slot(table):
        result = np.zeros((slots, table.shape[0], padded), table.dtype)
        result[:, :, :comps] = table.reshape(table.shape[0], slots, comps).transpose(1, 0, 2)
        return result

    taps = np.zeros((slots, padded, 12), np.float32)
    taps[:, :comps] = tap_table().reshape(slots, comps, 12)
    drift_rows, stress_rows = coupling_tables(layers)
    push = coriolis * np.concatenate([drift_rows[layers:], -drift_rows[:layers]], 0)
    outer = by_slot(two_pieces(push))
    push = source_step * push
    push[0] += stress_rows[0]
    push[layers] += stress_rows[1]
    through = by_slot(two_pieces(push))
    tables = stencil_tables(seg, width, chunk_rows, edge_rows, pack)
    north_mask = (taps[:, :, 7] != 0).astype(BF16).reshape(slots, 1, padded)
    turn = turn_table(ROWS, rows)
    pay_turn = np.zeros((high * 2 * layers,) * 2, np.float32)
    for l in range(2 * layers):
        for i in range(high):
            pay_turn[l * high + i, i * 2 * layers + l] = 1
    pay_turn = pay_turn.astype(BF16)
    velocity = ocean_vel.reshape(2, layers, high, 128)
    inside, across, spread, pick = tables
    raw = (spectrum, turn, taps, across, proj_weight.T, back_weight, outer, through, inside, spread, pick, pay_turn,
           np.ascontiguousarray(turn.T))
    raw = [jnp.asarray(each) for each in raw]
    exchange = pltpu.VMEM((chunks, slots, padded, lanes), BF16)
    pay_rows = 2 * layers
    state, velocity = pl.pallas_call(
        functools.partial(steps_kernel, (comps, rows, width, slots)),
        out_shape=(
            jax.ShapeDtypeStruct((comps, rows, width), BF16),
            jax.ShapeDtypeStruct((2, layers, high, 128), F32),
        ),
        in_specs=whole(1, pltpu.SMEM) + whole(5) + whole(13, pl.ANY),
        out_specs=tuple(whole(2)),
        scratch_shapes=[
            pltpu.VMEM((padded, points + 2 * edge), BF16),
            pltpu.VMEM((1, points + 2 * edge), F32),
            pltpu.VMEM((1, points), F32),
            pltpu.VMEM((1, points), F32),
            pltpu.VMEM((2, high, 128), F32),
            pltpu.VMEM((slots, 2, high, 128), F32),
            pltpu.VMEM((4, high, 128), F32),
            pltpu.VMEM((slots, 4, high, 128), F32),
            pltpu.VMEM((8, points), F32),
            pltpu.VMEM((8, tile_points), F32),
            *[pltpu.VMEM(each.shape, each.dtype) for each in raw],
            pltpu.VMEM((slots, rank_rows, padded), BF16),
            pltpu.VMEM((slots, padded, rank_rows), BF16),
            pltpu.VMEM((outer.shape[1], rank_rows), BF16),
            pltpu.VMEM((slots, chunks, ROWS, 128), BF16),
            *[pltpu.VMEM((chunks, slots, ROWS, 128), BF16)] * 3,
            pltpu.VMEM((chunk_rows, padded, width), F32),
            pltpu.VMEM((chunk_rows, padded, 2 * width), BF16),
            pltpu.VMEM((slots, chunks, padded, lanes), BF16),
            exchange,
            exchange,
            pltpu.VMEM((slots, padded, tile_points + 256), BF16),
            pltpu.VMEM((slots, padded, tile_points + 256), BF16),
            exchange,
            exchange,
            pltpu.VMEM((slots, padded, lanes), BF16),
            exchange,
            exchange,
            pltpu.VMEM((STEPS, chunks, pay_rows, lanes), F32),
            pltpu.VMEM((STEPS, slots, pay_rows, part), BF16),
            pltpu.VMEM((STEPS, slots, pay_rows, part), BF16),
            pltpu.VMEM((2, slots, padded, 128), BF16),
            pltpu.VMEM((2, slots, padded, 128), BF16),
            pltpu.VMEM((chunks, 2, slots // pack, pack * edge_rows, padded), BF16),
            pltpu.VMEM((chunks, 2, slots // pack, pack * edge_rows, padded), BF16),
        ]
        + [pltpu.VMEM((padded, edge), BF16)] * 4
        + [pltpu.VMEM((1, edge), F32)] * 4
        + [pltpu.SemaphoreType.DMA((chunks, 4 * slots))] * 4
        + [pltpu.SemaphoreType.DMA((slots,))] * 4
        + [pltpu.SemaphoreType.DMA((4,))] * 2
        + [pltpu.SemaphoreType.DMA((2,))] * 2
        + [pltpu.SemaphoreType.DMA((chunks, 2))] * 2
        + [pltpu.SemaphoreType.DMA((STEPS, slots))] * 2
        + [pltpu.SemaphoreType.DMA((len(raw),))],
        compiler_params=pltpu.CompilerParams(
            vmem_limit_bytes=VMEM_LIMIT, collective_id=0, has_side_effects=True
        ),
        name="steps",
    )(owners, land_sea, velocity, mixing.reshape(layers, high, 128), active_layers.reshape(high, 128),
      jnp.asarray(north_mask), *raw)
    state, velocity = pl.pallas_call(
        handing_kernel,
        out_shape=(
            jax.ShapeDtypeStruct(state.shape, BF16),
            jax.ShapeDtypeStruct(velocity.shape, F32),
        ),
        in_specs=whole(2, pl.ANY),
        out_specs=tuple(whole(2, pl.ANY)),
        scratch_shapes=[
            pltpu.VMEM(state.shape, BF16),
            pltpu.VMEM(velocity.shape, F32),
            pltpu.SemaphoreType.DMA((2, 7)),
        ],
        name="hand",
    )(state, velocity)
    return (state, velocity.reshape(ocean_vel.shape))


def solution(mesh):
    placed = (
        P("spec", "space", None),
        P("space", None),
        P(),
        P(),
        P(),
        P(None, None, "spec", "space", None),
        P(None, "spec", "space", None),
        P("spec", "space", None),
    )
    return jax.shard_map(
        body,
        mesh=mesh,
        in_specs=placed,
        out_specs=(P("spec", "space", None), P(None, None, "spec", "space", None)),
        check_vma=False,
    )
```

```python
import functools
import math

import jax
import jax.numpy as jnp
import numpy as np
from jax import lax
from jax.experimental import pallas as pl
from jax.experimental.pallas import tpu as pltpu
from jax.sharding import PartitionSpec as P

NDIR = 36
NFREQ = 36
K = NDIR * NFREQ
STEPS = 2

courant_scale = 0.5
current_scale = 0.15
source_step = 0.25
coriolis = 0.3
stress_scale = 0.5
drift_scale = 4.0

MESH = pl.DeviceIdType.MESH
F32 = jnp.float32
BF16 = jnp.bfloat16
VMEM_LIMIT = 60 * 1024 * 1024
ROWS = 16


def tap_table():
    component = np.arange(K)
    frequency = component // NDIR
    direction = component % NDIR
    angle = (direction + 0.5) * (2.0 * math.pi / NDIR)
    speed = courant_scale * np.exp(-2.0 * frequency / NFREQ)
    eastward = (4 * direction + 2 < NDIR) | (4 * direction + 2 > 3 * NDIR)
    northward = 2 * direction + 1 < NDIR
    forward = (1.0 / 6.0, -1.0, 0.5, 2.0 / 6.0, 0.0)
    backward = (0.0, -2.0 / 6.0, -0.5, 1.0, -1.0 / 6.0)
    columns = [speed * np.cos(angle), speed * np.sin(angle)]
    for mask in (eastward, northward):
        for f, b in zip(forward, backward):
            columns.append(np.where(mask, f, b))
    return np.stack(columns, 1).astype(np.float32)


def coupling_tables(layers):
    component = np.arange(K)
    frequency = component // NDIR
    angle = (component % NDIR + 0.5) * (2.0 * math.pi / NDIR)
    wavenum = 0.02 * np.exp(6.0 * frequency / NFREQ)
    depth = np.arange(layers)[:, None] + 0.5
    decay_rows = wavenum[None, :] ** 1.5 * np.exp(-2.0 * wavenum[None, :] * depth)
    decay_rows = decay_rows / np.sqrt(np.sum(decay_rows * decay_rows, axis=1, keepdims=True))
    drift_rows = drift_scale * np.concatenate(
        [decay_rows * np.cos(angle)[None, :], decay_rows * np.sin(angle)[None, :]], 0
    )
    stress = wavenum / np.sqrt(np.sum(wavenum * wavenum))
    stress_rows = -stress_scale * np.stack([stress * np.cos(angle), stress * np.sin(angle)], 0)
    return (drift_rows.astype(np.float32), stress_rows.astype(np.float32))


def two_pieces(rows):
    first = rows.astype(BF16)
    second = (rows - first.astype(np.float32)).astype(BF16)
    return np.concatenate([first, second], 0)


FORWARD = (1, -6, 3, 2, 0)
BACKWARD = (0, -2, -3, 6, -1)


def stencil_tables(seg, width, rows_in_chunk, edge_rows, pack):
    lanes = rows_in_chunk * seg
    inside = np.zeros((4, lanes + 256, lanes), np.float32)
    across = np.zeros((2, width, width), np.float32)
    spread = np.zeros((2, 2 * edge_rows, lanes), np.float32)
    pick = np.zeros((2 * edge_rows, lanes), np.float32)
    for v, taps in enumerate((FORWARD, BACKWARD)):
        for b in range(lanes):
            for k in range(-2, 3):
                inside[v, 128 + b + k * seg, b] = taps[k + 2]
                if b // seg == (b + k) // seg:
                    inside[2 + v, b + k, b] = taps[k + 2]
        for b in range(width):
            for k in range(-2, 3):
                if 0 <= b + k < width:
                    across[v, b + k, b] = taps[k + 2]
        for k in range(rows_in_chunk):
            for i in range(2):
                for c in range(seg):
                    for row, offset in ((k * 2 + i, i - 2 - c), (edge_rows + k * 2 + i, seg + i - c)):
                        if abs(offset) <= 2:
                            spread[v, row, k * seg + c] = taps[offset + 2]
    for k in range(rows_in_chunk):
        for i in range(2):
            pick[k * 2 + i, k * seg + i] = 1
            pick[edge_rows + k * 2 + i, k * seg + seg - 2 + i] = 1
    inside = np.concatenate([inside[0], inside[1], inside[2, :lanes], inside[3, :lanes]], 0)
    held = np.zeros((pack, 2, 2, pack, edge_rows, lanes), np.float32)
    for i in range(pack):
        held[i, :, :, i] = spread.reshape(2, 2, edge_rows, lanes)
    held = held.reshape(pack, 4 * pack * edge_rows, lanes)
    tables = (inside, across.reshape(2 * width, width), held, pick)
    return [table.astype(BF16) for table in tables]


def turn_table(first, second):
    table = np.zeros((first * second, first * second), np.float32)
    for c in range(first):
        for r in range(second):
            table[r * first + c, c * second + r] = 1
    return table.astype(BF16)


def steps_kernel(
    sizes, owners, land_sea, velocity, mixing, active, north_mask,
    spectrum_raw, turn_raw, taps_raw, across_raw,
    proj_raw, back_raw, outer_raw, through_raw, inside_raw, spread_raw, pick_raw, pay_turn_raw, unturn_raw,
    out, new_velocity,
    field, east, north, land_row, surface, surfaces, deeper, deepers, strip_rows, tile,
    spectrum, turn, taps, across, proj_held, back_held, outer, through, inside, spread, pick, pay_turn, unturn,
    proj, back, inner, rest_out, rest_in, rest_made, rest_back,
    flow_rows, flow_cols, blocks, got, state, flux_e, flux_w, flux_n, flux_s, drift, made, returned,
    pay, pay_out, pay_in, row_out, row_in, col_out, col_in,
    head, tail, before, after, east_head, east_tail, east_before, east_after,
    send_in, recv_in, send_back, recv_back, send_top, recv_top, send_deep, recv_deep, send_edge, recv_edge,
    send_row, recv_row, send_col, recv_col, send_pay, recv_pay, held_sem,
):
    comps, rows, width, slots = sizes
    padded = field.shape[0]
    chunks, lanes = got.shape[0], got.shape[3]
    seg = width // slots
    per_tile = 128 // seg
    tiles = lanes // 128
    chunk_rows = lanes // seg
    high = velocity.shape[2]
    block = high * 128
    block_rows = block // width
    part = block_rows * seg
    points = rows * width
    tile_points = rows * seg
    layers = mixing.shape[0]
    groups = padded // ROWS
    pack = slots // col_out.shape[2]
    me = lax.axis_index("spec")
    strip = lax.axis_index("space")
    strips = lax.axis_size("space")
    edge = 2 * width
    has_before = strip > 0
    has_after = strip < strips - 1
    has_left = me > 0
    has_right = me < slots - 1
    odd = lax.rem(strip, 2) == 1

    def peer(delta):
        return lax.rem(me + delta, slots)

    def flip(base):
        return jnp.where(odd, chunks - 1 - base, base)

    ahead = 2

    def first_order(t):
        return flip(jnp.where(t < 2, 1 - t, t) if chunks > 1 else t)

    def copy(source, target, send, receive, device):
        return pltpu.make_async_remote_copy(
            src_ref=source, dst_ref=target, send_sem=send, recv_sem=receive,
            device_id=device, device_id_type=MESH,
        )

    body_rows = comps // ROWS * ROWS
    main = pl.ds(0, body_rows)

    parts = 3 if groups % 3 == 0 else 1
    part_rows = padded // parts
    last_part = pl.ds((parts - 1) * part_rows, body_rows - (parts - 1) * part_rows)
    many = next(n for n in (4, 7, 3, 2, 1) if part_rows // ROWS % n == 0)

    def inward(j, delta, at, p):
        return copy(
            blocks.at[peer(delta), j, at], got.at[j, me, at],
            send_in.at[j, p * slots + delta], recv_in.at[j, p * slots + delta], {"spec": peer(delta)},
        )

    def inward_parts(j, delta):
        early = [inward(j, delta, pl.ds(p * part_rows, part_rows), p) for p in range(parts - 1)]
        return early + [inward(j, delta, last_part, parts - 1)]

    def homeward(j, delta):
        return copy(
            made.at[j, peer(delta), main], returned.at[j, me, main],
            send_back.at[j, delta], recv_back.at[j, delta], {"spec": peer(delta)},
        )

    def inward_rest(j, delta):
        return copy(
            rest_out.at[peer(delta), j], rest_in.at[j, me],
            send_in.at[j, parts * slots + delta], recv_in.at[j, parts * slots + delta], {"spec": peer(delta)},
        )

    def homeward_rest(j, delta):
        return copy(
            rest_made.at[j, peer(delta)], rest_back.at[j, me],
            send_back.at[j, slots + delta], recv_back.at[j, slots + delta], {"spec": peer(delta)},
        )

    rest = comps - body_rows
    tile_row = lax.broadcasted_iota(jnp.int32, (ROWS, 128), 0)

    def fold(value):
        value = jnp.where(jnp.concatenate([tile_row] * tiles, 1) < rest, value.astype(F32), 0.0)
        folded = value[:, :128]
        for v in range(1, tiles):
            folded = folded + pltpu.roll(value[:, v * 128 : (v + 1) * 128], v * rest, 0)
        return folded.astype(BF16)

    def unfold(value):
        value = value.astype(F32)
        parts = []
        for v in range(tiles):
            moved = pltpu.roll(value, ROWS - v * rest, 0) if v else value
            parts.append(jnp.where(tile_row < rest, moved, 0.0))
        return jnp.concatenate(parts, 1).astype(BF16)

    def upward(delta):
        return copy(
            surface, surfaces.at[me], send_top.at[delta], recv_top.at[delta], {"spec": peer(delta)}
        )

    def downward(delta):
        return copy(
            deeper, deepers.at[me], send_deep.at[delta], recv_deep.at[delta], {"spec": peer(delta)}
        )

    def pay_over(step, delta):
        return copy(
            pay_out.at[step, peer(delta)], pay_in.at[step, me],
            send_pay.at[step, delta], recv_pay.at[step, delta], {"spec": peer(delta)},
        )

    def to_before(source, target, i):
        return copy(source, target, send_edge.at[i], recv_edge.at[i], {"space": strip - 1})

    def to_after(source, target, i):
        return copy(source, target, send_edge.at[i], recv_edge.at[i], {"space": strip + 1})

    def row_up():
        return copy(row_out.at[0], row_in.at[1], send_row.at[0], recv_row.at[0], {"space": strip - 1})

    def row_down():
        return copy(row_out.at[1], row_in.at[0], send_row.at[1], recv_row.at[1], {"space": strip + 1})

    def col_left(j):
        return copy(col_out.at[j, 0], col_in.at[j, 1], send_col.at[j, 0], recv_col.at[j, 0], {"spec": me - 1})

    def col_right(j):
        return copy(col_out.at[j, 1], col_in.at[j, 0], send_col.at[j, 1], recv_col.at[j, 1], {"spec": me + 1})

    barrier = pltpu.get_barrier_semaphore()
    for delta in range(1, slots):
        pl.semaphore_signal(barrier, inc=1, device_id={"spec": peer(delta)}, device_id_type=MESH)

    @pl.when(has_before)
    def _():
        pl.semaphore_signal(barrier, inc=1, device_id={"space": strip - 1}, device_id_type=MESH)

    @pl.when(has_after)
    def _():
        pl.semaphore_signal(barrier, inc=1, device_id={"space": strip + 1}, device_id_type=MESH)

    held = [
        pltpu.make_async_copy(source, target, held_sem.at[i])
        for i, (source, target) in enumerate((
            (spectrum_raw, spectrum), (turn_raw, turn), (taps_raw, taps), (across_raw, across),
            (proj_raw, proj_held), (back_raw, back_held), (outer_raw, outer), (through_raw, through),
            (inside_raw, inside), (spread_raw, spread), (pick_raw, pick), (pay_turn_raw, pay_turn),
            (unturn_raw, unturn),
        ))
    ]
    for each in held:
        each.start()
    for i in range(2):
        surface[i] = velocity[i, 0]
        deeper[i] = velocity[i, 1]
    deeper[2] = mixing[0]
    deeper[3] = active[...].astype(F32)
    expected = slots - 1 + has_before.astype(jnp.int32) + has_after.astype(jnp.int32)
    pl.semaphore_wait(barrier, expected)
    for delta in range(1, slots):
        upward(delta).start()
    for delta in range(1, slots):
        downward(delta).start()
    surfaces[me] = surface[...]
    deepers[me] = deeper[...]

    land = land_sea[...].astype(F32)
    for r in range(rows):
        land_row[:, r * width : (r + 1) * width] = land[r : r + 1, :]

    def turned(value, count):
        wet = (value.astype(F32) * land[None]).astype(BF16).reshape(count * rows, width)
        return jnp.dot(turn[:, : count * rows], wet, preferred_element_type=F32).astype(BF16)

    def place_turned(value, at):
        for r in range(rows):
            field[at, (r + 2) * width : (r + 3) * width] = value[r * ROWS : (r + 1) * ROWS]

    def by_groups(count, body):
        many = next(n for n in (4, 5, 3, 2, 1) if count % n == 0)

        def some(q, carry):
            for i in range(many):
                body(pl.ds(pl.multiple_of((q * many + i) * ROWS, ROWS), ROWS))
            return carry

        lax.fori_loop(0, count // many, some, 0)

    def turn_group(at):
        place_turned(turned(spectrum[at], ROWS), at)

    whole_groups = comps // ROWS
    for each in held[:4]:
        each.wait()
    by_groups(whole_groups, turn_group)
    if rest:
        place_turned(turned(spectrum[whole_groups * ROWS :], rest), slice(whole_groups * ROWS, padded))
    head[...] = field[:, edge : 2 * edge]
    tail[...] = field[:, points : points + edge]

    @pl.when(has_before)
    def _():
        to_before(head, after, 0).start()

    @pl.when(has_after)
    def _():
        to_after(tail, before, 1).start()

    for delta in range(1, slots):
        upward(delta).wait()
    for b in range(slots):
        here = jnp.zeros((2, high, 128), F32)
        for s in range(slots):
            here = here + (owners[s] == b).astype(F32) * surfaces[s]
        for i in range(high):
            at = b * block + i * 128
            strip_rows[0:1, at : at + 128] = here[0, i : i + 1]
            strip_rows[1:2, at : at + 128] = here[1, i : i + 1]
    east[:, edge : edge + points] = current_scale * strip_rows[0:1, :]
    north[...] = current_scale * strip_rows[1:2, :]
    east_head[...] = east[:, edge : 2 * edge]
    east_tail[...] = east[:, points : points + edge]

    @pl.when(has_before)
    def _():
        to_before(east_head, east_after, 2).start()

    @pl.when(has_after)
    def _():
        to_after(east_tail, east_before, 3).start()

    def take_halos():
        @pl.when(has_after)
        def _():
            to_after(head, after, 0).wait_recv()
            to_after(east_head, east_after, 2).wait_recv()
            field[:, edge + points :] = after[...]
            east[:, edge + points :] = east_after[...]

        @pl.when(jnp.logical_not(has_after))
        def _():
            field[:, edge + points :] = jnp.zeros((padded, edge), BF16)
            east[:, edge + points :] = jnp.zeros((1, edge), F32)

        @pl.when(has_before)
        def _():
            to_before(tail, before, 1).wait_recv()
            to_before(east_tail, east_before, 3).wait_recv()
            field[:, :edge] = before[...]
            east[:, :edge] = east_before[...]

        @pl.when(jnp.logical_not(has_before))
        def _():
            field[:, :edge] = jnp.zeros((padded, edge), BF16)
            east[:, :edge] = jnp.zeros((1, edge), F32)

    def grouped(body):
        many = 3 if groups % 3 == 0 else 1

        def some(q, carry):
            for i in range(many):
                body(pl.ds(pl.multiple_of((q * many + i) * ROWS, ROWS), ROWS))
            return carry

        lax.fori_loop(0, groups // many, some, 0)

    halves = width // 128

    def wide(tap, i):
        return jnp.broadcast_to(tap[:, i : i + 1], (ROWS, 128))

    def advect_first(t, carry):
        @pl.when(t == min(1, chunks - 1))
        def _():
            take_halos()

        j = first_order(t)
        base = j * lanes * slots

        def lane(row, half):
            return pl.ds(pl.multiple_of(base + row * width + half * 128, 128), 128)

        def along_columns(here):
            tap = taps[me, here, :]
            speed = wide(tap, 1)
            northward = wide(tap, 7) != 0.0
            for c in range(chunk_rows):
                for half in range(halves):
                    along = (speed + north[:, lane(c, half)]) * field[here, lane(c + 2, half)].astype(F32)
                    at = half * 128
                    flow_cols[c, here, at : at + 128] = jnp.where(northward, along, 0.0).astype(BF16)
                    at = width + half * 128
                    flow_cols[c, here, at : at + 128] = jnp.where(northward, 0.0, along).astype(BF16)


        def along_rows(here):
            tap = taps[me, here, :]
            speed = wide(tap, 0)
            row_tap = [wide(tap, 2 + i) for i in range(5)]
            done = {}
            for half in range(halves):
                masked = {}
                flow = {}
                for r in range(-2, chunk_rows + 2):
                    masked[r] = field[here, lane(r + 2, half)].astype(F32)
                    flow[r] = (speed + east[:, lane(r + 2, half)]) * masked[r]
                    c = r - 2
                    if c < 0:
                        continue
                    total = masked.pop(c) - flow_rows[c, here, half * 128 : (half + 1) * 128] * (1.0 / 6.0)
                    for i in range(5):
                        total = total - row_tap[i] * flow[c - 2 + i]
                    flow.pop(c - 2)
                    done[c, half] = total * land_row[:, lane(c, half)]
            for d in range(slots):
                half, at = d * seg // 128, d * seg % 128
                for v in range(tiles):
                    blocks[d, j, here, v * 128 : (v + 1) * 128] = jnp.concatenate(
                        [done[v * per_tile + h, half][:, at : at + seg] for h in range(per_tile)], 1
                    ).astype(BF16)

        def one_part(p, carry):
            low = p * part_rows
            here = pl.ds(pl.multiple_of(low, ROWS), part_rows)

            def over(body):
                def some(q, carry):
                    for i in range(many):
                        body(pl.ds(pl.multiple_of(low + (q * many + i) * ROWS, ROWS), ROWS))
                    return carry

                lax.fori_loop(0, part_rows // ROWS // many, some, 0)

            over(along_columns)

            def one_row(c, carry):
                flow_rows[c, here] = jnp.dot(flow_cols[c, here], across[...], preferred_element_type=F32)
                return carry

            lax.fori_loop(0, chunk_rows, one_row, 0)
            over(along_rows)
            if parts > 1:

                @pl.when((p < parts - 1) & (t < ahead))
                def _():
                    for delta in range(1, slots):
                        inward(j, delta, here, p).start()

            return carry

        lax.fori_loop(0, parts, one_part, 0)
        if rest:
            for delta in range(1, slots):
                rest_out[peer(delta), j] = fold(blocks[peer(delta), j, body_rows:])

        @pl.when(t < ahead)
        def _():
            for delta in range(1, slots):
                inward(j, delta, last_part, parts - 1).start()
                if rest:
                    inward_rest(j, delta).start()

        return carry

    lax.fori_loop(0, chunks, advect_first, 0)

    @pl.when(jnp.logical_not(has_left))
    def _():
        col_in[:, 0] = jnp.zeros_like(col_in[:, 0])

    @pl.when(jnp.logical_not(has_right))
    def _():
        col_in[:, 1] = jnp.zeros_like(col_in[:, 1])

    zeros = jnp.zeros((padded, 128), BF16)

    def clear(g, carry):
        for flux in (flux_e, flux_w):

            @pl.when(jnp.logical_not(has_before))
            def _():
                flux[g, :, :128] = zeros

            @pl.when(jnp.logical_not(has_after))
            def _():
                flux[g, :, 128 + tile_points :] = zeros

        return carry

    lax.fori_loop(0, slots, clear, 0)
    for j in range(chunks):
        got[j, me] = blocks[me, j]

    for delta in range(1, slots):
        downward(delta).wait()
    for b in range(slots):
        here = jnp.zeros((4, high, 128), F32)
        for s in range(slots):
            here = here + (owners[s] == b).astype(F32) * deepers[s]
        for f in range(4):
            for i in range(high):
                at = b * block + i * 128
                strip_rows[2 + f : 3 + f, at : at + 128] = here[f, i : i + 1]
    strip_rows[6:7, :] = land_row[...]
    strip_rows[7:8, :] = land_row[...]
    pieces_of = [[] for _ in range(slots)]
    for r in range(rows):
        line = strip_rows[:, r * width : (r + 1) * width]
        for d in range(slots):
            pieces_of[d].append(line[:, d * seg : (d + 1) * seg])
    mine = jnp.zeros((8, tile_points), F32)
    for d in range(slots):
        mine = mine + (me == d).astype(F32) * jnp.concatenate(pieces_of[d], 1)
    tile[...] = mine
    for each in held[4:]:
        each.wait()
    eye = lax.broadcasted_iota(jnp.int32, (proj.shape[1], proj.shape[1]), 0)
    eye = (eye == lax.broadcasted_iota(jnp.int32, eye.shape, 1)).astype(F32).astype(BF16)
    mixed_rows = jnp.zeros((through.shape[1], proj.shape[1]), F32)
    for g in range(slots):
        low = g * comps // ROWS * ROWS
        window = min(padded + ROWS, slots * comps - low)
        row = lax.broadcasted_iota(jnp.int32, (padded, window), 0)
        shift = lax.broadcasted_iota(jnp.int32, (padded, window), 1) - row
        shift = ((shift == g * comps - low) & (row < comps)).astype(F32).astype(BF16)
        back[g] = jnp.dot(shift, back_held[low : low + window], preferred_element_type=F32).astype(BF16)
        aligned = jnp.dot(shift, proj_held[low : low + window], preferred_element_type=F32).astype(BF16)
        proj[g] = lax.dot_general(
            eye, aligned, (((1,), (1,)), ((), ())), preferred_element_type=F32
        ).astype(BF16)
        mixed_rows = mixed_rows + jnp.dot(through[g], back[g], preferred_element_type=F32)
    half = mixed_rows.shape[0] // 2
    mixed_rows = mixed_rows[:half] + mixed_rows[half:]
    first = mixed_rows.astype(BF16)
    inner[:half] = first
    inner[half:] = (mixed_rows - first.astype(F32)).astype(BF16)

    def project(values, step, j):
        projected = jnp.dot(proj[0], values[0], preferred_element_type=F32)
        more = jnp.dot(outer[0], values[0], preferred_element_type=F32)
        for g in range(1, slots):
            projected = projected + jnp.dot(proj[g], values[g], preferred_element_type=F32)
            more = more + jnp.dot(outer[g], values[g], preferred_element_type=F32)
        cubed = (projected * projected * projected).astype(BF16)
        more = more + jnp.dot(inner[...], cubed, preferred_element_type=F32)
        half = more.shape[0] // 2
        payload = more[:half] + more[half:]
        pay[step, j] = payload
        return cubed, payload

    def send_payload(step):
        whole_pay = jnp.concatenate([pay[step, j] for j in range(chunks)], 1)
        for s in range(slots):
            value = jnp.zeros((whole_pay.shape[0], part), F32)
            for b in range(slots):
                value = value + (owners[s] == b).astype(F32) * whole_pay[:, b * part : (b + 1) * part]
            pay_out[step, s] = value.astype(BF16)
        pay_in[step, me] = pay_out[step, me]
        for delta in range(1, slots):
            pay_over(step, delta).start()

    def source_first(t):
        j = first_order(t)
        for delta in range(1, slots):
            for each in inward_parts(j, delta):
                each.wait_recv()
            if rest:
                inward_rest(j, delta).wait_recv()
                sender = lax.rem(me + slots - delta, slots)
                got[j, sender, body_rows:] = unfold(rest_in[j, sender])
        cubed, payload = project(got.at[j], 0, j)
        own = tile[:, pl.ds(pl.multiple_of(j * lanes, 128), lanes)]
        u0, v0, u1, v1 = own[0:1], own[1:2], own[2:3], own[3:4]
        mix, depth = own[4:5], own[5:6]
        live = (depth > 0.5).astype(F32)
        below = mix * (depth > 1.5).astype(F32)
        floor = mix * ((depth > 0.5) & (depth < 1.5)).astype(F32)
        push_u, push_v = payload[0:1], payload[layers : layers + 1]
        new_u = live * (u0 + coriolis * v0 - below * (u0 - u1) - floor * u0 + push_u)
        new_v = live * (v0 - coriolis * u0 - below * (v0 - v1) - floor * v0 + push_v)
        east_here = current_scale * new_u
        north_here = current_scale * new_v

        def one_group(g):
            transfer = jnp.dot(back[g], cubed, preferred_element_type=F32)
            updated = (got[j, g].astype(F32) + source_step * transfer).astype(BF16)
            state[j, g] = updated
            updated = updated.astype(F32)
            along_x = (taps[g, :, 0:1] + east_here) * updated
            eastward = taps[g, :, 2:3] != 0.0
            at = pl.ds(pl.multiple_of(128 + j * lanes, 128), lanes)
            flux_e[g, :, at] = jnp.where(eastward, along_x, 0.0).astype(BF16)
            flux_w[g, :, at] = jnp.where(eastward, 0.0, along_x).astype(BF16)
            along_y = (taps[g, :, 1:2] + north_here) * updated
            northward = taps[g, :, 7:8] != 0.0
            flux_n[j, g] = jnp.where(northward, along_y, 0.0).astype(BF16)
            flux_s[j, g] = jnp.where(northward, 0.0, along_y).astype(BF16)
            along_y = along_y.astype(BF16)
            ends = lax.dot_general(
                pick[...], along_y, (((1,), (1,)), ((), ())), preferred_element_type=F32
            )

            @pl.when(j == 0)
            def _():
                row_out[0, g] = along_x[:, :128].astype(BF16)

            @pl.when(j == chunks - 1)
            def _():
                row_out[1, g] = along_x[:, lanes - 128 :].astype(BF16)

            half = ends.shape[0] // 2
            return ends[:half], ends[half:]

        def one_source(p, carry):
            ends = [one_group(p * pack + i) for i in range(pack)]
            for side in range(2):
                col_out[j, side, p] = jnp.concatenate([both[side] for both in ends], 0).astype(BF16)
            return carry

        lax.fori_loop(0, slots // pack, one_source, 0)

        @pl.when(has_left)
        def _():
            col_left(j).start()

        @pl.when(has_right)
        def _():
            col_right(j).start()

        @pl.when((j == 0) & has_before)
        def _():
            row_up().start()

        @pl.when((j == chunks - 1) & has_after)
        def _():
            row_down().start()

    def advect_second(j):
        def put(place, at):
            def one(g, carry):
                eastward = taps[g, :, 2:3] != 0.0
                value = row_in[place, g].astype(F32)
                flux_e[g, :, at : at + 128] = jnp.where(eastward, value, 0.0).astype(BF16)
                flux_w[g, :, at : at + 128] = jnp.where(eastward, 0.0, value).astype(BF16)
                return carry

            lax.fori_loop(0, slots, one, 0)

        @pl.when((j == 0) & has_before)
        def _():
            row_down().wait_recv()
            put(0, 0)

        @pl.when((j == chunks - 1) & has_after)
        def _():
            row_up().wait_recv()
            put(1, 128 + tile_points)

        @pl.when(has_left)
        def _():
            col_right(j).wait_recv()

        @pl.when(has_right)
        def _():
            col_left(j).wait_recv()

        start = pl.multiple_of(j * lanes, 128)
        land_here = tile[6:7, pl.ds(start, lanes)]

        def one_advect(g, carry):
            rows_at = pl.ds(start, lanes + 256)
            every = jnp.concatenate(
                [flux_e[g, :, rows_at], flux_w[g, :, rows_at], flux_n[j, g], flux_s[j, g]], 1
            )
            ends = jnp.concatenate([col_in[j, 0, g // pack], col_in[j, 1, g // pack]], 0)
            ends_north = ends * north_mask[g]
            ends = jnp.concatenate([ends_north, ends - ends_north], 0)
            change = jnp.dot(every, inside[...], preferred_element_type=F32) + lax.dot_general(
                ends, spread[lax.rem(g, pack)], (((0,), (0,)), ((), ())), preferred_element_type=F32
            )
            total = (state[j, g].astype(F32) - change * (1.0 / 6.0)) * land_here
            drift[g] = total.astype(BF16)
            return carry

        lax.fori_loop(0, slots, one_advect, 0)

    def source_second(t):
        j = flip(t)
        advect_second(j)
        cubed, _ = project(drift, 1, j)

        for delta in range(slots):
            g = peer(delta)
            transfer = jnp.dot(back[g], cubed, preferred_element_type=F32)
            updated = (drift[g].astype(F32) + source_step * transfer).astype(BF16)
            if delta:
                made[j, g] = updated
                homeward(j, delta).start()
                if rest:
                    rest_made[j, g] = fold(updated[body_rows:])
                    homeward_rest(j, delta).start()
            else:
                returned[j, g] = updated

        @pl.when(t == chunks - 1)
        def _():
            send_payload(1)

    def middle(u, carry):
        @pl.when(u < chunks)
        def _():
            source_first(u)

        @pl.when(u + ahead < chunks)
        def _():
            j = first_order(u + ahead)
            for delta in range(1, slots):
                for each in inward_parts(j, delta):
                    each.start()
                if rest:
                    inward_rest(j, delta).start()

        @pl.when(u == chunks - 1)
        def _():
            send_payload(0)

        @pl.when(u > 0)
        def _():
            source_second(u - 1)

        return carry

    lax.fori_loop(0, chunks + 1, middle, 0)

    layer = lax.broadcasted_iota(jnp.int32, (layers, high, 128), 0)
    depth = active[...][None]
    live = (layer < depth).astype(F32)
    bottom = mixing[...] * (layer == depth - 1).astype(F32)
    upper = mixing[...] * ((layer + 1 < depth) & (layer < layers - 1)).astype(F32)
    nothing = jnp.zeros((1, high, 128), F32)

    def mixed(value):
        between = upper * (value - jnp.concatenate([value[1:], nothing], 0))
        return jnp.concatenate([nothing, between[:-1]], 0) - between - bottom * value

    def ocean_step(step, east_old, north_old):
        for delta in range(1, slots):
            pay_over(step, delta).wait_recv()
        lines = []
        for i in range(high):
            pieces = []
            for h in range(per_tile):
                r, d = divmod(i * per_tile + h, slots)
                pieces.append(pay_in[step, d].astype(F32)[:, r * seg : (r + 1) * seg])
            lines.append(jnp.concatenate(pieces, 1))
        lines = jnp.concatenate(lines, 0).astype(BF16)
        push = jnp.dot(pay_turn[...], lines, preferred_element_type=F32).reshape(2, layers, high, 128)
        new_velocity[0] = live * (east_old + coriolis * north_old + mixed(east_old) + push[0])
        new_velocity[1] = live * (north_old - coriolis * east_old + mixed(north_old) + push[1])

    ocean_step(0, velocity[0], velocity[1])

    def unpack(t, carry):
        j = flip(t)
        for delta in range(1, slots):
            homeward(j, delta).wait_recv()
            if rest:
                homeward_rest(j, delta).wait_recv()
                sender = lax.rem(me + slots - delta, slots)
                returned[j, sender, body_rows:] = unfold(rest_back[j, sender])

        def one_group(here):
            parts = [returned[j, d, here, :].astype(F32) for d in range(slots)]
            for k in range(chunk_rows):
                line = jnp.concatenate([p[:, k * seg : (k + 1) * seg] for p in parts], 1)
                at = pl.ds(pl.multiple_of((j * chunk_rows + k) * width, 128), width)
                field[here, at] = line.astype(BF16)

        grouped(one_group)
        return carry

    lax.fori_loop(0, chunks, unpack, 0)

    def unturned(at, count):
        value = jnp.concatenate([field[at, r * width : (r + 1) * width] for r in range(rows)], 0)
        back_again = jnp.dot(unturn[: count * rows], value, preferred_element_type=F32)
        return back_again.astype(BF16).reshape(count, rows, width)

    def unturn_group(at):
        out[at] = unturned(at, ROWS)

    by_groups(whole_groups, unturn_group)
    if rest:
        out[whole_groups * ROWS :] = unturned(slice(whole_groups * ROWS, padded), rest)
    for step in range(1, STEPS):
        ocean_step(step, new_velocity[0], new_velocity[1])

    @pl.when(has_before)
    def _():
        to_before(head, after, 0).wait_send()
        to_before(east_head, east_after, 2).wait_send()
        row_up().wait_send()

    @pl.when(has_after)
    def _():
        to_after(tail, before, 1).wait_send()
        to_after(east_tail, east_before, 3).wait_send()
        row_down().wait_send()

    for j in range(chunks):
        for delta in range(1, slots):
            for each in inward_parts(j, delta):
                each.wait_send()
            homeward(j, delta).wait_send()
            if rest:
                inward_rest(j, delta).wait_send()
                homeward_rest(j, delta).wait_send()

        @pl.when(has_left)
        def _():
            col_left(j).wait_send()

        @pl.when(has_right)
        def _():
            col_right(j).wait_send()

    for step in range(STEPS):
        for delta in range(1, slots):
            pay_over(step, delta).wait_send()


def handing_kernel(spectrum, velocity, new_spectrum, new_velocity, waves, ocean, sems):
    count = spectrum.shape[0]
    parts = 6
    pieces = [(velocity, ocean, new_velocity)]
    for i in range(parts):
        low, high = i * count // parts, (i + 1) * count // parts
        at = pl.ds(low, high - low)
        pieces.append((spectrum.at[at], waves.at[at], new_spectrum.at[at]))
    loads = [pltpu.make_async_copy(a, b, sems.at[0, i]) for i, (a, b, _) in enumerate(pieces)]
    stores = [pltpu.make_async_copy(b, c, sems.at[1, i]) for i, (_, b, c) in enumerate(pieces)]
    for each in loads:
        each.start()
    for load, store in zip(loads, stores):
        load.wait()
        store.start()
    for each in stores:
        each.wait()


def whole(count, memory=pltpu.VMEM):
    return [pl.BlockSpec(memory_space=memory)] * count


def body(spectrum, land_sea, owners, proj_weight, back_weight, ocean_vel, mixing, active_layers):
    comps, rows, width = spectrum.shape
    slots = lax.axis_size("spec")
    points = rows * width
    block = points // slots
    seg = width // slots
    tile_points = rows * seg
    lanes = 256 if tile_points % 256 == 0 else tile_points
    chunks = tile_points // lanes
    chunk_rows = lanes // seg
    layers = mixing.shape[0]
    rank_rows = proj_weight.shape[0]
    padded = -(-comps // ROWS) * ROWS
    edge = 2 * width
    edge_rows = 2 * chunk_rows
    pack = max(1, ROWS // edge_rows)
    high = block // 128
    part = block // slots

    def by_slot(table):
        result = np.zeros((slots, table.shape[0], padded), table.dtype)
        result[:, :, :comps] = table.reshape(table.shape[0], slots, comps).transpose(1, 0, 2)
        return result

    taps = np.zeros((slots, padded, 12), np.float32)
    taps[:, :comps] = tap_table().reshape(slots, comps, 12)
    drift_rows, stress_rows = coupling_tables(layers)
    push = coriolis * np.concatenate([drift_rows[layers:], -drift_rows[:layers]], 0)
    outer = by_slot(two_pieces(push))
    push = source_step * push
    push[0] += stress_rows[0]
    push[layers] += stress_rows[1]
    through = by_slot(two_pieces(push))
    tables = stencil_tables(seg, width, chunk_rows, edge_rows, pack)
    north_mask = (taps[:, :, 7] != 0).astype(BF16).reshape(slots, 1, padded)
    turn = turn_table(ROWS, rows)
    pay_turn = np.zeros((high * 2 * layers,) * 2, np.float32)
    for l in range(2 * layers):
        for i in range(high):
            pay_turn[l * high + i, i * 2 * layers + l] = 1
    pay_turn = pay_turn.astype(BF16)
    velocity = ocean_vel.reshape(2, layers, high, 128)
    inside, across, spread, pick = tables
    raw = (spectrum, turn, taps, across, proj_weight.T, back_weight, outer, through, inside, spread, pick, pay_turn,
           np.ascontiguousarray(turn.T))
    raw = [jnp.asarray(each) for each in raw]
    exchange = pltpu.VMEM((chunks, slots, padded, lanes), BF16)
    pay_rows = 2 * layers
    state, velocity = pl.pallas_call(
        functools.partial(steps_kernel, (comps, rows, width, slots)),
        out_shape=(
            jax.ShapeDtypeStruct((comps, rows, width), BF16),
            jax.ShapeDtypeStruct((2, layers, high, 128), F32),
        ),
        in_specs=whole(1, pltpu.SMEM) + whole(5) + whole(13, pl.ANY),
        out_specs=tuple(whole(2)),
        scratch_shapes=[
            pltpu.VMEM((padded, points + 2 * edge), BF16),
            pltpu.VMEM((1, points + 2 * edge), F32),
            pltpu.VMEM((1, points), F32),
            pltpu.VMEM((1, points), F32),
            pltpu.VMEM((2, high, 128), F32),
            pltpu.VMEM((slots, 2, high, 128), F32),
            pltpu.VMEM((4, high, 128), F32),
            pltpu.VMEM((slots, 4, high, 128), F32),
            pltpu.VMEM((8, points), F32),
            pltpu.VMEM((8, tile_points), F32),
            *[pltpu.VMEM(each.shape, each.dtype) for each in raw],
            pltpu.VMEM((slots, rank_rows, padded), BF16),
            pltpu.VMEM((slots, padded, rank_rows), BF16),
            pltpu.VMEM((outer.shape[1], rank_rows), BF16),
            pltpu.VMEM((slots, chunks, ROWS, 128), BF16),
            *[pltpu.VMEM((chunks, slots, ROWS, 128), BF16)] * 3,
            pltpu.VMEM((chunk_rows, padded, width), F32),
            pltpu.VMEM((chunk_rows, padded, 2 * width), BF16),
            pltpu.VMEM((slots, chunks, padded, lanes), BF16),
            exchange,
            exchange,
            pltpu.VMEM((slots, padded, tile_points + 256), BF16),
            pltpu.VMEM((slots, padded, tile_points + 256), BF16),
            exchange,
            exchange,
            pltpu.VMEM((slots, padded, lanes), BF16),
            exchange,
            exchange,
            pltpu.VMEM((STEPS, chunks, pay_rows, lanes), F32),
            pltpu.VMEM((STEPS, slots, pay_rows, part), BF16),
            pltpu.VMEM((STEPS, slots, pay_rows, part), BF16),
            pltpu.VMEM((2, slots, padded, 128), BF16),
            pltpu.VMEM((2, slots, padded, 128), BF16),
            pltpu.VMEM((chunks, 2, slots // pack, pack * edge_rows, padded), BF16),
            pltpu.VMEM((chunks, 2, slots // pack, pack * edge_rows, padded), BF16),
        ]
        + [pltpu.VMEM((padded, edge), BF16)] * 4
        + [pltpu.VMEM((1, edge), F32)] * 4
        + [pltpu.SemaphoreType.DMA((chunks, 4 * slots))] * 4
        + [pltpu.SemaphoreType.DMA((slots,))] * 4
        + [pltpu.SemaphoreType.DMA((4,))] * 2
        + [pltpu.SemaphoreType.DMA((2,))] * 2
        + [pltpu.SemaphoreType.DMA((chunks, 2))] * 2
        + [pltpu.SemaphoreType.DMA((STEPS, slots))] * 2
        + [pltpu.SemaphoreType.DMA((len(raw),))],
        compiler_params=pltpu.CompilerParams(
            vmem_limit_bytes=VMEM_LIMIT, collective_id=0, has_side_effects=True
        ),
        name="steps",
    )(owners, land_sea, velocity, mixing.reshape(layers, high, 128), active_layers.reshape(high, 128),
      jnp.asarray(north_mask), *raw)
    state, velocity = pl.pallas_call(
        handing_kernel,
        out_shape=(
            jax.ShapeDtypeStruct(state.shape, BF16),
            jax.ShapeDtypeStruct(velocity.shape, F32),
        ),
        in_specs=whole(2, pl.ANY),
        out_specs=tuple(whole(2, pl.ANY)),
        scratch_shapes=[
            pltpu.VMEM(state.shape, BF16),
            pltpu.VMEM(velocity.shape, F32),
            pltpu.SemaphoreType.DMA((2, 7)),
        ],
        name="hand",
    )(state, velocity)
    return (state, velocity.reshape(ocean_vel.shape))


def solution(mesh):
    placed = (
        P("spec", "space", None),
        P("space", None),
        P(),
        P(),
        P(),
        P(None, None, "spec", "space", None),
        P(None, "spec", "space", None),
        P("spec", "space", None),
    )
    return jax.shard_map(
        body,
        mesh=mesh,
        in_specs=placed,
        out_specs=(P("spec", "space", None), P(None, None, "spec", "space", None)),
        check_vma=False,
    )
```

```python
import functools
import math

import jax
import jax.numpy as jnp
import numpy as np
from jax import lax
from jax.experimental import pallas as pl
from jax.experimental.pallas import tpu as pltpu
from jax.sharding import PartitionSpec as P

NDIR = 36
NFREQ = 36
K = NDIR * NFREQ
STEPS = 2

courant_scale = 0.5
current_scale = 0.15
source_step = 0.25
coriolis = 0.3
stress_scale = 0.5
drift_scale = 4.0

MESH = pl.DeviceIdType.MESH
F32 = jnp.float32
BF16 = jnp.bfloat16
VMEM_LIMIT = 60 * 1024 * 1024
ROWS = 16


def tap_table():
    component = np.arange(K)
    frequency = component // NDIR
    direction = component % NDIR
    angle = (direction + 0.5) * (2.0 * math.pi / NDIR)
    speed = courant_scale * np.exp(-2.0 * frequency / NFREQ)
    eastward = (4 * direction + 2 < NDIR) | (4 * direction + 2 > 3 * NDIR)
    northward = 2 * direction + 1 < NDIR
    forward = (1.0 / 6.0, -1.0, 0.5, 2.0 / 6.0, 0.0)
    backward = (0.0, -2.0 / 6.0, -0.5, 1.0, -1.0 / 6.0)
    columns = [speed * np.cos(angle), speed * np.sin(angle)]
    for mask in (eastward, northward):
        for f, b in zip(forward, backward):
            columns.append(np.where(mask, f, b))
    return np.stack(columns, 1).astype(np.float32)


def coupling_tables(layers):
    component = np.arange(K)
    frequency = component // NDIR
    angle = (component % NDIR + 0.5) * (2.0 * math.pi / NDIR)
    wavenum = 0.02 * np.exp(6.0 * frequency / NFREQ)
    depth = np.arange(layers)[:, None] + 0.5
    decay_rows = wavenum[None, :] ** 1.5 * np.exp(-2.0 * wavenum[None, :] * depth)
    decay_rows = decay_rows / np.sqrt(np.sum(decay_rows * decay_rows, axis=1, keepdims=True))
    drift_rows = drift_scale * np.concatenate(
        [decay_rows * np.cos(angle)[None, :], decay_rows * np.sin(angle)[None, :]], 0
    )
    stress = wavenum / np.sqrt(np.sum(wavenum * wavenum))
    stress_rows = -stress_scale * np.stack([stress * np.cos(angle), stress * np.sin(angle)], 0)
    return (drift_rows.astype(np.float32), stress_rows.astype(np.float32))


def two_pieces(rows):
    first = rows.astype(BF16)
    second = (rows - first.astype(np.float32)).astype(BF16)
    return np.concatenate([first, second], 0)


FORWARD = (1, -6, 3, 2, 0)
BACKWARD = (0, -2, -3, 6, -1)


def stencil_tables(seg, width, rows_in_chunk, edge_rows, pack):
    lanes = rows_in_chunk * seg
    inside = np.zeros((4, lanes + 256, lanes), np.float32)
    across = np.zeros((2, width, width), np.float32)
    spread = np.zeros((2, 2 * edge_rows, lanes), np.float32)
    pick = np.zeros((2 * edge_rows, lanes), np.float32)
    for v, taps in enumerate((FORWARD, BACKWARD)):
        for b in range(lanes):
            for k in range(-2, 3):
                inside[v, 128 + b + k * seg, b] = taps[k + 2]
                if b // seg == (b + k) // seg:
                    inside[2 + v, b + k, b] = taps[k + 2]
        for b in range(width):
            for k in range(-2, 3):
                if 0 <= b + k < width:
                    across[v, b + k, b] = taps[k + 2]
        for k in range(rows_in_chunk):
            for i in range(2):
                for c in range(seg):
                    for row, offset in ((k * 2 + i, i - 2 - c), (edge_rows + k * 2 + i, seg + i - c)):
                        if abs(offset) <= 2:
                            spread[v, row, k * seg + c] = taps[offset + 2]
    for k in range(rows_in_chunk):
        for i in range(2):
            pick[k * 2 + i, k * seg + i] = 1
            pick[edge_rows + k * 2 + i, k * seg + seg - 2 + i] = 1
    inside = np.concatenate([inside[0], inside[1], inside[2, :lanes], inside[3, :lanes]], 0)
    held = np.zeros((pack, 2, 2, pack, edge_rows, lanes), np.float32)
    for i in range(pack):
        held[i, :, :, i] = spread.reshape(2, 2, edge_rows, lanes)
    held = held.reshape(pack, 4 * pack * edge_rows, lanes)
    tables = (inside, across.reshape(2 * width, width), held, pick)
    return [table.astype(BF16) for table in tables]


def turn_table(first, second):
    table = np.zeros((first * second, first * second), np.float32)
    for c in range(first):
        for r in range(second):
            table[r * first + c, c * second + r] = 1
    return table.astype(BF16)


def steps_kernel(
    sizes, owners, land_sea, velocity, mixing, active, north_mask,
    spectrum_raw, turn_raw, taps_raw, across_raw,
    proj_raw, back_raw, outer_raw, through_raw, inside_raw, spread_raw, pick_raw, pay_turn_raw, unturn_raw,
    out, new_velocity,
    field, east, north, land_row, surface, surfaces, deeper, deepers, strip_rows, tile,
    spectrum, turn, taps, across, proj_held, back_held, outer, through, inside, spread, pick, pay_turn, unturn,
    proj, back, inner, rest_out, rest_in, rest_made, rest_back,
    flow_rows, flow_cols, blocks, got, state, flux_e, flux_w, flux_n, flux_s, drift, made, returned,
    pay, pay_out, pay_in, row_out, row_in, col_out, col_in,
    head, tail, before, after, east_head, east_tail, east_before, east_after,
    send_in, recv_in, send_back, recv_back, send_top, recv_top, send_deep, recv_deep, send_edge, recv_edge,
    send_row, recv_row, send_col, recv_col, send_pay, recv_pay, held_sem, out_sem, out_held,
):
    comps, rows, width, slots = sizes
    padded = field.shape[0]
    chunks, lanes = got.shape[0], got.shape[3]
    seg = width // slots
    per_tile = 128 // seg
    tiles = lanes // 128
    chunk_rows = lanes // seg
    high = velocity.shape[2]
    block = high * 128
    block_rows = block // width
    part = block_rows * seg
    points = rows * width
    tile_points = rows * seg
    layers = mixing.shape[0]
    groups = padded // ROWS
    pack = slots // col_out.shape[2]
    me = lax.axis_index("spec")
    strip = lax.axis_index("space")
    strips = lax.axis_size("space")
    edge = 2 * width
    has_before = strip > 0
    has_after = strip < strips - 1
    has_left = me > 0
    has_right = me < slots - 1
    odd = lax.rem(strip, 2) == 1

    def peer(delta):
        return lax.rem(me + delta, slots)

    def flip(base):
        return jnp.where(odd, chunks - 1 - base, base)

    ahead = 2

    def first_order(t):
        return flip(jnp.where(t < 2, 1 - t, t) if chunks > 1 else t)

    def copy(source, target, send, receive, device):
        return pltpu.make_async_remote_copy(
            src_ref=source, dst_ref=target, send_sem=send, recv_sem=receive,
            device_id=device, device_id_type=MESH,
        )

    body_rows = comps // ROWS * ROWS
    main = pl.ds(0, body_rows)

    parts = 3 if groups % 3 == 0 else 1
    part_rows = padded // parts
    last_part = pl.ds((parts - 1) * part_rows, body_rows - (parts - 1) * part_rows)
    many = next(n for n in (4, 7, 3, 2, 1) if part_rows // ROWS % n == 0)

    def inward(j, delta, at, p):
        return copy(
            blocks.at[peer(delta), j, at], got.at[j, me, at],
            send_in.at[j, p * slots + delta], recv_in.at[j, p * slots + delta], {"spec": peer(delta)},
        )

    def inward_parts(j, delta):
        early = [inward(j, delta, pl.ds(p * part_rows, part_rows), p) for p in range(parts - 1)]
        return early + [inward(j, delta, last_part, parts - 1)]

    def homeward(j, delta):
        return copy(
            made.at[j, peer(delta), main], returned.at[j, me, main],
            send_back.at[j, delta], recv_back.at[j, delta], {"spec": peer(delta)},
        )

    def inward_rest(j, delta):
        return copy(
            rest_out.at[peer(delta), j], rest_in.at[j, me],
            send_in.at[j, parts * slots + delta], recv_in.at[j, parts * slots + delta], {"spec": peer(delta)},
        )

    def homeward_rest(j, delta):
        return copy(
            rest_made.at[j, peer(delta)], rest_back.at[j, me],
            send_back.at[j, slots + delta], recv_back.at[j, slots + delta], {"spec": peer(delta)},
        )

    rest = comps - body_rows
    tile_row = lax.broadcasted_iota(jnp.int32, (ROWS, 128), 0)

    def fold(value):
        value = jnp.where(jnp.concatenate([tile_row] * tiles, 1) < rest, value.astype(F32), 0.0)
        folded = value[:, :128]
        for v in range(1, tiles):
            folded = folded + pltpu.roll(value[:, v * 128 : (v + 1) * 128], v * rest, 0)
        return folded.astype(BF16)

    def unfold(value):
        value = value.astype(F32)
        parts = []
        for v in range(tiles):
            moved = pltpu.roll(value, ROWS - v * rest, 0) if v else value
            parts.append(jnp.where(tile_row < rest, moved, 0.0))
        return jnp.concatenate(parts, 1).astype(BF16)

    def upward(delta):
        return copy(
            surface, surfaces.at[me], send_top.at[delta], recv_top.at[delta], {"spec": peer(delta)}
        )

    def downward(delta):
        return copy(
            deeper, deepers.at[me], send_deep.at[delta], recv_deep.at[delta], {"spec": peer(delta)}
        )

    def pay_over(step, delta):
        return copy(
            pay_out.at[step, peer(delta)], pay_in.at[step, me],
            send_pay.at[step, delta], recv_pay.at[step, delta], {"spec": peer(delta)},
        )

    def to_before(source, target, i):
        return copy(source, target, send_edge.at[i], recv_edge.at[i], {"space": strip - 1})

    def to_after(source, target, i):
        return copy(source, target, send_edge.at[i], recv_edge.at[i], {"space": strip + 1})

    def row_up():
        return copy(row_out.at[0], row_in.at[1], send_row.at[0], recv_row.at[0], {"space": strip - 1})

    def row_down():
        return copy(row_out.at[1], row_in.at[0], send_row.at[1], recv_row.at[1], {"space": strip + 1})

    def col_left(j):
        return copy(col_out.at[j, 0], col_in.at[j, 1], send_col.at[j, 0], recv_col.at[j, 0], {"spec": me - 1})

    def col_right(j):
        return copy(col_out.at[j, 1], col_in.at[j, 0], send_col.at[j, 1], recv_col.at[j, 1], {"spec": me + 1})

    barrier = pltpu.get_barrier_semaphore()
    for delta in range(1, slots):
        pl.semaphore_signal(barrier, inc=1, device_id={"spec": peer(delta)}, device_id_type=MESH)

    @pl.when(has_before)
    def _():
        pl.semaphore_signal(barrier, inc=1, device_id={"space": strip - 1}, device_id_type=MESH)

    @pl.when(has_after)
    def _():
        pl.semaphore_signal(barrier, inc=1, device_id={"space": strip + 1}, device_id_type=MESH)

    held = [
        pltpu.make_async_copy(source, target, held_sem.at[i])
        for i, (source, target) in enumerate((
            (spectrum_raw, spectrum), (turn_raw, turn), (taps_raw, taps), (across_raw, across),
            (proj_raw, proj_held), (back_raw, back_held), (outer_raw, outer), (through_raw, through),
            (inside_raw, inside), (spread_raw, spread), (pick_raw, pick), (pay_turn_raw, pay_turn),
            (unturn_raw, unturn),
        ))
    ]
    for each in held:
        each.start()
    for i in range(2):
        surface[i] = velocity[i, 0]
        deeper[i] = velocity[i, 1]
    deeper[2] = mixing[0]
    deeper[3] = active[...].astype(F32)
    expected = slots - 1 + has_before.astype(jnp.int32) + has_after.astype(jnp.int32)
    pl.semaphore_wait(barrier, expected)
    for delta in range(1, slots):
        upward(delta).start()
    for delta in range(1, slots):
        downward(delta).start()
    surfaces[me] = surface[...]
    deepers[me] = deeper[...]

    land = land_sea[...].astype(F32)
    for r in range(rows):
        land_row[:, r * width : (r + 1) * width] = land[r : r + 1, :]

    def turned(value, count):
        wet = (value.astype(F32) * land[None]).astype(BF16).reshape(count * rows, width)
        return jnp.dot(turn[:, : count * rows], wet, preferred_element_type=F32).astype(BF16)

    def place_turned(value, at):
        for r in range(rows):
            field[at, (r + 2) * width : (r + 3) * width] = value[r * ROWS : (r + 1) * ROWS]

    def by_groups(count, body):
        many = next(n for n in (4, 5, 3, 2, 1) if count % n == 0)

        def some(q, carry):
            for i in range(many):
                body(pl.ds(pl.multiple_of((q * many + i) * ROWS, ROWS), ROWS))
            return carry

        lax.fori_loop(0, count // many, some, 0)

    def turn_group(at):
        place_turned(turned(spectrum[at], ROWS), at)

    whole_groups = comps // ROWS
    for each in held[:4]:
        each.wait()
    by_groups(whole_groups, turn_group)
    if rest:
        place_turned(turned(spectrum[whole_groups * ROWS :], rest), slice(whole_groups * ROWS, padded))
    head[...] = field[:, edge : 2 * edge]
    tail[...] = field[:, points : points + edge]

    @pl.when(has_before)
    def _():
        to_before(head, after, 0).start()

    @pl.when(has_after)
    def _():
        to_after(tail, before, 1).start()

    for delta in range(1, slots):
        upward(delta).wait()
    for b in range(slots):
        here = jnp.zeros((2, high, 128), F32)
        for s in range(slots):
            here = here + (owners[s] == b).astype(F32) * surfaces[s]
        for i in range(high):
            at = b * block + i * 128
            strip_rows[0:1, at : at + 128] = here[0, i : i + 1]
            strip_rows[1:2, at : at + 128] = here[1, i : i + 1]
    east[:, edge : edge + points] = current_scale * strip_rows[0:1, :]
    north[...] = current_scale * strip_rows[1:2, :]
    east_head[...] = east[:, edge : 2 * edge]
    east_tail[...] = east[:, points : points + edge]

    @pl.when(has_before)
    def _():
        to_before(east_head, east_after, 2).start()

    @pl.when(has_after)
    def _():
        to_after(east_tail, east_before, 3).start()

    def take_halos():
        @pl.when(has_after)
        def _():
            to_after(head, after, 0).wait_recv()
            to_after(east_head, east_after, 2).wait_recv()
            field[:, edge + points :] = after[...]
            east[:, edge + points :] = east_after[...]

        @pl.when(jnp.logical_not(has_after))
        def _():
            field[:, edge + points :] = jnp.zeros((padded, edge), BF16)
            east[:, edge + points :] = jnp.zeros((1, edge), F32)

        @pl.when(has_before)
        def _():
            to_before(tail, before, 1).wait_recv()
            to_before(east_tail, east_before, 3).wait_recv()
            field[:, :edge] = before[...]
            east[:, :edge] = east_before[...]

        @pl.when(jnp.logical_not(has_before))
        def _():
            field[:, :edge] = jnp.zeros((padded, edge), BF16)
            east[:, :edge] = jnp.zeros((1, edge), F32)

    def grouped(body):
        many = 3 if groups % 3 == 0 else 1

        def some(q, carry):
            for i in range(many):
                body(pl.ds(pl.multiple_of((q * many + i) * ROWS, ROWS), ROWS))
            return carry

        lax.fori_loop(0, groups // many, some, 0)

    halves = width // 128

    def wide(tap, i):
        return jnp.broadcast_to(tap[:, i : i + 1], (ROWS, 128))

    def advect_first(t, carry):
        @pl.when(t == min(1, chunks - 1))
        def _():
            take_halos()

        j = first_order(t)
        base = j * lanes * slots

        def lane(row, half):
            return pl.ds(pl.multiple_of(base + row * width + half * 128, 128), 128)

        def along_columns(here):
            tap = taps[me, here, :]
            speed = wide(tap, 1)
            northward = wide(tap, 7) != 0.0
            for c in range(chunk_rows):
                for half in range(halves):
                    along = (speed + north[:, lane(c, half)]) * field[here, lane(c + 2, half)].astype(F32)
                    at = half * 128
                    flow_cols[c, here, at : at + 128] = jnp.where(northward, along, 0.0).astype(BF16)
                    at = width + half * 128
                    flow_cols[c, here, at : at + 128] = jnp.where(northward, 0.0, along).astype(BF16)


        def along_rows(here):
            tap = taps[me, here, :]
            speed = wide(tap, 0)
            row_tap = [wide(tap, 2 + i) for i in range(5)]
            done = {}
            for half in range(halves):
                masked = {}
                flow = {}
                for r in range(-2, chunk_rows + 2):
                    masked[r] = field[here, lane(r + 2, half)].astype(F32)
                    flow[r] = (speed + east[:, lane(r + 2, half)]) * masked[r]
                    c = r - 2
                    if c < 0:
                        continue
                    total = masked.pop(c) - flow_rows[c, here, half * 128 : (half + 1) * 128] * (1.0 / 6.0)
                    for i in range(5):
                        total = total - row_tap[i] * flow[c - 2 + i]
                    flow.pop(c - 2)
                    done[c, half] = total * land_row[:, lane(c, half)]
            for d in range(slots):
                half, at = d * seg // 128, d * seg % 128
                for v in range(tiles):
                    blocks[d, j, here, v * 128 : (v + 1) * 128] = jnp.concatenate(
                        [done[v * per_tile + h, half][:, at : at + seg] for h in range(per_tile)], 1
                    ).astype(BF16)

        def one_part(p, carry):
            low = p * part_rows
            here = pl.ds(pl.multiple_of(low, ROWS), part_rows)

            def over(body):
                def some(q, carry):
                    for i in range(many):
                        body(pl.ds(pl.multiple_of(low + (q * many + i) * ROWS, ROWS), ROWS))
                    return carry

                lax.fori_loop(0, part_rows // ROWS // many, some, 0)

            over(along_columns)

            def one_row(c, carry):
                flow_rows[c, here] = jnp.dot(flow_cols[c, here], across[...], preferred_element_type=F32)
                return carry

            lax.fori_loop(0, chunk_rows, one_row, 0)
            over(along_rows)
            if parts > 1:

                @pl.when((p < parts - 1) & (t < ahead))
                def _():
                    for delta in range(1, slots):
                        inward(j, delta, here, p).start()

            return carry

        lax.fori_loop(0, parts, one_part, 0)
        if rest:
            for delta in range(1, slots):
                rest_out[peer(delta), j] = fold(blocks[peer(delta), j, body_rows:])

        @pl.when(t < ahead)
        def _():
            for delta in range(1, slots):
                inward(j, delta, last_part, parts - 1).start()
                if rest:
                    inward_rest(j, delta).start()

        return carry

    lax.fori_loop(0, chunks, advect_first, 0)

    @pl.when(jnp.logical_not(has_left))
    def _():
        col_in[:, 0] = jnp.zeros_like(col_in[:, 0])

    @pl.when(jnp.logical_not(has_right))
    def _():
        col_in[:, 1] = jnp.zeros_like(col_in[:, 1])

    zeros = jnp.zeros((padded, 128), BF16)

    def clear(g, carry):
        for flux in (flux_e, flux_w):

            @pl.when(jnp.logical_not(has_before))
            def _():
                flux[g, :, :128] = zeros

            @pl.when(jnp.logical_not(has_after))
            def _():
                flux[g, :, 128 + tile_points :] = zeros

        return carry

    lax.fori_loop(0, slots, clear, 0)
    for j in range(chunks):
        got[j, me] = blocks[me, j]

    for delta in range(1, slots):
        downward(delta).wait()
    for b in range(slots):
        here = jnp.zeros((4, high, 128), F32)
        for s in range(slots):
            here = here + (owners[s] == b).astype(F32) * deepers[s]
        for f in range(4):
            for i in range(high):
                at = b * block + i * 128
                strip_rows[2 + f : 3 + f, at : at + 128] = here[f, i : i + 1]
    strip_rows[6:7, :] = land_row[...]
    strip_rows[7:8, :] = land_row[...]
    pieces_of = [[] for _ in range(slots)]
    for r in range(rows):
        line = strip_rows[:, r * width : (r + 1) * width]
        for d in range(slots):
            pieces_of[d].append(line[:, d * seg : (d + 1) * seg])
    mine = jnp.zeros((8, tile_points), F32)
    for d in range(slots):
        mine = mine + (me == d).astype(F32) * jnp.concatenate(pieces_of[d], 1)
    tile[...] = mine
    for each in held[4:]:
        each.wait()
    eye = lax.broadcasted_iota(jnp.int32, (proj.shape[1], proj.shape[1]), 0)
    eye = (eye == lax.broadcasted_iota(jnp.int32, eye.shape, 1)).astype(F32).astype(BF16)
    mixed_rows = jnp.zeros((through.shape[1], proj.shape[1]), F32)
    for g in range(slots):
        low = g * comps // ROWS * ROWS
        window = min(padded + ROWS, slots * comps - low)
        row = lax.broadcasted_iota(jnp.int32, (padded, window), 0)
        shift = lax.broadcasted_iota(jnp.int32, (padded, window), 1) - row
        shift = ((shift == g * comps - low) & (row < comps)).astype(F32).astype(BF16)
        back[g] = jnp.dot(shift, back_held[low : low + window], preferred_element_type=F32).astype(BF16)
        aligned = jnp.dot(shift, proj_held[low : low + window], preferred_element_type=F32).astype(BF16)
        proj[g] = lax.dot_general(
            eye, aligned, (((1,), (1,)), ((), ())), preferred_element_type=F32
        ).astype(BF16)
        mixed_rows = mixed_rows + jnp.dot(through[g], back[g], preferred_element_type=F32)
    half = mixed_rows.shape[0] // 2
    mixed_rows = mixed_rows[:half] + mixed_rows[half:]
    first = mixed_rows.astype(BF16)
    inner[:half] = first
    inner[half:] = (mixed_rows - first.astype(F32)).astype(BF16)

    def project(values, step, j):
        projected = jnp.dot(proj[0], values[0], preferred_element_type=F32)
        more = jnp.dot(outer[0], values[0], preferred_element_type=F32)
        for g in range(1, slots):
            projected = projected + jnp.dot(proj[g], values[g], preferred_element_type=F32)
            more = more + jnp.dot(outer[g], values[g], preferred_element_type=F32)
        cubed = (projected * projected * projected).astype(BF16)
        more = more + jnp.dot(inner[...], cubed, preferred_element_type=F32)
        half = more.shape[0] // 2
        payload = more[:half] + more[half:]
        pay[step, j] = payload
        return cubed, payload

    def send_payload(step):
        whole_pay = jnp.concatenate([pay[step, j] for j in range(chunks)], 1)
        for s in range(slots):
            value = jnp.zeros((whole_pay.shape[0], part), F32)
            for b in range(slots):
                value = value + (owners[s] == b).astype(F32) * whole_pay[:, b * part : (b + 1) * part]
            pay_out[step, s] = value.astype(BF16)
        pay_in[step, me] = pay_out[step, me]
        for delta in range(1, slots):
            pay_over(step, delta).start()

    def source_first(t):
        j = first_order(t)
        for delta in range(1, slots):
            for each in inward_parts(j, delta):
                each.wait_recv()
            if rest:
                inward_rest(j, delta).wait_recv()
                sender = lax.rem(me + slots - delta, slots)
                got[j, sender, body_rows:] = unfold(rest_in[j, sender])
        cubed, payload = project(got.at[j], 0, j)
        own = tile[:, pl.ds(pl.multiple_of(j * lanes, 128), lanes)]
        u0, v0, u1, v1 = own[0:1], own[1:2], own[2:3], own[3:4]
        mix, depth = own[4:5], own[5:6]
        live = (depth > 0.5).astype(F32)
        below = mix * (depth > 1.5).astype(F32)
        floor = mix * ((depth > 0.5) & (depth < 1.5)).astype(F32)
        push_u, push_v = payload[0:1], payload[layers : layers + 1]
        new_u = live * (u0 + coriolis * v0 - below * (u0 - u1) - floor * u0 + push_u)
        new_v = live * (v0 - coriolis * u0 - below * (v0 - v1) - floor * v0 + push_v)
        east_here = current_scale * new_u
        north_here = current_scale * new_v

        def one_group(g):
            transfer = jnp.dot(back[g], cubed, preferred_element_type=F32)
            updated = (got[j, g].astype(F32) + source_step * transfer).astype(BF16)
            state[j, g] = updated
            updated = updated.astype(F32)
            along_x = (taps[g, :, 0:1] + east_here) * updated
            eastward = taps[g, :, 2:3] != 0.0
            at = pl.ds(pl.multiple_of(128 + j * lanes, 128), lanes)
            flux_e[g, :, at] = jnp.where(eastward, along_x, 0.0).astype(BF16)
            flux_w[g, :, at] = jnp.where(eastward, 0.0, along_x).astype(BF16)
            along_y = (taps[g, :, 1:2] + north_here) * updated
            northward = taps[g, :, 7:8] != 0.0
            flux_n[j, g] = jnp.where(northward, along_y, 0.0).astype(BF16)
            flux_s[j, g] = jnp.where(northward, 0.0, along_y).astype(BF16)
            along_y = along_y.astype(BF16)
            ends = lax.dot_general(
                pick[...], along_y, (((1,), (1,)), ((), ())), preferred_element_type=F32
            )

            @pl.when(j == 0)
            def _():
                row_out[0, g] = along_x[:, :128].astype(BF16)

            @pl.when(j == chunks - 1)
            def _():
                row_out[1, g] = along_x[:, lanes - 128 :].astype(BF16)

            half = ends.shape[0] // 2
            return ends[:half], ends[half:]

        def one_source(p, carry):
            ends = [one_group(p * pack + i) for i in range(pack)]
            for side in range(2):
                col_out[j, side, p] = jnp.concatenate([both[side] for both in ends], 0).astype(BF16)
            return carry

        lax.fori_loop(0, slots // pack, one_source, 0)

        @pl.when(has_left)
        def _():
            col_left(j).start()

        @pl.when(has_right)
        def _():
            col_right(j).start()

        @pl.when((j == 0) & has_before)
        def _():
            row_up().start()

        @pl.when((j == chunks - 1) & has_after)
        def _():
            row_down().start()

    def advect_second(j):
        def put(place, at):
            def one(g, carry):
                eastward = taps[g, :, 2:3] != 0.0
                value = row_in[place, g].astype(F32)
                flux_e[g, :, at : at + 128] = jnp.where(eastward, value, 0.0).astype(BF16)
                flux_w[g, :, at : at + 128] = jnp.where(eastward, 0.0, value).astype(BF16)
                return carry

            lax.fori_loop(0, slots, one, 0)

        @pl.when((j == 0) & has_before)
        def _():
            row_down().wait_recv()
            put(0, 0)

        @pl.when((j == chunks - 1) & has_after)
        def _():
            row_up().wait_recv()
            put(1, 128 + tile_points)

        @pl.when(has_left)
        def _():
            col_right(j).wait_recv()

        @pl.when(has_right)
        def _():
            col_left(j).wait_recv()

        start = pl.multiple_of(j * lanes, 128)
        land_here = tile[6:7, pl.ds(start, lanes)]

        def one_advect(g, carry):
            rows_at = pl.ds(start, lanes + 256)
            every = jnp.concatenate(
                [flux_e[g, :, rows_at], flux_w[g, :, rows_at], flux_n[j, g], flux_s[j, g]], 1
            )
            ends = jnp.concatenate([col_in[j, 0, g // pack], col_in[j, 1, g // pack]], 0)
            ends_north = ends * north_mask[g]
            ends = jnp.concatenate([ends_north, ends - ends_north], 0)
            change = jnp.dot(every, inside[...], preferred_element_type=F32) + lax.dot_general(
                ends, spread[lax.rem(g, pack)], (((0,), (0,)), ((), ())), preferred_element_type=F32
            )
            total = (state[j, g].astype(F32) - change * (1.0 / 6.0)) * land_here
            drift[g] = total.astype(BF16)
            return carry

        lax.fori_loop(0, slots, one_advect, 0)

    def source_second(t):
        j = flip(t)
        advect_second(j)
        cubed, _ = project(drift, 1, j)

        for delta in [*range(1, slots), 0]:
            g = peer(delta)
            transfer = jnp.dot(back[g], cubed, preferred_element_type=F32)
            updated = (drift[g].astype(F32) + source_step * transfer).astype(BF16)
            if delta:
                made[j, g] = updated
                homeward(j, delta).start()
                if rest:
                    rest_made[j, g] = fold(updated[body_rows:])
                    homeward_rest(j, delta).start()
            else:
                returned[j, g] = updated

        @pl.when(t == chunks - 1)
        def _():
            send_payload(1)

    def middle(u, carry):
        @pl.when(u < chunks)
        def _():
            source_first(u)

        @pl.when(u + ahead < chunks)
        def _():
            j = first_order(u + ahead)
            for delta in range(1, slots):
                for each in inward_parts(j, delta):
                    each.start()
                if rest:
                    inward_rest(j, delta).start()

        @pl.when(u == chunks - 1)
        def _():
            send_payload(0)

        @pl.when(u > 0)
        def _():
            source_second(u - 1)

        return carry

    lax.fori_loop(0, chunks + 1, middle, 0)

    layer = lax.broadcasted_iota(jnp.int32, (layers, high, 128), 0)
    depth = active[...][None]
    live = (layer < depth).astype(F32)
    bottom = mixing[...] * (layer == depth - 1).astype(F32)
    upper = mixing[...] * ((layer + 1 < depth) & (layer < layers - 1)).astype(F32)
    nothing = jnp.zeros((1, high, 128), F32)

    def mixed(value):
        between = upper * (value - jnp.concatenate([value[1:], nothing], 0))
        return jnp.concatenate([nothing, between[:-1]], 0) - between - bottom * value

    def ocean_step(step, east_old, north_old):
        for delta in range(1, slots):
            pay_over(step, delta).wait_recv()
        lines = []
        for i in range(high):
            pieces = []
            for h in range(per_tile):
                r, d = divmod(i * per_tile + h, slots)
                pieces.append(pay_in[step, d].astype(F32)[:, r * seg : (r + 1) * seg])
            lines.append(jnp.concatenate(pieces, 1))
        lines = jnp.concatenate(lines, 0).astype(BF16)
        push = jnp.dot(pay_turn[...], lines, preferred_element_type=F32).reshape(2, layers, high, 128)
        new_velocity[0] = live * (east_old + coriolis * north_old + mixed(east_old) + push[0])
        new_velocity[1] = live * (north_old - coriolis * east_old + mixed(north_old) + push[1])

    ocean_step(0, velocity[0], velocity[1])

    def unpack(t, carry):
        j = flip(t)
        for delta in range(1, slots):
            homeward(j, delta).wait_recv()
            if rest:
                homeward_rest(j, delta).wait_recv()
                sender = lax.rem(me + slots - delta, slots)
                returned[j, sender, body_rows:] = unfold(rest_back[j, sender])

        def one_group(here):
            parts = [returned[j, d, here, :].astype(F32) for d in range(slots)]
            for k in range(chunk_rows):
                line = jnp.concatenate([p[:, k * seg : (k + 1) * seg] for p in parts], 1)
                at = pl.ds(pl.multiple_of((j * chunk_rows + k) * width, 128), width)
                field[here, at] = line.astype(BF16)

        grouped(one_group)
        return carry

    lax.fori_loop(0, chunks, unpack, 0)

    def unturned(at, count):
        value = jnp.concatenate([field[at, r * width : (r + 1) * width] for r in range(rows)], 0)
        back_again = jnp.dot(unturn[: count * rows], value, preferred_element_type=F32)
        return back_again.astype(BF16).reshape(count, rows, width)

    def leave(at, i):
        return pltpu.make_async_copy(out_held.at[at], out.at[at], out_sem.at[i])

    last_rows = pl.ds(whole_groups * ROWS, rest)

    def unturn_group(at):
        out_held[at] = unturned(at, ROWS)
        leave(at, at.start // ROWS).start()

    by_groups(whole_groups, unturn_group)
    if rest:
        out_held[whole_groups * ROWS :] = unturned(slice(whole_groups * ROWS, padded), rest)
        leave(last_rows, whole_groups).start()
    for step in range(1, STEPS):
        ocean_step(step, new_velocity[0], new_velocity[1])
    for q in range(whole_groups):
        leave(pl.ds(q * ROWS, ROWS), q).wait()
    if rest:
        leave(last_rows, whole_groups).wait()

    @pl.when(has_before)
    def _():
        to_before(head, after, 0).wait_send()
        to_before(east_head, east_after, 2).wait_send()
        row_up().wait_send()

    @pl.when(has_after)
    def _():
        to_after(tail, before, 1).wait_send()
        to_after(east_tail, east_before, 3).wait_send()
        row_down().wait_send()

    for j in range(chunks):
        for delta in range(1, slots):
            for each in inward_parts(j, delta):
                each.wait_send()
            homeward(j, delta).wait_send()
            if rest:
                inward_rest(j, delta).wait_send()
                homeward_rest(j, delta).wait_send()

        @pl.when(has_left)
        def _():
            col_left(j).wait_send()

        @pl.when(has_right)
        def _():
            col_right(j).wait_send()

    for step in range(STEPS):
        for delta in range(1, slots):
            pay_over(step, delta).wait_send()


def handing_kernel(spectrum, velocity, new_spectrum, new_velocity, waves, ocean, sems):
    count = spectrum.shape[0]
    parts = 6
    pieces = [(velocity, ocean, new_velocity)]
    for i in range(parts):
        low, high = i * count // parts, (i + 1) * count // parts
        at = pl.ds(low, high - low)
        pieces.append((spectrum.at[at], waves.at[at], new_spectrum.at[at]))
    loads = [pltpu.make_async_copy(a, b, sems.at[0, i]) for i, (a, b, _) in enumerate(pieces)]
    stores = [pltpu.make_async_copy(b, c, sems.at[1, i]) for i, (_, b, c) in enumerate(pieces)]
    for each in loads:
        each.start()
    for load, store in zip(loads, stores):
        load.wait()
        store.start()
    for each in stores:
        each.wait()


def whole(count, memory=pltpu.VMEM):
    return [pl.BlockSpec(memory_space=memory)] * count


def body(spectrum, land_sea, owners, proj_weight, back_weight, ocean_vel, mixing, active_layers):
    comps, rows, width = spectrum.shape
    slots = lax.axis_size("spec")
    points = rows * width
    block = points // slots
    seg = width // slots
    tile_points = rows * seg
    lanes = 256 if tile_points % 256 == 0 else tile_points
    chunks = tile_points // lanes
    chunk_rows = lanes // seg
    layers = mixing.shape[0]
    rank_rows = proj_weight.shape[0]
    padded = -(-comps // ROWS) * ROWS
    edge = 2 * width
    edge_rows = 2 * chunk_rows
    pack = max(1, ROWS // edge_rows)
    high = block // 128
    part = block // slots

    def by_slot(table):
        result = np.zeros((slots, table.shape[0], padded), table.dtype)
        result[:, :, :comps] = table.reshape(table.shape[0], slots, comps).transpose(1, 0, 2)
        return result

    taps = np.zeros((slots, padded, 12), np.float32)
    taps[:, :comps] = tap_table().reshape(slots, comps, 12)
    drift_rows, stress_rows = coupling_tables(layers)
    push = coriolis * np.concatenate([drift_rows[layers:], -drift_rows[:layers]], 0)
    outer = by_slot(two_pieces(push))
    push = source_step * push
    push[0] += stress_rows[0]
    push[layers] += stress_rows[1]
    through = by_slot(two_pieces(push))
    tables = stencil_tables(seg, width, chunk_rows, edge_rows, pack)
    north_mask = (taps[:, :, 7] != 0).astype(BF16).reshape(slots, 1, padded)
    turn = turn_table(ROWS, rows)
    pay_turn = np.zeros((high * 2 * layers,) * 2, np.float32)
    for l in range(2 * layers):
        for i in range(high):
            pay_turn[l * high + i, i * 2 * layers + l] = 1
    pay_turn = pay_turn.astype(BF16)
    velocity = ocean_vel.reshape(2, layers, high, 128)
    inside, across, spread, pick = tables
    raw = (spectrum, turn, taps, across, proj_weight.T, back_weight, outer, through, inside, spread, pick, pay_turn,
           np.ascontiguousarray(turn.T))
    raw = [jnp.asarray(each) for each in raw]
    exchange = pltpu.VMEM((chunks, slots, padded, lanes), BF16)
    pay_rows = 2 * layers
    state, velocity = pl.pallas_call(
        functools.partial(steps_kernel, (comps, rows, width, slots)),
        out_shape=(
            jax.ShapeDtypeStruct((comps, rows, width), BF16),
            jax.ShapeDtypeStruct((2, layers, high, 128), F32),
        ),
        in_specs=whole(1, pltpu.SMEM) + whole(5) + whole(13, pl.ANY),
        out_specs=tuple(whole(1, pl.ANY) + whole(1)),
        scratch_shapes=[
            pltpu.VMEM((padded, points + 2 * edge), BF16),
            pltpu.VMEM((1, points + 2 * edge), F32),
            pltpu.VMEM((1, points), F32),
            pltpu.VMEM((1, points), F32),
            pltpu.VMEM((2, high, 128), F32),
            pltpu.VMEM((slots, 2, high, 128), F32),
            pltpu.VMEM((4, high, 128), F32),
            pltpu.VMEM((slots, 4, high, 128), F32),
            pltpu.VMEM((8, points), F32),
            pltpu.VMEM((8, tile_points), F32),
            *[pltpu.VMEM(each.shape, each.dtype) for each in raw],
            pltpu.VMEM((slots, rank_rows, padded), BF16),
            pltpu.VMEM((slots, padded, rank_rows), BF16),
            pltpu.VMEM((outer.shape[1], rank_rows), BF16),
            pltpu.VMEM((slots, chunks, ROWS, 128), BF16),
            *[pltpu.VMEM((chunks, slots, ROWS, 128), BF16)] * 3,
            pltpu.VMEM((chunk_rows, padded, width), F32),
            pltpu.VMEM((chunk_rows, padded, 2 * width), BF16),
            pltpu.VMEM((slots, chunks, padded, lanes), BF16),
            exchange,
            exchange,
            pltpu.VMEM((slots, padded, tile_points + 256), BF16),
            pltpu.VMEM((slots, padded, tile_points + 256), BF16),
            exchange,
            exchange,
            pltpu.VMEM((slots, padded, lanes), BF16),
            exchange,
            exchange,
            pltpu.VMEM((STEPS, chunks, pay_rows, lanes), F32),
            pltpu.VMEM((STEPS, slots, pay_rows, part), BF16),
            pltpu.VMEM((STEPS, slots, pay_rows, part), BF16),
            pltpu.VMEM((2, slots, padded, 128), BF16),
            pltpu.VMEM((2, slots, padded, 128), BF16),
            pltpu.VMEM((chunks, 2, slots // pack, pack * edge_rows, padded), BF16),
            pltpu.VMEM((chunks, 2, slots // pack, pack * edge_rows, padded), BF16),
        ]
        + [pltpu.VMEM((padded, edge), BF16)] * 4
        + [pltpu.VMEM((1, edge), F32)] * 4
        + [pltpu.SemaphoreType.DMA((chunks, 4 * slots))] * 4
        + [pltpu.SemaphoreType.DMA((slots,))] * 4
        + [pltpu.SemaphoreType.DMA((4,))] * 2
        + [pltpu.SemaphoreType.DMA((2,))] * 2
        + [pltpu.SemaphoreType.DMA((chunks, 2))] * 2
        + [pltpu.SemaphoreType.DMA((STEPS, slots))] * 2
        + [
            pltpu.SemaphoreType.DMA((len(raw),)),
            pltpu.SemaphoreType.DMA((padded // ROWS,)),
            pltpu.VMEM((comps, rows, width), BF16),
        ],
        compiler_params=pltpu.CompilerParams(
            vmem_limit_bytes=VMEM_LIMIT, collective_id=0, has_side_effects=True
        ),
        name="steps",
    )(owners, land_sea, velocity, mixing.reshape(layers, high, 128), active_layers.reshape(high, 128),
      jnp.asarray(north_mask), *raw)
    state, velocity = pl.pallas_call(
        handing_kernel,
        out_shape=(
            jax.ShapeDtypeStruct(state.shape, BF16),
            jax.ShapeDtypeStruct(velocity.shape, F32),
        ),
        in_specs=whole(2, pl.ANY),
        out_specs=tuple(whole(2, pl.ANY)),
        scratch_shapes=[
            pltpu.VMEM(state.shape, BF16),
            pltpu.VMEM(velocity.shape, F32),
            pltpu.SemaphoreType.DMA((2, 7)),
        ],
        name="hand",
    )(state, velocity)
    return (state, velocity.reshape(ocean_vel.shape))


def solution(mesh):
    placed = (
        P("spec", "space", None),
        P("space", None),
        P(),
        P(),
        P(),
        P(None, None, "spec", "space", None),
        P(None, "spec", "space", None),
        P("spec", "space", None),
    )
    return jax.shard_map(
        body,
        mesh=mesh,
        in_specs=placed,
        out_specs=(P("spec", "space", None), P(None, None, "spec", "space", None)),
        check_vma=False,
    )
```
